32 devices in a mesh: dp: 8 (over z, x), tensor: 4 (over y, core).
Axes of the slice: x: 2, y: 2, z: 4, core: 2. Of those that a mesh axis runs over, the one named last changes fastest.
Arguments:
- hidden_in: bfloat16 [10240, 2048], P(('dp', 'tensor')), may hold values from -6 to 6
- skip_mask: int32 [10240], P(('dp', 'tensor')), may hold values 0 or 1
- parents: int32 [8, 10], P('dp'), may hold values from 0 to 5, as said below
- attention_gain: bfloat16 [2048], P('dp'), may hold values from 0.099609375 to 1.8984375
- query_weight: bfloat16 [2048, 2048], P('dp', 'tensor'), may hold values from -0.25 to 0.25
- key_weight: bfloat16 [2048, 512], P('dp', 'tensor'), may hold values from -0.125 to 0.125
- value_weight: bfloat16 [2048, 512], P('dp', 'tensor'), may hold values from -0.125 to 0.125
- output_weight: bfloat16 [2048, 2048], P('dp', 'tensor'), may hold values from -0.5 to 0.5
- feedforward_gain: bfloat16 [2048], P('dp'), may hold values from 0.099609375 to 1.8984375
- gate_weight: bfloat16 [2048, 5632], P('dp', 'tensor'), may hold values from -0.125 to 0.125
- up_weight: bfloat16 [2048, 5632], P('dp', 'tensor'), may hold values from -0.125 to 0.125
- down_weight: bfloat16 [2048, 5632], P('dp', 'tensor'), may hold values from -0.15625 to 0.15625
- grad_out: bfloat16 [10240, 2048], P(('dp', 'tensor')), may hold values from -6 to 6
Outputs:
- layer_out: bfloat16 [10240, 2048], P(('dp', 'tensor'))
- input_grad: float32 [10240, 2048], P(('dp', 'tensor'))
- grad_attention_gain: float32 [2048], P('dp')
- grad_query_weight: float32 [2048, 2048], P('dp', 'tensor')
- grad_key_weight: float32 [2048, 512], P('dp', 'tensor')
- grad_value_weight: float32 [2048, 512], P('dp', 'tensor')
- grad_output_weight: float32 [2048, 2048], P('dp', 'tensor')
- grad_feedforward_gain: float32 [2048], P('dp')
- grad_gate_weight: float32 [2048, 5632], P('dp', 'tensor')
- grad_up_weight: float32 [2048, 5632], P('dp', 'tensor')
- grad_down_weight: float32 [2048, 5632], P('dp', 'tensor')
The draws below stay inside these ranges and needn't reach their ends.
Inputs may be any that keep to these rules, and one draw needn't show every extreme that they name: `parents`: in every tree, blocks 0 to 3 form a chain (block 0 is its own parent, block b has parent b - 1); the next 2 blocks have parent 4 - 1; each of the last 4 blocks has one of those 2 blocks as parent, and each of those 2 blocks is parent of exactly 2 of the last 4 blocks.
All inputs are finite; a program needn't handle non-finite values. No bound on the sum of `skip_mask` on one device may be relied on, other than what follows from the above.
Results may differ from the reference program's by a relative error of at most 0.023.
Values may be sent and summed in bfloat16 or wider, within the bound.
No kernel may reach another device: no remote copies, remote signals or barrier semaphores. Data moves between devices by JAX's collectives and lax.ppermute only.
A program may use at most 192 MiB of HBM per device.

```python
import math
from functools import partial
import jax
import jax.numpy as jnp
from jax import lax

D = 2048
HEADS = 16
KV = 4
HD = 128
FF = 5632
BLOCK = 128
TRUNK = 4
BRANCH = 2
LEAF = 4
TREE_LEN = 1280
TREES = 8
TOKENS = 10240


def draw_parents(key, part):
    blocks = jnp.arange(TRUNK + BRANCH, dtype=jnp.int32)
    fixed_part = jnp.where(blocks < TRUNK, jnp.maximum(blocks - 1, 0), TRUNK - 1).astype(jnp.int32)
    subkeys = jax.random.split(jax.random.fold_in(key, 7), TREES)
    orders = jax.vmap(lambda subkey: jax.random.permutation(subkey, LEAF))(subkeys).astype(jnp.int32)
    leaf_parents = TRUNK + orders // (LEAF // BRANCH)
    return jnp.concatenate([jnp.broadcast_to(fixed_part[None, :], (TREES, TRUNK + BRANCH)), leaf_parents], axis=1).astype(jnp.int32)


def touch_ends(values, own_key, smallest, largest):
    longest = values.shape.index(max(values.shape))
    spots = []
    for shift in (0, 1):
        where = [jax.random.randint(jax.random.fold_in(own_key, axis), (), 0, length) for axis, length in enumerate(values.shape)]
        where[longest] = (where[longest] + shift) % values.shape[longest]
        spots.append(tuple(where))
    return values.at[spots[0]].set(smallest).at[spots[1]].set(largest)


def strengthened(entries, own_key, source, target, parts, factor):
    def block_of(axis_at):
        return (jnp.arange(entries.shape[axis_at]) // (entries.shape[axis_at] // parts)).reshape((-1,) + (1,) * (entries.ndim - 1 - axis_at))

    one_side = jax.random.permutation(own_key, parts)[block_of(target)]
    far = (block_of(target) + parts // 2) % parts
    return jnp.where((block_of(source) == one_side) | (block_of(source) == far), factor * entries, entries)


def steps_of(stream_key, dims, pieces, low, high):
    def one(axis_at, shards_of):
        steps = jax.random.uniform(jax.random.fold_in(jax.random.fold_in(stream_key, 6), axis_at), (shards_of,), jnp.float32, low / len(pieces), high / len(pieces))
        return jnp.repeat(jnp.exp(steps), dims[axis_at] // shards_of).reshape((-1,) + (1,) * (len(dims) - axis_at - 1))

    gain = one(*pieces[0])
    for cut in pieces[1:]:
        gain = gain * one(*cut)
    return gain


def centred(own_key, dims, spread, most, shards=(), kind=jnp.bfloat16):
    factor_of = steps_of(own_key, dims, shards, -0.22, 0.18) if shards else 1.0
    values = jax.random.normal(own_key, dims, jnp.float32) * spread * factor_of
    return jnp.minimum(jnp.maximum(values, -most), most).astype(kind)


def bell_draw_with(stream_key, dims, deviation, reach, pieces, heavy, kind=jnp.bfloat16):
    drawn = deviation * jax.random.normal(stream_key, dims, jnp.float32)
    if pieces:
        drawn = drawn * steps_of(stream_key, dims, pieces, -0.22, 0.18)
    return jnp.clip(strengthened(drawn, jax.random.fold_in(stream_key, 3), *heavy), -reach, reach).astype(kind)


def setup_inputs(seed: int = 0) -> dict:
    key_of = jax.random.split(jax.random.key(seed), 14)
    hidden_in = centred(key_of[0], (TOKENS, D), 1.0, 6.0, ((0, 32),))
    skip_mask = touch_ends((jax.random.randint(key_of[1], (TOKENS,), 0, 4) < 1).astype(jnp.int32), jax.random.fold_in(key_of[1], 1), 0, 1)
    parents = draw_parents(jax.random.fold_in(key_of[13], 71), 0)
    attention_gain = jnp.clip(1.0 + 0.18 * jax.random.normal(key_of[3], (D,), jnp.float32), 0.099609375, 1.8984375).astype(jnp.bfloat16)
    query_weight = centred(key_of[4], (D, HEADS * HD), (D // 4) ** -0.5, 0.25, ((0, 8), (1, 4)))
    key_weight = centred(key_of[5], (D, KV * HD), D ** -0.5, 0.125, ((0, 8), (1, 4)))
    value_weight = centred(key_of[6], (D, KV * HD), D ** -0.5, 0.125, ((0, 8), (1, 4)))
    output_weight = centred(key_of[7], (D, HEADS * HD), (HEADS * HD // 16) ** -0.5, 0.5, ((0, 8), (1, 4)))
    feedforward_gain = jnp.clip(1.0 + 0.18 * jax.random.normal(key_of[8], (D,), jnp.float32), 0.099609375, 1.8984375).astype(jnp.bfloat16)
    gate_weight = centred(key_of[9], (D, FF), D ** -0.5, 0.125, ((0, 8), (1, 4)))
    up_weight = centred(key_of[10], (D, FF), D ** -0.5, 0.125, ((0, 8), (1, 4)))
    down_weight = centred(key_of[11], (D, FF), (FF // 4) ** -0.5, 0.15625, ((0, 8), (1, 4)))
    grad_out = bell_draw_with(key_of[12], (TOKENS, D), 1.0, 6.0, ((0, 32),), (0, 1, 32, 2.75))
    return {"hidden_in": hidden_in, "skip_mask": skip_mask, "parents": parents, "attention_gain": attention_gain, "query_weight": query_weight, "key_weight": key_weight, "value_weight": value_weight, "output_weight": output_weight, "feedforward_gain": feedforward_gain, "gate_weight": gate_weight, "up_weight": up_weight, "down_weight": down_weight, "grad_out": grad_out}


@jax.custom_vjp
def low(v):
    return lax.optimization_barrier(v.astype(jnp.bfloat16)).astype(jnp.float32)

@jax.custom_vjp
def low_back(v):
    return v

def low_keep(v):
    return (low(v), None)

def low_pass(kept, grad):
    return (grad,)

def back_keep(v):
    return (v, None)

def back_low(kept, grad):
    return (low(grad),)
low.defvjp(low_keep, low_pass)
low_back.defvjp(back_keep, back_low)
epsilon = 1e-05
masked_score = -1000000000.0
highest = lax.Precision.HIGHEST

def tree_layout(parent_ids):
    count = parent_ids.shape[0]
    blocks = jnp.arange(count, dtype=jnp.int32)
    ancestor = blocks[:, None] == blocks[None, :]
    current = blocks
    for sweep in range(count):
        current = lax.optimization_barrier(jnp.sum(jnp.where(blocks[None, :] == current[:, None], parent_ids[None, :], 0), axis=1)).astype(jnp.int32)
        ancestor = ancestor | (blocks[None, :] == current[:, None])
    depth = (lax.optimization_barrier(jnp.sum(ancestor.astype(jnp.int32), axis=1)) - 1).astype(jnp.int32)
    return (ancestor, depth)

def tree_tables(ancestor, depth, block_len, head_size):
    count = depth.shape[0]
    length = count * block_len
    visible = jnp.broadcast_to(ancestor[:, None, :, None], (count, block_len, count, block_len)).reshape(length, length)
    places = jnp.arange(length, dtype=jnp.int32)
    block_of = places // block_len
    later = (block_of[:, None] == block_of[None, :]) & (places[None, :] > places[:, None])
    allowed = visible & jnp.logical_not(later)
    block_ids = jnp.arange(count, dtype=jnp.int32)
    row_depth = lax.optimization_barrier(jnp.sum(jnp.where(block_of[:, None] == block_ids[None, :], depth[None, :], 0), axis=1)).astype(jnp.int32)
    position = (row_depth * block_len + places % block_len).astype(jnp.float32)
    half_size = head_size // 2
    freqs = jnp.exp(jnp.arange(half_size, dtype=jnp.float32) * (-2.0 * math.log(10000.0) / head_size))
    angles = position[:, None] * freqs[None, :]
    cosine = jnp.concatenate([jnp.cos(angles), jnp.cos(angles)], axis=1)[:, None, :]
    sine = jnp.concatenate([jnp.sin(angles), jnp.sin(angles)], axis=1)[:, None, :]
    return (allowed, cosine, sine)

def rotate(values_in, cosine, sine):
    half_size = values_in.shape[-1] // 2
    turned = jnp.concatenate([-values_in[..., half_size:], values_in[..., :half_size]], axis=-1)
    return values_in * cosine + turned * sine

def rms_scale(values_in):
    return lax.rsqrt(lax.optimization_barrier(jnp.mean(values_in * values_in, axis=-1, keepdims=True)) + epsilon)

def head_group(operands, allowed, scale):
    queries, keys_rot, values_in = operands
    scores = low_back(jnp.einsum('gld,md->glm', queries, keys_rot, precision=highest) * scale)
    scores = jnp.where(allowed[None], scores, masked_score)
    probs = low(jax.nn.softmax(scores, axis=-1))
    return jnp.einsum('glm,md->gld', probs, values_in, precision=highest)

def layer(hidden, params, keep, allowed, cosine, sine):
    attention_gain, query_weight, key_weight, value_weight, output_weight, feedforward_gain, gate_weight, up_weight, down_weight = params
    length = hidden.shape[0]
    head_size = cosine.shape[-1]
    heads = query_weight.shape[1] // head_size
    kv_heads = key_weight.shape[1] // head_size
    group = heads // kv_heads
    scale = head_size ** (-0.5)
    normed = low(hidden * rms_scale(hidden) * attention_gain)
    query_raw = low_back(jnp.dot(normed, query_weight, precision=highest)).reshape(length, heads, head_size)
    key_raw = low_back(jnp.dot(normed, key_weight, precision=highest)).reshape(length, kv_heads, head_size)
    values_all = low(low_back(jnp.dot(normed, value_weight, precision=highest))).reshape(length, kv_heads, head_size)
    queries = low(rotate(query_raw, cosine, sine))
    keys_rot = low(rotate(key_raw, cosine, sine))
    grouped = queries.reshape(length, kv_heads, group, head_size).transpose(1, 2, 0, 3)
    attend = jax.checkpoint(partial(head_group, allowed=allowed, scale=scale))
    mixed = lax.map(attend, (grouped, keys_rot.transpose(1, 0, 2), values_all.transpose(1, 0, 2)))
    mixed = low(low_back(mixed)).transpose(2, 0, 1, 3).reshape(length, heads * head_size)
    attended = low_back(jnp.dot(mixed, output_weight.T, precision=highest))
    middle = hidden + keep * attended
    normed_ff = low(middle * rms_scale(middle) * feedforward_gain)
    gate = low_back(jnp.dot(normed_ff, gate_weight, precision=highest))
    upward = low_back(jnp.dot(normed_ff, up_weight, precision=highest))
    hidden_ff = low(jax.nn.silu(gate) * upward)
    branch = low_back(jnp.dot(hidden_ff, down_weight.T, precision=highest))
    return middle + keep * branch

def reference(hidden_in, skip_mask, parents, attention_gain, query_weight, key_weight, value_weight, output_weight, feedforward_gain, gate_weight, up_weight, down_weight, grad_out):
    weights = jax.tree.map(lambda weight: weight.astype(jnp.float32), (attention_gain, query_weight, key_weight, value_weight, output_weight, feedforward_gain, gate_weight, up_weight, down_weight))
    inputs = hidden_in.reshape(TREES, TREE_LEN, D)
    keeps = (1 - skip_mask).astype(jnp.float32).reshape(TREES, TREE_LEN, 1)
    cotangents = grad_out.reshape(TREES, TREE_LEN, D)

    def per_tree(totals, operands):
        tree_in, keep, parent_ids, tree_grad = operands
        ancestor, depth = tree_layout(parent_ids)
        allowed, cosine, sine = tree_tables(ancestor, depth, BLOCK, HD)

        def forward(hidden, *params):
            return layer(hidden, params, keep, allowed, cosine, sine)
        result, pullback = jax.vjp(forward, tree_in.astype(jnp.float32), *weights)
        grads = pullback(tree_grad.astype(jnp.float32))
        totals = jax.tree.map(lambda left, right: left + right, totals, tuple(grads[1:]))
        return (totals, (result.astype(jnp.bfloat16), grads[0]))
    zeros = jax.tree.map(jnp.zeros_like, weights)
    totals, (outputs, input_grads) = lax.scan(per_tree, zeros, (inputs, keeps, parents, cotangents))
    return (outputs.reshape(TOKENS, D), input_grads.reshape(TOKENS, D), totals[0], totals[1], totals[2], totals[3], totals[4], totals[5], totals[6], totals[7], totals[8])
```

```python
import math

import jax
import jax.numpy as jnp
from jax import lax
from jax.experimental import pallas as pl
from jax.experimental.pallas import tpu as pltpu
from jax.sharding import Mesh
from jax.sharding import PartitionSpec as P

HD = 128
TRUNK = 4
BRANCH = 2
PIECES = 4
SHARE = 4
VMEM = 32 * 2**20

epsilon = 1e-05
masked_score = -1000000000.0
bf16 = jnp.bfloat16
f32 = jnp.float32


def dot_nn(a, b):
    return lax.dot_general(a, b, (((1,), (0,)), ((), ())), preferred_element_type=f32)


def dot_nt(a, b):
    return lax.dot_general(a, b, (((1,), (1,)), ((), ())), preferred_element_type=f32)


def dot_tn(a, b):
    return lax.dot_general(a, b, (((0,), (0,)), ((), ())), preferred_element_type=f32)


def place_pieces(table, groups, tree, blocks, into_tree):
    size = tree.shape[0] // PIECES
    piece = 0
    for group in groups:
        for at in range(0, group.shape[0], size):
            start = pl.multiple_of(table[blocks + piece], 64)
            here = slice(at, at + size)
            if into_tree:
                tree[pl.ds(start, size), :] = group[here, :].astype(tree.dtype)
            else:
                group[here, :] = tree[pl.ds(start, size), :].astype(group.dtype)
            piece += 1


def segments(table, rows, block, block_len, key_at, value_at):
    def part(start, size):
        return (
            rows[pl.ds(start, size), key_at : key_at + HD],
            rows[pl.ds(start, size), value_at : value_at + HD],
        )

    found = []
    trunk = min(block, TRUNK)
    if trunk:
        found.append((0, trunk * block_len) + part(0, trunk * block_len))
    if block >= TRUNK + BRANCH:
        start = pl.multiple_of(table[block] * block_len, block_len)
        found.append((start, block_len) + part(start, block_len))
    start = block * block_len
    found.append((start, block_len) + part(start, block_len))
    return found


def block_probs(stacked, found, block_len, scale):
    rows = stacked.shape[0]
    scores = [dot_nt(stacked, keys) * scale for _, _, keys, _ in found]
    row = lax.broadcasted_iota(jnp.int32, (rows, block_len), 0) % block_len
    column = lax.broadcasted_iota(jnp.int32, (rows, block_len), 1)
    scores[-1] = jnp.where(column <= row, scores[-1], masked_score)
    top = jnp.max(scores[0], axis=-1, keepdims=True)
    for part in scores[1:]:
        top = jnp.maximum(top, jnp.max(part, axis=-1, keepdims=True))
    raw = [jnp.exp(part - top) for part in scores]
    total = jnp.sum(raw[0], axis=-1, keepdims=True)
    for part in raw[1:]:
        total = total + jnp.sum(part, axis=-1, keepdims=True)
    inverse = 1.0 / total
    return [part * inverse for part in raw]


def stack_heads(rows, block, block_len, heads):
    here = slice(block * block_len, (block + 1) * block_len)
    return jnp.concatenate([rows[here, h * HD : (h + 1) * HD] for h in range(heads)], axis=0)


def attend_kernel(
    blocks, heads, table, raw, cosine, sine, mixed_near, mixed_far, rotated, tree, result
):
    length = tree.shape[0]
    block_len = length // blocks
    key_at, value_at = heads * HD, (heads + 1) * HD
    place_pieces(table, [raw], tree, blocks, True)

    def turn(block, carry):
        here = pl.ds(pl.multiple_of(block * block_len, block_len), block_len)
        cos, sin = cosine[here, :], sine[here, :]
        for h in range(heads + 1):
            there = slice(h * HD, (h + 1) * HD)
            values = tree[here, there]
            turned = values * cos + pltpu.roll(values, HD // 2, 1) * sin
            rotated[here, there] = turned.astype(bf16)
        rotated[here, value_at : value_at + HD] = tree[here, value_at : value_at + HD].astype(bf16)
        return carry

    lax.fori_loop(0, blocks, turn, 0)
    for block in range(blocks):
        stacked = stack_heads(rotated, block, block_len, heads)
        found = segments(table, rotated, block, block_len, key_at, value_at)
        probs = block_probs(stacked, found, block_len, HD ** (-0.5))
        out = dot_nn(probs[0].astype(bf16), found[0][3])
        for part, (_, _, _, values) in zip(probs[1:], found[1:]):
            out = out + dot_nn(part.astype(bf16), values)
        out = out.astype(bf16)
        for h in range(heads):
            result[block * block_len : (block + 1) * block_len, h * HD : (h + 1) * HD] = out[
                h * block_len : (h + 1) * block_len, :
            ]
    place_pieces(table, [mixed_near, mixed_far], result, blocks, False)


def attend_back_kernel(
    blocks,
    heads,
    table,
    rotated,
    grads,
    cosine,
    sine,
    packed_near,
    packed_far,
    tree,
    keys,
    values,
    result,
):
    length = rotated.shape[0]
    block_len = length // blocks
    key_at, value_at = heads * HD, (heads + 1) * HD
    scale = HD ** (-0.5)
    place_pieces(table, [grads], tree, blocks, True)
    keys[...] = jnp.zeros_like(keys)
    values[...] = jnp.zeros_like(values)

    def turn_back(rows, here):
        return rows * cosine[here, :] + pltpu.roll(rows * sine[here, :], HD // 2, 1)

    for block in range(blocks):
        here = slice(block * block_len, (block + 1) * block_len)
        stacked = stack_heads(rotated, block, block_len, heads)
        cotangent = stack_heads(tree, block, block_len, heads)
        found = segments(table, rotated, block, block_len, key_at, value_at)
        probs = block_probs(stacked, found, block_len, scale)
        prob_grads = [dot_nt(cotangent, part) for _, _, _, part in found]
        delta = jnp.sum(probs[0] * prob_grads[0], axis=-1, keepdims=True)
        for part, grad in zip(probs[1:], prob_grads[1:]):
            delta = delta + jnp.sum(part * grad, axis=-1, keepdims=True)
        query_grad = None
        for (start, size, key_rows, _), part, grad in zip(found, probs, prob_grads):
            score_grad = (part * (grad - delta)).astype(bf16)
            term = dot_nn(score_grad, key_rows)
            query_grad = term if query_grad is None else query_grad + term
            there = pl.ds(start, size)
            keys[there, :] += dot_tn(score_grad, stacked) * scale
            values[there, :] += dot_tn(part.astype(bf16), cotangent)
        query_grad = query_grad * scale
        for h in range(heads):
            rows = query_grad[h * block_len : (h + 1) * block_len, :]
            result[here, h * HD : (h + 1) * HD] = turn_back(rows, here).astype(bf16)

    def finish(block, carry):
        here = pl.ds(pl.multiple_of(block * block_len, block_len), block_len)
        result[here, key_at : key_at + HD] = turn_back(keys[here, :], here).astype(bf16)
        result[here, value_at : value_at + HD] = values[here, :].astype(bf16)
        return carry

    lax.fori_loop(0, blocks, finish, 0)
    place_pieces(table, [packed_near, packed_far], result, blocks, False)


def attention_calls(length, blocks, heads):
    width = (heads + 2) * HD
    vmem = pl.BlockSpec(memory_space=pltpu.VMEM)
    smem = pl.BlockSpec(memory_space=pltpu.SMEM)
    params = pltpu.CompilerParams(vmem_limit_bytes=VMEM)
    pairs = (TRUNK * (TRUNK + 1) // 2 + (blocks - TRUNK) * (TRUNK + 1) + 4) * heads
    pairs = pairs * (length // blocks) ** 2

    def forward(*operands):
        return attend_kernel(blocks, heads, *operands)

    def backward(*operands):
        return attend_back_kernel(blocks, heads, *operands)

    ahead = pl.pallas_call(
        forward,
        in_specs=[smem] + [vmem] * 3,
        out_specs=[vmem] * 3,
        out_shape=[shaped(length // 2, heads * HD, bf16)] * 2 + [shaped(length, width, bf16)],
        scratch_shapes=[pltpu.VMEM((length, width), f32), pltpu.VMEM((length, heads * HD), bf16)],
        compiler_params=params,
        cost_estimate=cost(16 * pairs * HD, length * width * 8),
        name="attend",
    )
    back = pl.pallas_call(
        backward,
        in_specs=[smem] + [vmem] * 4,
        out_specs=[vmem] * 2,
        out_shape=[shaped(length // 2, width, bf16)] * 2,
        scratch_shapes=[
            pltpu.VMEM((length, heads * HD), bf16),
            pltpu.VMEM((length, HD), f32),
            pltpu.VMEM((length, HD), f32),
            pltpu.VMEM((length, width), bf16),
        ],
        compiler_params=params,
        cost_estimate=cost(24 * pairs * HD, length * width * 8),
        name="attend_back",
    )
    return ahead, back


def rotation_tables(blocks, block_len):
    depths = [min(block, TRUNK) + (block >= TRUNK + BRANCH) for block in range(blocks)]
    length = blocks * block_len
    places = jnp.arange(length, dtype=jnp.int32)
    row_depth = jnp.zeros((length,), jnp.int32)
    for block, depth in enumerate(depths):
        row_depth = jnp.where(places // block_len == block, depth, row_depth)
    position = (row_depth * block_len + places % block_len).astype(f32)
    half = HD // 2
    freqs = jnp.exp(jnp.arange(half, dtype=f32) * (-2.0 * math.log(10000.0) / HD))
    angles = position[:, None] * freqs[None, :]
    cosine, sine = jnp.cos(angles), jnp.sin(angles)
    return (
        jnp.concatenate([cosine, cosine], axis=1),
        jnp.concatenate([-sine, sine], axis=1),
    )


def spec(block, index):
    return pl.BlockSpec(block, index)


def whole(shape):
    return pl.BlockSpec(shape, lambda *_: (0,) * len(shape))


def cost(flops, moved):
    return pl.CostEstimate(flops=flops // SHARE, bytes_accessed=moved // SHARE, transcendentals=0)


def shaped(rows, columns, kind):
    return jax.ShapeDtypeStruct((rows, columns), kind)


def runs(order, width):
    run = width // order.shape[0]
    for j in range(order.shape[0]):
        yield slice(j * run, (j + 1) * run), pl.ds(pl.multiple_of(order[j] * run, HD), run)


def row_call(kernel, name, rows, tile, order, operands, results):
    def place(array, offset):
        if offset is None:
            return whole(array.shape)
        steps = array.shape[0] // tile
        return spec((tile, array.shape[1]), lambda i: ((i + offset) % steps, 0))

    return pl.pallas_call(
        kernel,
        grid=(rows // tile,),
        in_specs=[pl.BlockSpec(memory_space=pltpu.SMEM)] + [place(*pair) for pair in operands],
        out_specs=[spec((tile, columns), lambda i: (i, 0)) for columns, _ in results],
        out_shape=[shaped(rows, columns, kind) for columns, kind in results],
        compiler_params=pltpu.CompilerParams(vmem_limit_bytes=VMEM),
        cost_estimate=cost(rows * 2048 * 10, rows * 2048 * 8),
        name=name,
    )(order, *[array for array, _ in operands])


def row_mean(values):
    return jnp.mean(values, axis=-1, keepdims=True)


def norm_kernel(order, rows, gain, normed):
    values = rows[...].astype(f32)
    scale = lax.rsqrt(row_mean(values * values) + epsilon)
    for here, there in runs(order, rows.shape[1]):
        unit = rows[:, there].astype(f32) * scale
        normed[:, here] = (unit * gain[:, here]).astype(bf16)


def pack_kernel(*refs):
    gains, weights, result = refs[0], refs[1:-1], refs[-1]
    at = 0
    for weight in weights:
        result[:, at : at + weight.shape[1]] = weight[...]
        at += weight.shape[1]
    rows = jnp.concatenate([gains[...], jnp.zeros((HD - gains.shape[0], gains.shape[1]), f32)])
    result[:, at:] = rows.T.astype(bf16)


def kept_kernel(order, rows, keep, result):
    for here, there in runs(order, rows.shape[1]):
        result[:, here] = (rows[:, there].astype(f32) * keep[...]).astype(bf16)


def middle_kernel(order, rows, keep, mine, got, gain, middle, normed):
    for here, there in runs(order, rows.shape[1]):
        attended = mine[:, here].astype(f32) + got[:, here].astype(f32)
        middle[:, here] = rows[:, there].astype(f32) + keep[...] * attended
    values = middle[...]
    scale = lax.rsqrt(row_mean(values * values) + epsilon)
    normed[...] = (values * scale * gain[...]).astype(bf16)


def middle_back_kernel(order, cotangent, keep, mine, got, gain, middle, grad, kept):
    values = middle[...]
    scale = lax.rsqrt(row_mean(values * values) + epsilon)
    unit = values * scale
    scaled = (mine[...].astype(f32) + got[...].astype(f32)) * gain[...]
    mean = row_mean(scaled * unit)
    change = scale * (scaled - unit * mean)
    for here, there in runs(order, middle.shape[1]):
        total = cotangent[:, there].astype(f32) + change[:, here]
        grad[:, here] = total
        kept[:, here] = (keep[...] * total).astype(bf16)


def layer_kernel(order, middle, keep, mine, got, result):
    for here, there in runs(order, middle.shape[1]):
        branch = mine[:, here].astype(f32) + got[:, here].astype(f32)
        result[:, there] = (middle[:, here] + keep[...] * branch).astype(bf16)


def input_kernel(order, rows, mine, got, gain, middle_grad, result, scaled):
    values = rows[...].astype(f32)
    scale = lax.rsqrt(row_mean(values * values) + epsilon)
    scaled[...] = (mine[...].astype(f32) + got[...].astype(f32)) * gain[...]
    total = None
    for here, there in runs(order, rows.shape[1]):
        term = jnp.sum(scaled[:, here] * rows[:, there].astype(f32), axis=-1, keepdims=True)
        total = term if total is None else total + term
    mean = total * scale / rows.shape[1]
    for here, there in runs(order, rows.shape[1]):
        unit = rows[:, there].astype(f32) * scale
        result[:, there] = middle_grad[:, here] + scale * (scaled[:, here] - unit * mean)


def column_cuts(width):
    return [slice(at, min(at + 256, width)) for at in range(0, width, 256)]


def of_group(near, far, steps):
    tile = 2 * near.shape[0] // steps
    last = steps // 2 - 1
    return [
        spec((tile, near.shape[1]), lambda i: (jnp.minimum(i, last), 0)),
        spec((tile, far.shape[1]), lambda i: (jnp.maximum(i - last - 1, 0), 0)),
    ]


def resident(slots):
    return [
        pl.BlockSpec(slot.shape, lambda i: (0, 0), pipeline_mode=pl.Buffered(1)) for slot in slots
    ]


def in_halves(steps, work):
    for side in range(2):

        @pl.when(pl.program_id(0) // (steps // 2) == side)
        def _(side=side):
            work(side)


def product(rows, weights, cut):
    total, at = None, 0
    for weight in weights:
        term = dot_nn(rows[:, at : at + weight.shape[0]], weight[:, cut])
        total = term if total is None else total + term
        at += weight.shape[0]
    return total


def through(rows, weights, name, columns, kind):
    near, far = rows
    units = columns.stop - columns.start
    length, width = 2 * near.shape[0], near.shape[1]

    def kernel(*refs):
        slots, result = refs[2:-1], refs[-1]

        def work(side):
            for inside in column_cuts(units):
                cut = slice(columns.start + inside.start, columns.start + inside.stop)
                result[:, inside] = product(refs[side], slots, cut).astype(result.dtype)

        in_halves(2, work)

    return pl.pallas_call(
        kernel,
        grid=(2,),
        in_specs=of_group(near, far, 2) + resident(weights),
        out_specs=spec((length // 2, units), lambda i: (i, 0)),
        out_shape=shaped(length, units, kind),
        compiler_params=pltpu.CompilerParams(vmem_limit_bytes=VMEM),
        cost_estimate=cost(2 * length * width * units, 2 * width * (length + units)),
        name=name,
    )(near, far, *weights)


def gated(rows, hidden_grad, gates, ups):
    near, far = rows
    length, units = hidden_grad.shape
    width = near.shape[1]
    up_slots = [slot for slots, _, _ in ups for slot in slots]
    count = len(gates)

    def kernel(*refs):
        hidden_back, gate_refs = refs[2], refs[3 : 3 + count]
        up_refs = refs[3 + count : -3]
        hidden, gate_grad, up_grad = refs[-3:]

        def work(side):
            at = 0
            for slots, first, columns in ups:
                mine = up_refs[at : at + len(slots)]
                at += len(slots)
                for inside in column_cuts(columns.stop - columns.start):
                    cut = slice(first + inside.start, first + inside.stop)
                    there = slice(columns.start + inside.start, columns.start + inside.stop)
                    gate = product(refs[side], gate_refs, cut)
                    if len(slots) == 1 and count > 1:
                        step = mine[0].shape[1] // count
                        views = [
                            mine[0][:, slice(there.start + s * step, there.stop + s * step)]
                            for s in range(count)
                        ]
                        half = mine[0].shape[0]
                        upward = dot_nn(refs[side][:, :half], views[0])
                        for s in range(1, count):
                            rows_s = refs[side][:, s * half : (s + 1) * half]
                            upward = upward + dot_nn(rows_s, views[s])
                    else:
                        upward = product(refs[side], mine, there)
                    back = hidden_back[:, cut].astype(f32)
                    sigma = 1.0 / (1.0 + jnp.exp(-gate))
                    active = gate * sigma
                    hidden[:, cut] = (active * upward).astype(bf16)
                    slope = sigma * (1.0 + gate * (1.0 - sigma))
                    gate_grad[:, cut] = (back * upward * slope).astype(bf16)
                    up_grad[:, cut] = (back * active).astype(bf16)

        in_halves(4, work)

    here = spec((length // 4, units), lambda i: (i, 0))
    return pl.pallas_call(
        kernel,
        grid=(4,),
        in_specs=of_group(near, far, 4) + [here] + resident(list(gates) + up_slots),
        out_specs=[here] * 3,
        out_shape=[shaped(length, units, bf16)] * 3,
        compiler_params=pltpu.CompilerParams(vmem_limit_bytes=VMEM),
        cost_estimate=cost(4 * length * width * units, 2 * width * (length + 2 * units)),
        name="gated",
    )(near, far, hidden_grad, *gates, *up_slots)


def back_rows(grads, weights, side, name, far=None):
    width = sum(array.shape[0] for array in weights[0][0][0])
    tile = min(512, min(array.shape[0] for parts in weights for w in parts for array in w[0]))
    first = grads[0]
    count = first[0].shape[0] if isinstance(first, tuple) else first.shape[0] // 2
    operands, specs, plan = [], [], [[] for _ in range(width // tile)]
    work = 0
    for grad, parts in zip(grads, weights):
        at = len(operands)
        if isinstance(grad, tuple):
            specs.append(spec(grad[side].shape, lambda j: (0, 0)))
            operands.append(grad[side])
        else:
            specs.append(spec((count, grad.shape[1]), lambda j: (side, 0)))
            operands.append(grad)
        for arrays, unit, columns in parts:
            start = 0
            for array, cut in zip(arrays, columns):
                tiles = array.shape[0] // tile
                for j in range(start, start + tiles):
                    plan[j].append((at, unit, cut, len(operands)))
                operands.append(array)
                specs.append(
                    spec(
                        (tile, array.shape[1]),
                        lambda j, start=start, tiles=tiles: (jnp.clip(j - start, 0, tiles - 1), 0),
                    )
                )
                start += tiles
                work += 2 * count * array.shape[0] * (cut.stop - cut.start)
    if far is not None:
        operands.append(far)
        specs.append(spec((count, tile), lambda j: (0, j)))
    ranges = []
    for j, terms in enumerate(plan):
        if ranges and ranges[-1][2] == terms:
            ranges[-1][1] = j + 1
        else:
            ranges.append([j, j + 1, terms])

    def kernel(*refs):
        result = refs[-1]
        for low, high, terms in ranges:

            @pl.when((pl.program_id(0) >= low) & (pl.program_id(0) < high))
            def _(terms=terms):
                total = None
                for at, unit, cut, place in terms:
                    units = cut.stop - cut.start
                    term = dot_nt(refs[at][:, unit : unit + units], refs[place][:, cut])
                    total = term if total is None else total + term
                if far is not None:
                    total = total + refs[-2][...].astype(f32)
                result[...] = total.astype(result.dtype)

    return pl.pallas_call(
        kernel,
        grid=(width // tile,),
        in_specs=specs,
        out_specs=spec((count, tile), lambda j: (0, j)),
        out_shape=shaped(count, width, bf16),
        compiler_params=pltpu.CompilerParams(vmem_limit_bytes=VMEM),
        cost_estimate=cost(work, 2 * sum(operand.size for operand in operands)),
        name=name,
    )(*operands)


def weight_part(rows, grads, half, s, name, columns=None):
    near, far = rows
    pair = isinstance(grads, tuple)
    units = grads[0].shape[1] if pair else grads.shape[1]
    columns = slice(0, units) if columns is None else columns
    wide = columns.stop - columns.start
    tile = 512 if half % 512 == 0 else half
    tiles = half // tile
    count = near.shape[0]
    row_spec = spec((count, tile), lambda j: (0, s * tiles + j))

    def kernel(near_rows, far_rows, *refs):
        if pair:
            first, second = refs[0][:, columns], refs[1][:, columns]
        else:
            first, second = refs[0][:count, columns], refs[0][count:, columns]
        total = dot_tn(near_rows[...], first) + dot_tn(far_rows[...], second)
        refs[-1][...] = total.astype(bf16)

    operands = grads if pair else (grads,)
    return pl.pallas_call(
        kernel,
        grid=(tiles,),
        in_specs=[row_spec, row_spec] + [whole(operand.shape) for operand in operands],
        out_specs=spec((tile, wide), lambda j: (j, 0)),
        out_shape=shaped(half, wide, bf16),
        compiler_params=pltpu.CompilerParams(vmem_limit_bytes=VMEM),
        cost_estimate=cost(4 * count * half * wide, 4 * count * (half + wide)),
        name=name,
    )(near, far, *operands)


def make_body(outer, inner, rows_axis, cores_axis):
    def body(
        hidden_in,
        skip_mask,
        parents,
        attention_gain,
        query_weight,
        key_weight,
        value_weight,
        output_weight,
        feedforward_gain,
        gate_weight,
        up_weight,
        down_weight,
        grad_out,
    ):
        part = hidden_in.shape[0]
        shard = query_weight.shape[0]
        pieces = rows_axis * cores_axis
        length = part * pieces
        near = part * rows_axis
        blocks = parents.shape[1]
        heads = query_weight.shape[1] // HD
        half = outer * shard
        width = half * inner
        tile = part // 2
        at_inner = lax.axis_index("inner")
        at_row = lax.axis_index("row")
        at_core = lax.axis_index("core")
        slots = range(inner)
        fence = lax.optimization_barrier

        order = jnp.stack(
            [z * inner + (at_inner + s) % inner for s in slots for z in range(outer)]
        ).astype(jnp.int32)

        def from_inner(values, k):
            return lax.ppermute(values, "inner", [((i + k) % inner, i) for i in range(inner)])

        def swap(values, axis):
            return lax.ppermute(values, axis, [(0, 1), (1, 0)])

        def spread(values):
            return [values] + [from_inner(values, s) for s in range(1, inner)]

        def gather(values):
            return lax.all_gather(values, "outer", axis=0, tiled=True)

        def scatter(values):
            return lax.psum_scatter(values, "outer", scatter_dimension=0, tiled=True)

        def collect(parts):
            total = parts[0].astype(f32)
            for s in range(1, inner):
                total = total + from_inner(parts[s], inner - s).astype(f32)
            return total

        keep_own = (1 - skip_mask).astype(f32)
        units = up_weight.shape[1]
        late = units if inner > 1 else 0
        joint_width = (heads + 2) * HD
        packed = pl.pallas_call(
            pack_kernel,
            out_shape=shaped(shard, joint_width + heads * HD + HD, bf16),
            compiler_params=pltpu.CompilerParams(vmem_limit_bytes=VMEM),
            cost_estimate=cost(0, shard * joint_width * 4),
            name="pack",
        )(
            jnp.stack([attention_gain.astype(f32), feedforward_gain.astype(f32)]),
            query_weight,
            key_weight,
            value_weight,
            output_weight,
        )
        keep_got = swap(keep_own, "row")
        row_x = swap(hidden_in, "row")
        row_g = swap(grad_out, "row")
        up_late = jnp.concatenate(spread(up_weight[:, units - late :]), axis=1) if late else None
        row_x, keep_got, up_late = fence((row_x, keep_got, up_late))
        near_x = jnp.concatenate([hidden_in, row_x], axis=0)
        far_x = swap(near_x, "core")
        packed_own = gather(packed)
        packed_own, far_x = fence((packed_own, far_x))
        packed_slots = spread(packed_own)
        keep = jnp.concatenate([keep_own, keep_got], axis=0)[:, None]
        near_g = jnp.concatenate([grad_out, row_g], axis=0)
        (near_branch,) = row_call(
            kept_kernel, "kept", near, tile, order, [(near_g, 0), (keep, 0)], [(width, bf16)]
        )
        far_branch = swap(near_branch, "core")
        down_own = gather(down_weight)
        gate_own = gather(gate_weight)
        early = units - late
        up_own = gather(up_weight[:, :early]) if early else None
        up_both = [gather(up_late)] if late else []

        cosine, sine = rotation_tables(blocks, length // blocks)
        starts = [
            (((at_row + dy) % 2) * cores_axis + (at_core + dc) % 2) * part
            for dc in range(2)
            for dy in range(2)
        ]
        table = jnp.concatenate([parents[0], jnp.stack(starts).astype(jnp.int32)])
        packed_slots, near_branch, far_branch, down_own = fence(
            (packed_slots, near_branch, far_branch, down_own)
        )
        down_first = from_inner(down_own[: half // 2], 1) if inner > 1 else None
        gain_at = joint_width + heads * HD
        joint_columns = slice(0, joint_width)
        output_columns = slice(joint_width, gain_at)
        gains = [values[:, gain_at:].T[:2].astype(f32) for values in packed_slots]
        gain_one = jnp.concatenate([values[0:1] for values in gains], axis=1)
        gain_two = jnp.concatenate([values[1:2] for values in gains], axis=1)
        all_branch = (near_branch, far_branch)

        def norm(rows, name):
            (result,) = row_call(
                norm_kernel, name, near, tile, order, [(rows, 0), (gain_one, None)], [(width, bf16)]
            )
            return result

        normed = (norm(near_x, "norm_near"), norm(far_x, "norm_far"))

        def all_of(arrays):
            return [(arrays, 0, [slice(0, array.shape[1]) for array in arrays])]

        attend, attend_back = attention_calls(length, blocks, heads)
        raw = through(normed, packed_slots, "joint", joint_columns, f32)
        weight_down = [down_own]
        if inner > 1:
            raw, down_first, down_own = fence((raw, down_first, down_own))
            weight_down = [down_own, down_first, from_inner(down_own[half // 2 :], 1)]
        mixed_near, mixed_far, rotated = attend(table, raw, cosine, sine)
        mixed = (mixed_near, mixed_far)

        def packed_plan(columns):
            return [(packed_slots, 0, [columns] * inner)]

        attended_plan = [packed_plan(output_columns)]
        attended_far = swap(back_rows([mixed], attended_plan, 1, "attended_far"), "core")
        attended = back_rows([mixed], attended_plan, 0, "attended_near")
        attended = (attended.astype(f32) + attended_far.astype(f32)).astype(bf16)
        attended, gate_own = fence((attended, gate_own))
        got = swap(attended, "row")
        weight_gate = spread(gate_own)
        got, weight_down, up_own = fence((got, weight_down, up_own))
        weight_up = spread(up_own) if early else []
        swapped = part // tile
        middle, normed_ff = row_call(
            middle_kernel,
            "middle",
            near,
            tile,
            order,
            [(near_x, 0), (keep, 0), (attended, 0), (got, swapped), (gain_two, None)],
            [(width, f32), (width, bf16)],
        )
        all_ff = (normed_ff, swap(normed_ff, "core"))

        hidden_grad = through(all_branch, weight_down, "hidden_grad", slice(0, units), bf16)
        up_parts = [(weight_up, 0, slice(0, early))] if early else []
        up_plan = [(weight_up, 0, [slice(0, early)] * inner)] if early else []
        if late:
            up_parts.append((up_both, early, slice(0, late)))
            up_plan.append((up_both * inner, early, [slice(s * late, (s + 1) * late) for s in slots]))
        hidden_ff, gate_grad, up_grad = gated(all_ff, hidden_grad, weight_gate, up_parts)

        def weight_parts(rows, grads, name, columns=None):
            return [weight_part(rows, grads, half, s, name, columns) for s in slots]

        def core_sum(grads, weights, name):
            far = swap(back_rows(grads, weights, 1, name + "_far"), "core")
            return back_rows(grads, weights, 0, name + "_near", far)

        last = inner - 1
        up_late_sums = None
        if late:
            up_late_parts = weight_parts(all_ff, up_grad, "grad_up_late", slice(early, units))
            gate_grad, up_grad, hidden_ff, up_late_parts = fence(
                (gate_grad, up_grad, hidden_ff, up_late_parts)
            )
            up_late_sums = scatter(jnp.concatenate(up_late_parts, axis=1))
        down_last = weight_part(all_branch, hidden_ff, half, last, "grad_down")
        gate_grad, up_grad, down_last = fence((gate_grad, up_grad, down_last))
        back_plan = ([gate_grad, up_grad], [all_of(weight_gate), up_plan])
        ff_far = back_rows(*back_plan, 1, "normed_ff_grad_far")
        ff_far, gate_grad, up_grad = fence((ff_far, gate_grad, up_grad))
        ff_far = swap(ff_far, "core")
        gate_last = weight_part(all_ff, gate_grad, half, last, "grad_gate")
        gate_grad, up_grad, gate_last = fence((gate_grad, up_grad, gate_last))
        back_plan = ([gate_grad, up_grad], [all_of(weight_gate), up_plan])
        ff_grad = back_rows(*back_plan, 0, "normed_ff_grad_near", ff_far)
        ff_grad, gate_grad, up_grad, hidden_ff = fence((ff_grad, gate_grad, up_grad, hidden_ff))
        ff_got = swap(ff_grad, "row")

        def to_last(values):
            return from_inner(values, inner - last) if last else None

        def plus(values, got):
            if got is None:
                return values
            return (values.astype(f32) + got.astype(f32)).astype(bf16)

        down_got, gate_got = to_last(down_last), to_last(gate_last)
        up_last = up_got = None
        if early:
            up_last = weight_part(all_ff, up_grad, half, last, "grad_up", slice(0, early))
            up_got = to_last(up_last)
        own = [down_last, gate_last, up_last]
        if last:
            own = [
                weight_part(all_branch, hidden_ff, half, 0, "grad_down"),
                weight_part(all_ff, gate_grad, half, 0, "grad_gate"),
                weight_part(all_ff, up_grad, half, 0, "grad_up", slice(0, early))
                if early
                else None,
            ]
        ff_got, down_got, own, up_last = fence((ff_got, down_got, own, up_last))
        grad_down = scatter(plus(own[0], down_got))
        middle_grad, attended_grad = row_call(
            middle_back_kernel,
            "middle_back",
            near,
            tile,
            order,
            [
                (near_g, 0),
                (keep, 0),
                (ff_grad, 0),
                (ff_got, swapped),
                (gain_two, None),
                (middle, 0),
            ],
            [(width, f32), (width, bf16)],
        )
        all_attended = (attended_grad, swap(attended_grad, "core"))

        branch = core_sum([hidden_ff], [all_of(weight_down)], "branch")
        branch_got = swap(branch[part:], "row")
        (layer_out,) = row_call(
            layer_kernel,
            "layer",
            part,
            tile,
            order,
            [(middle, 0), (keep, 0), (branch, 0), (branch_got, 0)],
            [(width, bf16)],
        )

        mixed_grad = through(all_attended, packed_slots, "mixed_grad", output_columns, bf16)
        output_last = weight_part(all_attended, mixed, half, last, "grad_output")
        mixed_grad, output_last = fence((mixed_grad, output_last))
        packed_grad = tuple(attend_back(table, rotated, mixed_grad, cosine, sine))
        joint_last = weight_part(normed, packed_grad, half, last, "grad_joint")
        packed_grad, gate_got, up_late_sums, joint_last = fence(
            (packed_grad, gate_got, up_late_sums, joint_last)
        )
        grad_gate = scatter(plus(own[1], gate_got))
        output_sum, joint_sum = output_last, joint_last
        if last:
            output_sum = plus(
                weight_part(all_attended, mixed, half, 0, "grad_output"), to_last(output_last)
            )
            joint_sum = plus(
                weight_part(normed, packed_grad, half, 0, "grad_joint"), to_last(joint_last)
            )
        attention_sum = jnp.concatenate([output_sum, joint_sum], axis=1)
        grad_up = None
        if early:
            up_got, grad_down = fence((up_got, grad_down))
            grad_up = scatter(plus(own[2], up_got)).astype(f32)
        attention_sum, grad_down = fence((attention_sum, grad_down))
        attention_sum = scatter(attention_sum).astype(f32)
        grad_output = attention_sum[:, : heads * HD]
        grad_joint = attention_sum[:, heads * HD :]
        normed_grad = core_sum([packed_grad], [packed_plan(joint_columns)], "normed_grad")
        normed_got = swap(normed_grad[part:], "row")
        (input_grad,) = pl.pallas_call(
            input_kernel,
            grid=(part // tile,),
            in_specs=[
                pl.BlockSpec(memory_space=pltpu.SMEM),
                spec((tile, width), lambda i: (i, 0)),
                spec((tile, width), lambda i: (i, 0)),
                spec((tile, width), lambda i: (i, 0)),
                whole((1, width)),
                spec((tile, width), lambda i: (i, 0)),
            ],
            out_specs=[spec((tile, width), lambda i: (i, 0))],
            out_shape=[shaped(part, width, f32)],
            scratch_shapes=[pltpu.VMEM((tile, width), f32)],
            compiler_params=pltpu.CompilerParams(vmem_limit_bytes=VMEM),
            cost_estimate=cost(part * width * 10, part * width * 16),
            name="input_grad",
        )(order, hidden_in, normed_grad, normed_got, gain_one, middle_grad)
        if late:
            grad_late = collect([up_late_sums[:, s * late : (s + 1) * late] for s in slots])
            grad_up = grad_late if grad_up is None else jnp.concatenate([grad_up, grad_late], axis=1)
        grad_down, grad_gate, grad_up = [
            grad.astype(f32) for grad in (grad_down, grad_gate, grad_up)
        ]

        def gain_terms(pairs, gain):
            total = None
            for weight, grad in pairs:
                term = jnp.sum(weight.astype(f32) * grad, axis=1)
                total = term if total is None else total + term
            return total / gain.astype(f32)

        query_width = heads * HD
        grad_query = grad_joint[:, :query_width]
        grad_key = grad_joint[:, query_width : query_width + HD]
        grad_value = grad_joint[:, query_width + HD :]
        gain_grads = jnp.stack(
            [
                gain_terms(
                    [
                        (query_weight, grad_query),
                        (key_weight, grad_key),
                        (value_weight, grad_value),
                    ],
                    attention_gain,
                ),
                gain_terms([(gate_weight, grad_gate), (up_weight, grad_up)], feedforward_gain),
            ]
        )
        gain_grads = gain_grads + swap(gain_grads, "core")
        gain_grads = gain_grads + swap(gain_grads, "row")
        return (
            layer_out,
            input_grad,
            gain_grads[0],
            grad_query,
            grad_key,
            grad_value,
            grad_output,
            gain_grads[1],
            grad_gate,
            grad_up,
            grad_down,
        )

    return body


def solution(mesh):
    replicas = mesh.shape["dp"]
    inner = 2 if replicas % 2 == 0 else 1
    outer = replicas // inner
    cores = mesh.shape["tensor"] // 2
    grid = Mesh(mesh.devices.reshape(outer, inner, 2, cores), ("outer", "inner", "row", "core"))
    dp, tensor = ("outer", "inner"), ("row", "core")
    both = dp + tensor
    weight = P(dp, tensor)
    return jax.shard_map(
        make_body(outer, inner, 2, cores),
        mesh=grid,
        in_specs=(
            P(both, None),
            P(both),
            P(dp, None),
            P(dp),
            weight,
            weight,
            weight,
            weight,
            P(dp),
            weight,
            weight,
            weight,
            P(both, None),
        ),
        out_specs=(
            P(both, None),
            P(both, None),
            P(dp),
            weight,
            weight,
            weight,
            weight,
            P(dp),
            weight,
            weight,
            weight,
        ),
        check_vma=False,
    )
```

```python
import math

import jax
import jax.numpy as jnp
from jax import lax
from jax.experimental import pallas as pl
from jax.experimental.pallas import tpu as pltpu
from jax.sharding import Mesh
from jax.sharding import PartitionSpec as P

HD = 128
TRUNK = 4
BRANCH = 2
PIECES = 4
SHARE = 4
VMEM = 32 * 2**20

epsilon = 1e-05
masked_score = -1000000000.0
bf16 = jnp.bfloat16
f32 = jnp.float32


def dot_nn(a, b):
    return lax.dot_general(a, b, (((1,), (0,)), ((), ())), preferred_element_type=f32)


def dot_nt(a, b):
    return lax.dot_general(a, b, (((1,), (1,)), ((), ())), preferred_element_type=f32)


def dot_tn(a, b):
    return lax.dot_general(a, b, (((0,), (0,)), ((), ())), preferred_element_type=f32)


def place_pieces(table, groups, tree, blocks, into_tree):
    size = tree.shape[0] // PIECES
    piece = 0
    for group in groups:
        for at in range(0, group.shape[0], size):
            start = pl.multiple_of(table[blocks + piece], 64)
            here = slice(at, at + size)
            if into_tree:
                tree[pl.ds(start, size), :] = group[here, :].astype(tree.dtype)
            else:
                group[here, :] = tree[pl.ds(start, size), :].astype(group.dtype)
            piece += 1


def segments(table, rows, block, block_len, key_at, value_at):
    def part(start, size):
        return (
            rows[pl.ds(start, size), key_at : key_at + HD],
            rows[pl.ds(start, size), value_at : value_at + HD],
        )

    found = []
    trunk = min(block, TRUNK)
    if trunk:
        found.append((0, trunk * block_len) + part(0, trunk * block_len))
    if block >= TRUNK + BRANCH:
        start = pl.multiple_of(table[block] * block_len, block_len)
        found.append((start, block_len) + part(start, block_len))
    start = block * block_len
    found.append((start, block_len) + part(start, block_len))
    return found


def block_probs(stacked, found, block_len, scale):
    rows = stacked.shape[0]
    scores = [dot_nt(stacked, keys) * scale for _, _, keys, _ in found]
    row = lax.broadcasted_iota(jnp.int32, (rows, block_len), 0) % block_len
    column = lax.broadcasted_iota(jnp.int32, (rows, block_len), 1)
    scores[-1] = jnp.where(column <= row, scores[-1], masked_score)
    top = jnp.max(scores[0], axis=-1, keepdims=True)
    for part in scores[1:]:
        top = jnp.maximum(top, jnp.max(part, axis=-1, keepdims=True))
    raw = [jnp.exp(part - top) for part in scores]
    total = jnp.sum(raw[0], axis=-1, keepdims=True)
    for part in raw[1:]:
        total = total + jnp.sum(part, axis=-1, keepdims=True)
    inverse = 1.0 / total
    return [part * inverse for part in raw]


def stack_heads(rows, block, block_len, heads):
    here = slice(block * block_len, (block + 1) * block_len)
    return jnp.concatenate([rows[here, h * HD : (h + 1) * HD] for h in range(heads)], axis=0)


def attend_kernel(
    blocks, heads, table, raw, cosine, sine, mixed_near, mixed_far, rotated, tree, result
):
    length = tree.shape[0]
    block_len = length // blocks
    key_at, value_at = heads * HD, (heads + 1) * HD
    place_pieces(table, [raw], tree, blocks, True)

    def turn(block, carry):
        here = pl.ds(pl.multiple_of(block * block_len, block_len), block_len)
        cos, sin = cosine[here, :], sine[here, :]
        for h in range(heads + 1):
            there = slice(h * HD, (h + 1) * HD)
            values = tree[here, there]
            turned = values * cos + pltpu.roll(values, HD // 2, 1) * sin
            rotated[here, there] = turned.astype(bf16)
        rotated[here, value_at : value_at + HD] = tree[here, value_at : value_at + HD].astype(bf16)
        return carry

    lax.fori_loop(0, blocks, turn, 0)
    for block in range(blocks):
        stacked = stack_heads(rotated, block, block_len, heads)
        found = segments(table, rotated, block, block_len, key_at, value_at)
        probs = block_probs(stacked, found, block_len, HD ** (-0.5))
        out = dot_nn(probs[0].astype(bf16), found[0][3])
        for part, (_, _, _, values) in zip(probs[1:], found[1:]):
            out = out + dot_nn(part.astype(bf16), values)
        out = out.astype(bf16)
        for h in range(heads):
            result[block * block_len : (block + 1) * block_len, h * HD : (h + 1) * HD] = out[
                h * block_len : (h + 1) * block_len, :
            ]
    place_pieces(table, [mixed_near, mixed_far], result, blocks, False)


def attend_back_kernel(
    blocks,
    heads,
    table,
    rotated,
    grads,
    cosine,
    sine,
    packed_near,
    packed_far,
    tree,
    keys,
    values,
    result,
):
    length = rotated.shape[0]
    block_len = length // blocks
    key_at, value_at = heads * HD, (heads + 1) * HD
    scale = HD ** (-0.5)
    place_pieces(table, [grads], tree, blocks, True)
    keys[...] = jnp.zeros_like(keys)
    values[...] = jnp.zeros_like(values)

    def turn_back(rows, here):
        return rows * cosine[here, :] + pltpu.roll(rows * sine[here, :], HD // 2, 1)

    for block in range(blocks):
        here = slice(block * block_len, (block + 1) * block_len)
        stacked = stack_heads(rotated, block, block_len, heads)
        cotangent = stack_heads(tree, block, block_len, heads)
        found = segments(table, rotated, block, block_len, key_at, value_at)
        probs = block_probs(stacked, found, block_len, scale)
        prob_grads = [dot_nt(cotangent, part) for _, _, _, part in found]
        delta = jnp.sum(probs[0] * prob_grads[0], axis=-1, keepdims=True)
        for part, grad in zip(probs[1:], prob_grads[1:]):
            delta = delta + jnp.sum(part * grad, axis=-1, keepdims=True)
        query_grad = None
        for (start, size, key_rows, _), part, grad in zip(found, probs, prob_grads):
            score_grad = (part * (grad - delta)).astype(bf16)
            term = dot_nn(score_grad, key_rows)
            query_grad = term if query_grad is None else query_grad + term
            there = pl.ds(start, size)
            keys[there, :] += dot_tn(score_grad, stacked) * scale
            values[there, :] += dot_tn(part.astype(bf16), cotangent)
        query_grad = query_grad * scale
        for h in range(heads):
            rows = query_grad[h * block_len : (h + 1) * block_len, :]
            result[here, h * HD : (h + 1) * HD] = turn_back(rows, here).astype(bf16)

    def finish(block, carry):
        here = pl.ds(pl.multiple_of(block * block_len, block_len), block_len)
        result[here, key_at : key_at + HD] = turn_back(keys[here, :], here).astype(bf16)
        result[here, value_at : value_at + HD] = values[here, :].astype(bf16)
        return carry

    lax.fori_loop(0, blocks, finish, 0)
    place_pieces(table, [packed_near, packed_far], result, blocks, False)


def attention_calls(length, blocks, heads):
    width = (heads + 2) * HD
    vmem = pl.BlockSpec(memory_space=pltpu.VMEM)
    smem = pl.BlockSpec(memory_space=pltpu.SMEM)
    params = pltpu.CompilerParams(vmem_limit_bytes=VMEM)
    pairs = (TRUNK * (TRUNK + 1) // 2 + (blocks - TRUNK) * (TRUNK + 1) + 4) * heads
    pairs = pairs * (length // blocks) ** 2

    def forward(*operands):
        return attend_kernel(blocks, heads, *operands)

    def backward(*operands):
        return attend_back_kernel(blocks, heads, *operands)

    ahead = pl.pallas_call(
        forward,
        in_specs=[smem] + [vmem] * 3,
        out_specs=[vmem] * 3,
        out_shape=[shaped(length // 2, heads * HD, bf16)] * 2 + [shaped(length, width, bf16)],
        scratch_shapes=[pltpu.VMEM((length, width), f32), pltpu.VMEM((length, heads * HD), bf16)],
        compiler_params=params,
        cost_estimate=cost(16 * pairs * HD, length * width * 8),
        name="attend",
    )
    back = pl.pallas_call(
        backward,
        in_specs=[smem] + [vmem] * 4,
        out_specs=[vmem] * 2,
        out_shape=[shaped(length // 2, width, bf16)] * 2,
        scratch_shapes=[
            pltpu.VMEM((length, heads * HD), bf16),
            pltpu.VMEM((length, HD), f32),
            pltpu.VMEM((length, HD), f32),
            pltpu.VMEM((length, width), bf16),
        ],
        compiler_params=params,
        cost_estimate=cost(24 * pairs * HD, length * width * 8),
        name="attend_back",
    )
    return ahead, back


def rotation_tables(blocks, block_len):
    depths = [min(block, TRUNK) + (block >= TRUNK + BRANCH) for block in range(blocks)]
    length = blocks * block_len
    places = jnp.arange(length, dtype=jnp.int32)
    row_depth = jnp.zeros((length,), jnp.int32)
    for block, depth in enumerate(depths):
        row_depth = jnp.where(places // block_len == block, depth, row_depth)
    position = (row_depth * block_len + places % block_len).astype(f32)
    half = HD // 2
    freqs = jnp.exp(jnp.arange(half, dtype=f32) * (-2.0 * math.log(10000.0) / HD))
    angles = position[:, None] * freqs[None, :]
    cosine, sine = jnp.cos(angles), jnp.sin(angles)
    return (
        jnp.concatenate([cosine, cosine], axis=1),
        jnp.concatenate([-sine, sine], axis=1),
    )


def spec(block, index):
    return pl.BlockSpec(block, index)


def whole(shape):
    return pl.BlockSpec(shape, lambda *_: (0,) * len(shape))


def cost(flops, moved):
    return pl.CostEstimate(flops=flops // SHARE, bytes_accessed=moved // SHARE, transcendentals=0)


def shaped(rows, columns, kind):
    return jax.ShapeDtypeStruct((rows, columns), kind)


def in_hbm(rows, columns, kind):
    return pltpu.HBM((rows, columns), kind)


def runs(order, width):
    run = width // order.shape[0]
    for j in range(order.shape[0]):
        yield slice(j * run, (j + 1) * run), pl.ds(pl.multiple_of(order[j] * run, HD), run)


def row_call(kernel, name, rows, tile, order, operands, results):
    def place(array, offset):
        if offset is None:
            return whole(array.shape)
        steps = array.shape[0] // tile
        return spec((tile, array.shape[1]), lambda i: ((i + offset) % steps, 0))

    return pl.pallas_call(
        kernel,
        grid=(rows // tile,),
        in_specs=[pl.BlockSpec(memory_space=pltpu.SMEM)] + [place(*pair) for pair in operands],
        out_specs=[spec((tile, columns), lambda i: (i, 0)) for columns, _ in results],
        out_shape=[shaped(rows, columns, kind) for columns, kind in results],
        compiler_params=pltpu.CompilerParams(vmem_limit_bytes=VMEM),
        cost_estimate=cost(rows * 2048 * 10, rows * 2048 * 8),
        name=name,
    )(order, *[array for array, _ in operands])


def row_mean(values):
    return jnp.mean(values, axis=-1, keepdims=True)


def norm_kernel(order, rows, gain, normed):
    values = rows[...].astype(f32)
    scale = lax.rsqrt(row_mean(values * values) + epsilon)
    for here, there in runs(order, rows.shape[1]):
        unit = rows[:, there].astype(f32) * scale
        normed[:, here] = (unit * gain[:, here]).astype(bf16)


def pack_kernel(*refs):
    gains, weights, result = refs[0], refs[1:-1], refs[-1]
    at = 0
    for weight in weights:
        result[:, at : at + weight.shape[1]] = weight[...]
        at += weight.shape[1]
    rows = jnp.concatenate([gains[...], jnp.zeros((HD - gains.shape[0], gains.shape[1]), f32)])
    result[:, at:] = rows.T.astype(bf16)


def gains_kernel(*refs):
    slots, first, second = refs[:-2], refs[-2], refs[-1]
    at = 0
    for slot in slots:
        columns = slot[...].astype(f32).T
        here = slice(at, at + slot.shape[0])
        first[:, here] = columns[0:1, :]
        second[:, here] = columns[1:2, :]
        at += slot.shape[0]


def kept_kernel(order, rows, keep, result):
    for here, there in runs(order, rows.shape[1]):
        result[:, here] = (rows[:, there].astype(f32) * keep[...]).astype(bf16)


def middle_kernel(order, rows, keep, mine, got, gain, middle, normed):
    for here, there in runs(order, rows.shape[1]):
        attended = mine[:, here].astype(f32) + got[:, here].astype(f32)
        middle[:, here] = rows[:, there].astype(f32) + keep[...] * attended
    values = middle[...]
    scale = lax.rsqrt(row_mean(values * values) + epsilon)
    normed[...] = (values * scale * gain[...]).astype(bf16)


def middle_back_kernel(order, cotangent, keep, mine, got, gain, middle, grad, kept):
    values = middle[...]
    scale = lax.rsqrt(row_mean(values * values) + epsilon)
    unit = values * scale
    scaled = (mine[...].astype(f32) + got[...].astype(f32)) * gain[...]
    mean = row_mean(scaled * unit)
    change = scale * (scaled - unit * mean)
    for here, there in runs(order, middle.shape[1]):
        total = cotangent[:, there].astype(f32) + change[:, here]
        grad[:, here] = total
        kept[:, here] = (keep[...] * total).astype(bf16)


def layer_kernel(order, middle, keep, mine, got, result):
    for here, there in runs(order, middle.shape[1]):
        branch = mine[:, here].astype(f32) + got[:, here].astype(f32)
        result[:, there] = (middle[:, here] + keep[...] * branch).astype(bf16)


def input_kernel(order, rows, mine, got, gain, middle_grad, result, scaled):
    values = rows[...].astype(f32)
    scale = lax.rsqrt(row_mean(values * values) + epsilon)
    scaled[...] = (mine[...].astype(f32) + got[...].astype(f32)) * gain[...]
    total = None
    for here, there in runs(order, rows.shape[1]):
        term = jnp.sum(scaled[:, here] * rows[:, there].astype(f32), axis=-1, keepdims=True)
        total = term if total is None else total + term
    mean = total * scale / rows.shape[1]
    for here, there in runs(order, rows.shape[1]):
        unit = rows[:, there].astype(f32) * scale
        result[:, there] = middle_grad[:, here] + scale * (scaled[:, here] - unit * mean)


def column_cuts(width):
    return [slice(at, min(at + 256, width)) for at in range(0, width, 256)]


def of_group(near, far, steps):
    tile = 2 * near.shape[0] // steps
    last = steps // 2 - 1
    return [
        spec((tile, near.shape[1]), lambda i: (jnp.minimum(i, last), 0)),
        spec((tile, far.shape[1]), lambda i: (jnp.maximum(i - last - 1, 0), 0)),
    ]


def resident(slots):
    return [
        pl.BlockSpec(slot.shape, lambda i: (0, 0), pipeline_mode=pl.Buffered(1)) for slot in slots
    ]


def in_halves(steps, work):
    for side in range(2):

        @pl.when(pl.program_id(0) // (steps // 2) == side)
        def _(side=side):
            work(side)


def product(rows, weights, cut):
    total, at = None, 0
    for weight in weights:
        term = dot_nn(rows[:, at : at + weight.shape[0]], weight[:, cut])
        total = term if total is None else total + term
        at += weight.shape[0]
    return total


def through(rows, weights, name, columns, kind):
    near, far = rows
    units = columns.stop - columns.start
    length, width = 2 * near.shape[0], near.shape[1]

    def kernel(*refs):
        slots, result = refs[2:-1], refs[-1]

        def work(side):
            for inside in column_cuts(units):
                cut = slice(columns.start + inside.start, columns.start + inside.stop)
                result[:, inside] = product(refs[side], slots, cut).astype(result.dtype)

        in_halves(2, work)

    return pl.pallas_call(
        kernel,
        grid=(2,),
        in_specs=of_group(near, far, 2) + resident(weights),
        out_specs=spec((length // 2, units), lambda i: (i, 0)),
        out_shape=shaped(length, units, kind),
        compiler_params=pltpu.CompilerParams(vmem_limit_bytes=VMEM),
        cost_estimate=cost(2 * length * width * units, 2 * width * (length + units)),
        name=name,
    )(near, far, *weights)


def gate_product(rows, hidden_grad, gates):
    near, far = rows
    length, units = hidden_grad.shape
    width = near.shape[1]

    def kernel(*refs):
        hidden_back, slots = refs[2], refs[3:-2]
        gate_out, up_grad = refs[-2:]

        def work(side):
            for cut in column_cuts(units):
                gate = product(refs[side], slots, cut)
                gate_out[:, cut] = gate
                active = gate / (1.0 + jnp.exp(-gate))
                up_grad[:, cut] = (hidden_back[:, cut].astype(f32) * active).astype(bf16)

        in_halves(4, work)

    here = spec((length // 4, units), lambda i: (i, 0))
    return pl.pallas_call(
        kernel,
        grid=(4,),
        in_specs=of_group(near, far, 4) + [here] + resident(gates),
        out_specs=[here] * 2,
        out_shape=[in_hbm(length, units, f32), shaped(length, units, bf16)],
        compiler_params=pltpu.CompilerParams(vmem_limit_bytes=VMEM),
        cost_estimate=cost(2 * length * width * units, 2 * width * (length + units)),
        name="gate",
    )(near, far, hidden_grad, *gates)


def up_product(rows, hidden_grad, gate, ups):
    near, far = rows
    length, units = hidden_grad.shape
    width = near.shape[1]
    up_slots = [slot for slots, _, _ in ups for slot in slots]

    def kernel(*refs):
        hidden_back, gate_in = refs[2], refs[3]
        up_refs = refs[4:-2]
        hidden, gate_grad = refs[-2:]

        def work(side):
            rows_in, at = refs[side], 0
            for slots, first, columns in ups:
                mine = up_refs[at : at + len(slots)]
                at += len(slots)
                for inside in column_cuts(columns.stop - columns.start):
                    cut = slice(first + inside.start, first + inside.stop)
                    there = slice(columns.start + inside.start, columns.start + inside.stop)
                    if len(slots) == 1 and mine[0].shape[0] < width:
                        depth = mine[0].shape[0]
                        count = width // depth
                        step = mine[0].shape[1] // count
                        upward = None
                        for s in range(count):
                            view = mine[0][:, there.start + s * step : there.stop + s * step]
                            term = dot_nn(rows_in[:, s * depth : (s + 1) * depth], view)
                            upward = term if upward is None else upward + term
                    else:
                        upward = product(rows_in, mine, there)
                    value = gate_in[:, cut]
                    sigma = 1.0 / (1.0 + jnp.exp(-value))
                    back = hidden_back[:, cut].astype(f32) * upward * sigma
                    hidden[:, cut] = (value * sigma * upward).astype(bf16)
                    gate_grad[:, cut] = (back * (1.0 + value * (1.0 - sigma))).astype(bf16)

        in_halves(4, work)

    here = spec((length // 4, units), lambda i: (i, 0))
    return pl.pallas_call(
        kernel,
        grid=(4,),
        in_specs=of_group(near, far, 4) + [here, here] + resident(up_slots),
        out_specs=[here] * 2,
        out_shape=[shaped(length, units, bf16)] * 2,
        compiler_params=pltpu.CompilerParams(vmem_limit_bytes=VMEM),
        cost_estimate=cost(2 * length * width * units, 2 * width * (length + units)),
        name="up",
    )(near, far, hidden_grad, gate, *up_slots)


def back_rows(grads, weights, side, name, far=None):
    width = sum(array.shape[0] for array in weights[0][0][0])
    tile = min(512, min(array.shape[0] for parts in weights for w in parts for array in w[0]))
    first = grads[0]
    count = first[0].shape[0] if isinstance(first, tuple) else first.shape[0] // 2
    operands, specs, plan = [], [], [[] for _ in range(width // tile)]
    work = 0
    for grad, parts in zip(grads, weights):
        at = len(operands)
        if isinstance(grad, tuple):
            specs.append(spec(grad[side].shape, lambda j: (0, 0)))
            operands.append(grad[side])
        else:
            specs.append(spec((count, grad.shape[1]), lambda j: (side, 0)))
            operands.append(grad)
        for arrays, unit, columns in parts:
            start = 0
            for array, cut in zip(arrays, columns):
                tiles = array.shape[0] // tile
                for j in range(start, start + tiles):
                    plan[j].append((at, unit, cut, len(operands)))
                operands.append(array)
                specs.append(
                    spec(
                        (tile, array.shape[1]),
                        lambda j, start=start, tiles=tiles: (jnp.clip(j - start, 0, tiles - 1), 0),
                    )
                )
                start += tiles
                work += 2 * count * array.shape[0] * (cut.stop - cut.start)
    if far is not None:
        operands.append(far)
        specs.append(spec((count, tile), lambda j: (0, j)))
    ranges = []
    for j, terms in enumerate(plan):
        if ranges and ranges[-1][2] == terms:
            ranges[-1][1] = j + 1
        else:
            ranges.append([j, j + 1, terms])

    def kernel(*refs):
        result = refs[-1]
        for low, high, terms in ranges:

            @pl.when((pl.program_id(0) >= low) & (pl.program_id(0) < high))
            def _(terms=terms):
                total = None
                for at, unit, cut, place in terms:
                    units = cut.stop - cut.start
                    term = dot_nt(refs[at][:, unit : unit + units], refs[place][:, cut])
                    total = term if total is None else total + term
                if far is not None:
                    total = total + refs[-2][...].astype(f32)
                result[...] = total.astype(result.dtype)

    return pl.pallas_call(
        kernel,
        grid=(width // tile,),
        in_specs=specs,
        out_specs=spec((count, tile), lambda j: (0, j)),
        out_shape=shaped(count, width, bf16),
        compiler_params=pltpu.CompilerParams(vmem_limit_bytes=VMEM),
        cost_estimate=cost(work, 2 * sum(operand.size for operand in operands)),
        name=name,
    )(*operands)


def grad_terms(near, far, refs, columns, pair):
    count = near.shape[0]
    if pair:
        first, second = refs[0][:, columns], refs[1][:, columns]
    else:
        first, second = refs[0][:count, columns], refs[0][count:, columns]
    return (dot_tn(near[...], first) + dot_tn(far[...], second)).astype(bf16)


def weight_part(rows, grads, half, s, name, columns=None, parts=1):
    near, far = rows
    pair = isinstance(grads, tuple)
    units = grads[0].shape[1] if pair else grads.shape[1]
    columns = slice(0, units) if columns is None else columns
    wide = columns.stop - columns.start
    tile = min(512, half) if parts == 1 else half // 4
    tiles = half // tile
    edges = [0, tiles] if parts == 1 else [0, 1, tiles]
    count = near.shape[0]
    row_spec = spec((count, tile), lambda j: (0, s * tiles + j))
    operands = grads if pair else (grads,)

    def kernel(near_rows, far_rows, *refs):
        total = grad_terms(near_rows, far_rows, refs, columns, pair)
        for part in range(parts):

            @pl.when((pl.program_id(0) >= edges[part]) & (pl.program_id(0) < edges[part + 1]))
            def _(part=part):
                refs[len(operands) + part][...] = total

    found = pl.pallas_call(
        kernel,
        grid=(tiles,),
        in_specs=[row_spec, row_spec] + [whole(operand.shape) for operand in operands],
        out_specs=[
            spec(
                (tile, wide),
                lambda j, part=part: (
                    jnp.clip(j, edges[part], edges[part + 1] - 1) - edges[part],
                    0,
                ),
            )
            for part in range(parts)
        ],
        out_shape=[
            in_hbm((edges[part + 1] - edges[part]) * tile, wide, bf16) for part in range(parts)
        ],
        compiler_params=pltpu.CompilerParams(vmem_limit_bytes=VMEM),
        cost_estimate=cost(4 * count * half * wide, 4 * count * (half + wide)),
        name=name,
    )(near, far, *operands)
    return found if parts > 1 else found[0]


def weight_slots(rows, grads, half, name, columns):
    near, far = rows
    wide = columns.stop - columns.start
    tile = min(512, half)
    tiles = half // tile
    inner = near.shape[1] // half
    count = near.shape[0]
    row_spec = spec((count, tile), lambda j: (0, j))

    def kernel(near_rows, far_rows, *refs):
        refs[-1][...] = grad_terms(near_rows, far_rows, refs, columns, False)

    return pl.pallas_call(
        kernel,
        grid=(inner * tiles,),
        in_specs=[row_spec, row_spec, whole(grads.shape)],
        out_specs=spec((tile, wide), lambda j: (j % tiles, j // tiles)),
        out_shape=in_hbm(half, inner * wide, bf16),
        compiler_params=pltpu.CompilerParams(vmem_limit_bytes=VMEM),
        cost_estimate=cost(4 * count * half * inner * wide, 4 * count * (half + wide)),
        name=name,
    )(near, far, grads)


def make_body(outer, inner, rows_axis, cores_axis):
    def body(
        hidden_in,
        skip_mask,
        parents,
        attention_gain,
        query_weight,
        key_weight,
        value_weight,
        output_weight,
        feedforward_gain,
        gate_weight,
        up_weight,
        down_weight,
        grad_out,
    ):
        part = hidden_in.shape[0]
        shard = query_weight.shape[0]
        pieces = rows_axis * cores_axis
        length = part * pieces
        near = part * rows_axis
        blocks = parents.shape[1]
        heads = query_weight.shape[1] // HD
        half = outer * shard
        width = half * inner
        tile = part // 2
        at_inner = lax.axis_index("inner")
        at_row = lax.axis_index("row")
        at_core = lax.axis_index("core")
        slots = range(inner)
        fence = lax.optimization_barrier

        order = jnp.stack(
            [z * inner + (at_inner + s) % inner for s in slots for z in range(outer)]
        ).astype(jnp.int32)

        def from_inner(values, k):
            return lax.ppermute(values, "inner", [((i + k) % inner, i) for i in range(inner)])

        def swap(values, axis):
            return lax.ppermute(values, axis, [(0, 1), (1, 0)])

        def spread(values):
            return [values] + [from_inner(values, s) for s in range(1, inner)]

        def gather(values):
            return lax.all_gather(values, "outer", axis=0, tiled=True)

        def scatter(values):
            return lax.psum_scatter(values, "outer", scatter_dimension=0, tiled=True)

        def collect(parts):
            total = parts[0].astype(f32)
            for s in range(1, inner):
                total = total + from_inner(parts[s], inner - s).astype(f32)
            return total

        keep_own = (1 - skip_mask).astype(f32)
        units = up_weight.shape[1]
        late = units if inner > 1 else 0
        joint_width = (heads + 2) * HD
        packed = pl.pallas_call(
            pack_kernel,
            out_shape=shaped(shard, joint_width + heads * HD + HD, bf16),
            compiler_params=pltpu.CompilerParams(vmem_limit_bytes=VMEM),
            cost_estimate=cost(0, shard * joint_width * 4),
            name="pack",
        )(
            jnp.stack([attention_gain.astype(f32), feedforward_gain.astype(f32)]),
            query_weight,
            key_weight,
            value_weight,
            output_weight,
        )
        keep_got = swap(keep_own, "row")
        row_x = swap(hidden_in, "row")
        row_g = swap(grad_out, "row")
        up_late = jnp.concatenate(spread(up_weight[:, units - late :]), axis=1) if late else None
        row_x, keep_got, up_late = fence((row_x, keep_got, up_late))
        near_x = jnp.concatenate([hidden_in, row_x], axis=0)
        far_x = swap(near_x, "core")
        packed_own = gather(packed)
        packed_own, far_x = fence((packed_own, far_x))
        packed_slots = spread(packed_own)
        keep = jnp.concatenate([keep_own, keep_got], axis=0)[:, None]
        near_g = jnp.concatenate([grad_out, row_g], axis=0)
        (near_branch,) = row_call(
            kept_kernel, "kept", near, tile, order, [(near_g, 0), (keep, 0)], [(width, bf16)]
        )
        far_branch = swap(near_branch, "core")
        down_own = gather(down_weight)
        gate_own = gather(gate_weight)
        early = units - late
        up_own = gather(up_weight[:, :early]) if early else None
        up_both = [gather(up_late)] if late else []

        cosine, sine = rotation_tables(blocks, length // blocks)
        starts = [
            (((at_row + dy) % 2) * cores_axis + (at_core + dc) % 2) * part
            for dc in range(2)
            for dy in range(2)
        ]
        table = jnp.concatenate([parents[0], jnp.stack(starts).astype(jnp.int32)])
        packed_slots, near_branch, far_branch, down_own = fence(
            (packed_slots, near_branch, far_branch, down_own)
        )
        quarter = half // 4
        down_got = [from_inner(down_own[:quarter], 1)] if inner > 1 else []
        gain_at = joint_width + heads * HD
        joint_columns = slice(0, joint_width)
        output_columns = slice(joint_width, gain_at)
        gain_one, gain_two = pl.pallas_call(
            gains_kernel,
            grid=(1,),
            in_specs=[spec((half, HD), lambda i: (0, gain_at // HD))] * inner,
            out_specs=[whole((1, width))] * 2,
            out_shape=[shaped(1, width, f32)] * 2,
            compiler_params=pltpu.CompilerParams(vmem_limit_bytes=VMEM),
            cost_estimate=cost(0, width * 8),
            name="gains",
        )(*packed_slots)
        all_branch = (near_branch, far_branch)

        def norm(rows, name):
            (result,) = row_call(
                norm_kernel, name, near, tile, order, [(rows, 0), (gain_one, None)], [(width, bf16)]
            )
            return result

        normed = (norm(near_x, "norm_near"), norm(far_x, "norm_far"))

        def all_of(arrays):
            return [(arrays, 0, [slice(0, array.shape[1]) for array in arrays])]

        attend, attend_back = attention_calls(length, blocks, heads)
        raw = through(normed, packed_slots, "joint", joint_columns, f32)
        if inner > 1:
            raw, down_got, down_own = fence((raw, down_got, down_own))
            down_got = down_got + [from_inner(down_own[quarter : 2 * quarter], 1)]
        mixed_near, mixed_far, rotated = attend(table, raw, cosine, sine)
        if inner > 1:
            mixed_near, mixed_far, down_got, down_own = fence(
                (mixed_near, mixed_far, down_got, down_own)
            )
            down_got = down_got + [from_inner(down_own[2 * quarter : 3 * quarter], 1)]
        mixed = (mixed_near, mixed_far)

        def packed_plan(columns):
            return [(packed_slots, 0, [columns] * inner)]

        attended_plan = [packed_plan(output_columns)]
        attended_far = swap(back_rows([mixed], attended_plan, 1, "attended_far"), "core")
        attended = back_rows([mixed], attended_plan, 0, "attended_near")
        attended = (attended.astype(f32) + attended_far.astype(f32)).astype(bf16)
        attended, gate_own, down_got = fence((attended, gate_own, down_got))
        if inner > 1:
            down_got = down_got + [from_inner(down_own[3 * quarter :], 1)]
        weight_down = [down_own] + down_got
        got = swap(attended, "row")
        weight_gate = spread(gate_own)
        hidden_grad = through(all_branch, weight_down, "hidden_grad", slice(0, units), bf16)
        got, hidden_grad, up_own = fence((got, hidden_grad, up_own))
        weight_up = spread(up_own) if early else []
        swapped = part // tile
        middle, normed_ff = row_call(
            middle_kernel,
            "middle",
            near,
            tile,
            order,
            [(near_x, 0), (keep, 0), (attended, 0), (got, swapped), (gain_two, None)],
            [(width, f32), (width, bf16)],
        )
        all_ff = (normed_ff, swap(normed_ff, "core"))

        up_parts = [(weight_up, 0, slice(0, early))] if early else []
        up_plan = [(weight_up, 0, [slice(0, early)] * inner)] if early else []
        if late:
            up_parts.append((up_both, early, slice(0, late)))
            up_plan.append((up_both * inner, early, [slice(s * late, (s + 1) * late) for s in slots]))
        gate, up_grad = gate_product(all_ff, hidden_grad, weight_gate)
        def weight_parts(rows, grads, name, columns=None):
            return [weight_part(rows, grads, half, s, name, columns) for s in slots]

        def core_sum(grads, weights, name):
            far = swap(back_rows(grads, weights, 1, name + "_far"), "core")
            return back_rows(grads, weights, 0, name + "_near", far)

        last = inner - 1
        up_late_sums = None
        if late:
            up_late_parts = weight_slots(all_ff, up_grad, half, "grad_up_late", slice(early, units))
            gate, up_grad, up_late_parts = fence((gate, up_grad, up_late_parts))
            up_late_sums = scatter(up_late_parts)
        hidden_ff, gate_grad = up_product(all_ff, hidden_grad, gate, up_parts)
        down_last = weight_part(all_branch, hidden_ff, half, last, "grad_down")
        gate_grad, up_grad, down_last = fence((gate_grad, up_grad, down_last))
        back_plan = ([gate_grad, up_grad], [all_of(weight_gate), up_plan])
        ff_far = back_rows(*back_plan, 1, "normed_ff_grad_far")
        ff_far, gate_grad, up_grad = fence((ff_far, gate_grad, up_grad))
        ff_far = swap(ff_far, "core")
        gate_last = weight_part(all_ff, gate_grad, half, last, "grad_gate", parts=2)
        gate_grad, up_grad, gate_last = fence((gate_grad, up_grad, gate_last))
        back_plan = ([gate_grad, up_grad], [all_of(weight_gate), up_plan])
        ff_grad = back_rows(*back_plan, 0, "normed_ff_grad_near", ff_far)
        ff_grad, gate_grad, up_grad, hidden_ff = fence((ff_grad, gate_grad, up_grad, hidden_ff))
        ff_got = swap(ff_grad, "row")

        def to_last(values):
            return from_inner(values, inner - last) if last else None

        def plus(values, got):
            if got is None:
                return values
            return (values.astype(f32) + got.astype(f32)).astype(bf16)

        down_got = to_last(down_last)
        gate_got = [to_last(values) for values in gate_last]
        up_last = up_got = None
        if early:
            up_last = weight_part(all_ff, up_grad, half, last, "grad_up", slice(0, early))
            up_got = to_last(up_last)
        own = [down_last, jnp.concatenate(gate_last, axis=0), up_last]
        if last:
            own = [
                weight_part(all_branch, hidden_ff, half, 0, "grad_down"),
                weight_part(all_ff, gate_grad, half, 0, "grad_gate"),
                weight_part(all_ff, up_grad, half, 0, "grad_up", slice(0, early))
                if early
                else None,
            ]
        branch_plan = ([hidden_ff], [all_of(weight_down)])
        branch_far = back_rows(*branch_plan, 1, "branch_far")
        branch_near = back_rows(*branch_plan, 0, "branch_near")
        down_own, down_got, own[1], branch_far, branch_near = fence(
            (own[0], down_got, own[1], branch_far, branch_near)
        )
        down_sum = plus(down_own, down_got)
        ff_got, own, up_last, gate_got[0] = fence((ff_got, own, up_last, gate_got[0]))
        grad_down = scatter(down_sum)
        middle_grad, attended_grad = row_call(
            middle_back_kernel,
            "middle_back",
            near,
            tile,
            order,
            [
                (near_g, 0),
                (keep, 0),
                (ff_grad, 0),
                (ff_got, swapped),
                (gain_two, None),
                (middle, 0),
            ],
            [(width, f32), (width, bf16)],
        )
        all_attended = (attended_grad, swap(attended_grad, "core"))

        mixed_grad = through(all_attended, packed_slots, "mixed_grad", output_columns, bf16)
        output_last = weight_part(all_attended, mixed, half, last, "grad_output")
        mixed_grad, output_last = fence((mixed_grad, output_last))
        packed_grad = tuple(attend_back(table, rotated, mixed_grad, cosine, sine))
        joint_last = weight_part(normed, packed_grad, half, last, "grad_joint")
        packed_grad, gate_got, up_late_sums, joint_last = fence(
            (packed_grad, gate_got, up_late_sums, joint_last)
        )
        gate_sums = own[1]
        if last:
            rows = half // 4
            gate_sums = jnp.concatenate(
                [plus(own[1][:rows], gate_got[0]), plus(own[1][rows:], gate_got[1])], axis=0
            )
        grad_gate = scatter(gate_sums)
        normed_grad = core_sum([packed_grad], [packed_plan(joint_columns)], "normed_grad")
        normed_got = swap(normed_grad[part:], "row")
        output_sum, joint_sum = output_last, joint_last
        if last:
            output_own = weight_part(all_attended, mixed, half, 0, "grad_output")
            joint_own = weight_part(normed, packed_grad, half, 0, "grad_joint")
            output_own, joint_own, normed_grad = fence((output_own, joint_own, normed_grad))
            output_got, joint_got = to_last(output_last), to_last(joint_last)
            output_got, joint_got, normed_got, branch_far = fence(
                (output_got, joint_got, normed_got, branch_far)
            )
            output_sum = plus(output_own, output_got)
            joint_sum = plus(joint_own, joint_got)
        branch = (branch_near.astype(f32) + swap(branch_far, "core").astype(f32)).astype(bf16)
        branch_got = swap(branch[part:], "row")
        (layer_out,) = row_call(
            layer_kernel,
            "layer",
            part,
            tile,
            order,
            [(middle, 0), (keep, 0), (branch, 0), (branch_got, 0)],
            [(width, bf16)],
        )
        attention_sum = jnp.concatenate([output_sum, joint_sum], axis=1)
        grad_up = None
        if early:
            up_got, grad_down = fence((up_got, grad_down))
            grad_up = scatter(plus(own[2], up_got)).astype(f32)
        attention_sum, grad_down = fence((attention_sum, grad_down))
        attention_sum = scatter(attention_sum)
        (input_grad,) = pl.pallas_call(
            input_kernel,
            grid=(part // tile,),
            in_specs=[
                pl.BlockSpec(memory_space=pltpu.SMEM),
                spec((tile, width), lambda i: (i, 0)),
                spec((tile, width), lambda i: (i, 0)),
                spec((tile, width), lambda i: (i, 0)),
                whole((1, width)),
                spec((tile, width), lambda i: (i, 0)),
            ],
            out_specs=[spec((tile, width), lambda i: (i, 0))],
            out_shape=[shaped(part, width, f32)],
            scratch_shapes=[pltpu.VMEM((tile, width), f32)],
            compiler_params=pltpu.CompilerParams(vmem_limit_bytes=VMEM),
            cost_estimate=cost(part * width * 10, part * width * 16),
            name="input_grad",
        )(order, hidden_in, normed_grad, normed_got, gain_one, middle_grad)
        if late:
            grad_late = collect([up_late_sums[:, s * late : (s + 1) * late] for s in slots])
            grad_up = grad_late if grad_up is None else jnp.concatenate([grad_up, grad_late], axis=1)
        grad_down, grad_gate, grad_up = [
            grad.astype(f32) for grad in (grad_down, grad_gate, grad_up)
        ]

        attention_sum, input_grad, layer_out = fence((attention_sum, input_grad, layer_out))
        attention_sum = attention_sum.astype(f32)
        grad_output = attention_sum[:, : heads * HD]
        grad_joint = attention_sum[:, heads * HD :]

        def gain_terms(pairs, gain):
            total = None
            for weight, grad in pairs:
                term = jnp.sum(weight.astype(f32) * grad, axis=1)
                total = term if total is None else total + term
            return total / gain.astype(f32)

        query_width = heads * HD
        grad_query = grad_joint[:, :query_width]
        grad_key = grad_joint[:, query_width : query_width + HD]
        grad_value = grad_joint[:, query_width + HD :]
        gain_grads = jnp.stack(
            [
                gain_terms(
                    [
                        (query_weight, grad_query),
                        (key_weight, grad_key),
                        (value_weight, grad_value),
                    ],
                    attention_gain,
                ),
                gain_terms([(gate_weight, grad_gate), (up_weight, grad_up)], feedforward_gain),
            ]
        )
        gain_grads = gain_grads + swap(gain_grads, "core")
        gain_grads = gain_grads + swap(gain_grads, "row")
        return (
            layer_out,
            input_grad,
            gain_grads[0],
            grad_query,
            grad_key,
            grad_value,
            grad_output,
            gain_grads[1],
            grad_gate,
            grad_up,
            grad_down,
        )

    return body


def solution(mesh):
    replicas = mesh.shape["dp"]
    inner = 2 if replicas % 2 == 0 else 1
    outer = replicas // inner
    cores = mesh.shape["tensor"] // 2
    grid = Mesh(mesh.devices.reshape(outer, inner, 2, cores), ("outer", "inner", "row", "core"))
    dp, tensor = ("outer", "inner"), ("row", "core")
    both = dp + tensor
    weight = P(dp, tensor)
    return jax.shard_map(
        make_body(outer, inner, 2, cores),
        mesh=grid,
        in_specs=(
            P(both, None),
            P(both),
            P(dp, None),
            P(dp),
            weight,
            weight,
            weight,
            weight,
            P(dp),
            weight,
            weight,
            weight,
            P(both, None),
        ),
        out_specs=(
            P(both, None),
            P(both, None),
            P(dp),
            weight,
            weight,
            weight,
            weight,
            P(dp),
            weight,
            weight,
            weight,
        ),
        check_vma=False,
    )
```

```python
import math

import jax
import jax.numpy as jnp
from jax import lax
from jax.experimental import pallas as pl
from jax.experimental.pallas import tpu as pltpu
from jax.sharding import Mesh
from jax.sharding import PartitionSpec as P

HD = 128
TRUNK = 4
BRANCH = 2
PIECES = 4
SHARE = 4
VMEM = 32 * 2**20

epsilon = 1e-05
masked_score = -1000000000.0
bf16 = jnp.bfloat16
f32 = jnp.float32


def dot_nn(a, b):
    return lax.dot_general(a, b, (((1,), (0,)), ((), ())), preferred_element_type=f32)


def dot_nt(a, b):
    return lax.dot_general(a, b, (((1,), (1,)), ((), ())), preferred_element_type=f32)


def dot_tn(a, b):
    return lax.dot_general(a, b, (((0,), (0,)), ((), ())), preferred_element_type=f32)


def place_pieces(table, groups, tree, blocks, into_tree):
    size = tree.shape[0] // PIECES
    piece = 0
    for group in groups:
        for at in range(0, group.shape[0], size):
            start = pl.multiple_of(table[blocks + piece], 64)
            here = slice(at, at + size)
            if into_tree:
                tree[pl.ds(start, size), :] = group[here, :].astype(tree.dtype)
            else:
                group[here, :] = tree[pl.ds(start, size), :].astype(group.dtype)
            piece += 1


def segments(table, rows, block, block_len, key_at, value_at):
    def part(start, size):
        return (
            rows[pl.ds(start, size), key_at : key_at + HD],
            rows[pl.ds(start, size), value_at : value_at + HD],
        )

    found = []
    trunk = min(block, TRUNK)
    if trunk:
        found.append((0, trunk * block_len) + part(0, trunk * block_len))
    if block >= TRUNK + BRANCH:
        start = pl.multiple_of(table[block] * block_len, block_len)
        found.append((start, block_len) + part(start, block_len))
    start = block * block_len
    found.append((start, block_len) + part(start, block_len))
    return found


def block_probs(stacked, found, block_len, scale):
    rows = stacked.shape[0]
    scores = [dot_nt(stacked, keys) * scale for _, _, keys, _ in found]
    row = lax.broadcasted_iota(jnp.int32, (rows, block_len), 0) % block_len
    column = lax.broadcasted_iota(jnp.int32, (rows, block_len), 1)
    scores[-1] = jnp.where(column <= row, scores[-1], masked_score)
    top = jnp.max(scores[0], axis=-1, keepdims=True)
    for part in scores[1:]:
        top = jnp.maximum(top, jnp.max(part, axis=-1, keepdims=True))
    raw = [jnp.exp(part - top) for part in scores]
    total = jnp.sum(raw[0], axis=-1, keepdims=True)
    for part in raw[1:]:
        total = total + jnp.sum(part, axis=-1, keepdims=True)
    inverse = 1.0 / total
    return [part * inverse for part in raw]


def stack_heads(rows, block, block_len, heads):
    here = slice(block * block_len, (block + 1) * block_len)
    return jnp.concatenate([rows[here, h * HD : (h + 1) * HD] for h in range(heads)], axis=0)


def attend_kernel(
    blocks, heads, table, raw, cosine, sine, mixed_near, mixed_far, rotated, tree, result
):
    length = tree.shape[0]
    block_len = length // blocks
    key_at, value_at = heads * HD, (heads + 1) * HD
    place_pieces(table, [raw], tree, blocks, True)

    def turn(block, carry):
        here = pl.ds(pl.multiple_of(block * block_len, block_len), block_len)
        cos, sin = cosine[here, :], sine[here, :]
        for h in range(heads + 1):
            there = slice(h * HD, (h + 1) * HD)
            values = tree[here, there]
            turned = values * cos + pltpu.roll(values, HD // 2, 1) * sin
            rotated[here, there] = turned.astype(bf16)
        rotated[here, value_at : value_at + HD] = tree[here, value_at : value_at + HD].astype(bf16)
        return carry

    lax.fori_loop(0, blocks, turn, 0)
    for block in range(blocks):
        stacked = stack_heads(rotated, block, block_len, heads)
        found = segments(table, rotated, block, block_len, key_at, value_at)
        probs = block_probs(stacked, found, block_len, HD ** (-0.5))
        out = dot_nn(probs[0].astype(bf16), found[0][3])
        for part, (_, _, _, values) in zip(probs[1:], found[1:]):
            out = out + dot_nn(part.astype(bf16), values)
        out = out.astype(bf16)
        for h in range(heads):
            result[block * block_len : (block + 1) * block_len, h * HD : (h + 1) * HD] = out[
                h * block_len : (h + 1) * block_len, :
            ]
    place_pieces(table, [mixed_near, mixed_far], result, blocks, False)


def attend_back_kernel(
    blocks,
    heads,
    table,
    rotated,
    grads,
    cosine,
    sine,
    packed_near,
    packed_far,
    tree,
    keys,
    values,
    result,
):
    length = rotated.shape[0]
    block_len = length // blocks
    key_at, value_at = heads * HD, (heads + 1) * HD
    scale = HD ** (-0.5)
    place_pieces(table, [grads], tree, blocks, True)
    keys[...] = jnp.zeros_like(keys)
    values[...] = jnp.zeros_like(values)

    def turn_back(rows, here):
        return rows * cosine[here, :] + pltpu.roll(rows * sine[here, :], HD // 2, 1)

    for block in range(blocks):
        here = slice(block * block_len, (block + 1) * block_len)
        stacked = stack_heads(rotated, block, block_len, heads)
        cotangent = stack_heads(tree, block, block_len, heads)
        found = segments(table, rotated, block, block_len, key_at, value_at)
        probs = block_probs(stacked, found, block_len, scale)
        prob_grads = [dot_nt(cotangent, part) for _, _, _, part in found]
        delta = jnp.sum(probs[0] * prob_grads[0], axis=-1, keepdims=True)
        for part, grad in zip(probs[1:], prob_grads[1:]):
            delta = delta + jnp.sum(part * grad, axis=-1, keepdims=True)
        query_grad = None
        for (start, size, key_rows, _), part, grad in zip(found, probs, prob_grads):
            score_grad = (part * (grad - delta)).astype(bf16)
            term = dot_nn(score_grad, key_rows)
            query_grad = term if query_grad is None else query_grad + term
            there = pl.ds(start, size)
            keys[there, :] += dot_tn(score_grad, stacked) * scale
            values[there, :] += dot_tn(part.astype(bf16), cotangent)
        query_grad = query_grad * scale
        for h in range(heads):
            rows = query_grad[h * block_len : (h + 1) * block_len, :]
            result[here, h * HD : (h + 1) * HD] = turn_back(rows, here).astype(bf16)

    def finish(block, carry):
        here = pl.ds(pl.multiple_of(block * block_len, block_len), block_len)
        result[here, key_at : key_at + HD] = turn_back(keys[here, :], here).astype(bf16)
        result[here, value_at : value_at + HD] = values[here, :].astype(bf16)
        return carry

    lax.fori_loop(0, blocks, finish, 0)
    place_pieces(table, [packed_near, packed_far], result, blocks, False)


def attention_calls(length, blocks, heads):
    width = (heads + 2) * HD
    vmem = pl.BlockSpec(memory_space=pltpu.VMEM)
    smem = pl.BlockSpec(memory_space=pltpu.SMEM)
    params = pltpu.CompilerParams(vmem_limit_bytes=VMEM)
    pairs = (TRUNK * (TRUNK + 1) // 2 + (blocks - TRUNK) * (TRUNK + 1) + 4) * heads
    pairs = pairs * (length // blocks) ** 2

    def forward(*operands):
        return attend_kernel(blocks, heads, *operands)

    def backward(*operands):
        return attend_back_kernel(blocks, heads, *operands)

    ahead = pl.pallas_call(
        forward,
        in_specs=[smem] + [vmem] * 3,
        out_specs=[vmem] * 3,
        out_shape=[shaped(length // 2, heads * HD, bf16)] * 2 + [shaped(length, width, bf16)],
        scratch_shapes=[pltpu.VMEM((length, width), f32), pltpu.VMEM((length, heads * HD), bf16)],
        compiler_params=params,
        cost_estimate=cost(16 * pairs * HD, length * width * 8),
        name="attend",
    )
    back = pl.pallas_call(
        backward,
        in_specs=[smem] + [vmem] * 4,
        out_specs=[vmem] * 2,
        out_shape=[shaped(length // 2, width, bf16)] * 2,
        scratch_shapes=[
            pltpu.VMEM((length, heads * HD), bf16),
            pltpu.VMEM((length, HD), f32),
            pltpu.VMEM((length, HD), f32),
            pltpu.VMEM((length, width), bf16),
        ],
        compiler_params=params,
        cost_estimate=cost(24 * pairs * HD, length * width * 8),
        name="attend_back",
    )
    return ahead, back


def rotation_tables(blocks, block_len):
    depths = [min(block, TRUNK) + (block >= TRUNK + BRANCH) for block in range(blocks)]
    length = blocks * block_len
    places = jnp.arange(length, dtype=jnp.int32)
    row_depth = jnp.zeros((length,), jnp.int32)
    for block, depth in enumerate(depths):
        row_depth = jnp.where(places // block_len == block, depth, row_depth)
    position = (row_depth * block_len + places % block_len).astype(f32)
    half = HD // 2
    freqs = jnp.exp(jnp.arange(half, dtype=f32) * (-2.0 * math.log(10000.0) / HD))
    angles = position[:, None] * freqs[None, :]
    cosine, sine = jnp.cos(angles), jnp.sin(angles)
    return (
        jnp.concatenate([cosine, cosine], axis=1),
        jnp.concatenate([-sine, sine], axis=1),
    )


def spec(block, index):
    return pl.BlockSpec(block, index)


def whole(shape):
    return pl.BlockSpec(shape, lambda *_: (0,) * len(shape))


def cost(flops, moved):
    return pl.CostEstimate(flops=flops // SHARE, bytes_accessed=moved // SHARE, transcendentals=0)


def shaped(rows, columns, kind):
    return jax.ShapeDtypeStruct((rows, columns), kind)


def in_hbm(rows, columns, kind):
    return pltpu.HBM((rows, columns), kind)


def runs(order, width):
    run = width // order.shape[0]
    for j in range(order.shape[0]):
        yield slice(j * run, (j + 1) * run), pl.ds(pl.multiple_of(order[j] * run, HD), run)


def row_call(kernel, name, rows, tile, order, operands, results):
    def place(array, offset):
        if offset is None:
            return whole(array.shape)
        steps = array.shape[0] // tile
        return spec((tile, array.shape[1]), lambda i: ((i + offset) % steps, 0))

    return pl.pallas_call(
        kernel,
        grid=(rows // tile,),
        in_specs=[pl.BlockSpec(memory_space=pltpu.SMEM)] + [place(*pair) for pair in operands],
        out_specs=[spec((tile, columns), lambda i: (i, 0)) for columns, _ in results],
        out_shape=[shaped(rows, columns, kind) for columns, kind in results],
        compiler_params=pltpu.CompilerParams(vmem_limit_bytes=VMEM),
        cost_estimate=cost(rows * 2048 * 10, rows * 2048 * 8),
        name=name,
    )(order, *[array for array, _ in operands])


def row_mean(values):
    return jnp.mean(values, axis=-1, keepdims=True)


def norm_kernel(order, rows, gain, normed):
    values = rows[...].astype(f32)
    scale = lax.rsqrt(row_mean(values * values) + epsilon)
    for here, there in runs(order, rows.shape[1]):
        unit = rows[:, there].astype(f32) * scale
        normed[:, here] = (unit * gain[:, here]).astype(bf16)


def pack_kernel(*refs):
    gains, weights, result = refs[0], refs[1:-1], refs[-1]
    at = 0
    for weight in weights:
        result[:, at : at + weight.shape[1]] = weight[...]
        at += weight.shape[1]
    rows = jnp.concatenate([gains[...], jnp.zeros((HD - gains.shape[0], gains.shape[1]), f32)])
    result[:, at:] = rows.T.astype(bf16)


def gains_kernel(*refs):
    slots, first, second = refs[:-2], refs[-2], refs[-1]
    at = 0
    for slot in slots:
        columns = slot[...].astype(f32).T
        here = slice(at, at + slot.shape[0])
        first[:, here] = columns[0:1, :]
        second[:, here] = columns[1:2, :]
        at += slot.shape[0]


def kept_kernel(order, rows, keep, result):
    for here, there in runs(order, rows.shape[1]):
        result[:, here] = (rows[:, there].astype(f32) * keep[...]).astype(bf16)


def middle_kernel(order, rows, keep, mine, got, gain, middle, normed):
    for here, there in runs(order, rows.shape[1]):
        attended = mine[:, here].astype(f32) + got[:, here].astype(f32)
        middle[:, here] = rows[:, there].astype(f32) + keep[...] * attended
    values = middle[...]
    scale = lax.rsqrt(row_mean(values * values) + epsilon)
    normed[...] = (values * scale * gain[...]).astype(bf16)


def middle_back_kernel(order, cotangent, keep, mine, got, gain, middle, grad, kept):
    values = middle[...]
    scale = lax.rsqrt(row_mean(values * values) + epsilon)
    unit = values * scale
    scaled = (mine[...].astype(f32) + got[...].astype(f32)) * gain[...]
    mean = row_mean(scaled * unit)
    change = scale * (scaled - unit * mean)
    for here, there in runs(order, middle.shape[1]):
        total = cotangent[:, there].astype(f32) + change[:, here]
        grad[:, here] = total
        kept[:, here] = (keep[...] * total).astype(bf16)


def layer_kernel(order, middle, keep, mine, got, result):
    for here, there in runs(order, middle.shape[1]):
        branch = mine[:, here].astype(f32) + got[:, here].astype(f32)
        result[:, there] = (middle[:, here] + keep[...] * branch).astype(bf16)


def input_kernel(order, rows, mine, got, gain, middle_grad, result, scaled):
    values = rows[...].astype(f32)
    scale = lax.rsqrt(row_mean(values * values) + epsilon)
    scaled[...] = (mine[...].astype(f32) + got[...].astype(f32)) * gain[...]
    total = None
    for here, there in runs(order, rows.shape[1]):
        term = jnp.sum(scaled[:, here] * rows[:, there].astype(f32), axis=-1, keepdims=True)
        total = term if total is None else total + term
    mean = total * scale / rows.shape[1]
    for here, there in runs(order, rows.shape[1]):
        unit = rows[:, there].astype(f32) * scale
        result[:, there] = middle_grad[:, here] + scale * (scaled[:, here] - unit * mean)


def column_cuts(width):
    return [slice(at, min(at + 256, width)) for at in range(0, width, 256)]


def of_group(near, far, steps):
    tile = 2 * near.shape[0] // steps
    last = steps // 2 - 1
    return [
        spec((tile, near.shape[1]), lambda i: (jnp.minimum(i, last), 0)),
        spec((tile, far.shape[1]), lambda i: (jnp.maximum(i - last - 1, 0), 0)),
    ]


def resident(slots):
    return [
        pl.BlockSpec(slot.shape, lambda i: (0, 0), pipeline_mode=pl.Buffered(1)) for slot in slots
    ]


def in_halves(steps, work):
    for side in range(2):

        @pl.when(pl.program_id(0) // (steps // 2) == side)
        def _(side=side):
            work(side)


def product(rows, weights, cut):
    total, at = None, 0
    for weight in weights:
        term = dot_nn(rows[:, at : at + weight.shape[0]], weight[:, cut])
        total = term if total is None else total + term
        at += weight.shape[0]
    return total


def through(rows, weights, name, columns, kind):
    near, far = rows
    units = columns.stop - columns.start
    length, width = 2 * near.shape[0], near.shape[1]

    def kernel(*refs):
        slots, result = refs[2:-1], refs[-1]

        def work(side):
            for inside in column_cuts(units):
                cut = slice(columns.start + inside.start, columns.start + inside.stop)
                result[:, inside] = product(refs[side], slots, cut).astype(result.dtype)

        in_halves(2, work)

    return pl.pallas_call(
        kernel,
        grid=(2,),
        in_specs=of_group(near, far, 2) + resident(weights),
        out_specs=spec((length // 2, units), lambda i: (i, 0)),
        out_shape=shaped(length, units, kind),
        compiler_params=pltpu.CompilerParams(vmem_limit_bytes=VMEM),
        cost_estimate=cost(2 * length * width * units, 2 * width * (length + units)),
        name=name,
    )(near, far, *weights)


def gate_product(rows, hidden_grad, gates):
    near, far = rows
    length, units = hidden_grad.shape
    width = near.shape[1]

    def kernel(*refs):
        hidden_back, slots = refs[2], refs[3:-2]
        gate_out, up_grad = refs[-2:]

        def work(side):
            for cut in column_cuts(units):
                gate = product(refs[side], slots, cut)
                gate_out[:, cut] = gate
                active = gate / (1.0 + jnp.exp(-gate))
                up_grad[:, cut] = (hidden_back[:, cut].astype(f32) * active).astype(bf16)

        in_halves(4, work)

    here = spec((length // 4, units), lambda i: (i, 0))
    return pl.pallas_call(
        kernel,
        grid=(4,),
        in_specs=of_group(near, far, 4) + [here] + resident(gates),
        out_specs=[here] * 2,
        out_shape=[in_hbm(length, units, f32), shaped(length, units, bf16)],
        compiler_params=pltpu.CompilerParams(vmem_limit_bytes=VMEM),
        cost_estimate=cost(2 * length * width * units, 2 * width * (length + units)),
        name="gate",
    )(near, far, hidden_grad, *gates)


def up_product(rows, hidden_grad, gate, ups):
    near, far = rows
    length, units = hidden_grad.shape
    width = near.shape[1]
    up_slots = [slot for slots, _, _ in ups for slot in slots]

    def kernel(*refs):
        hidden_back, gate_in = refs[2], refs[3]
        up_refs = refs[4:-2]
        hidden, gate_grad = refs[-2:]

        def work(side):
            rows_in, at = refs[side], 0
            for slots, first, columns in ups:
                mine = up_refs[at : at + len(slots)]
                at += len(slots)
                for inside in column_cuts(columns.stop - columns.start):
                    cut = slice(first + inside.start, first + inside.stop)
                    there = slice(columns.start + inside.start, columns.start + inside.stop)
                    if len(slots) == 1 and mine[0].shape[0] < width:
                        depth = mine[0].shape[0]
                        count = width // depth
                        step = mine[0].shape[1] // count
                        upward = None
                        for s in range(count):
                            view = mine[0][:, there.start + s * step : there.stop + s * step]
                            term = dot_nn(rows_in[:, s * depth : (s + 1) * depth], view)
                            upward = term if upward is None else upward + term
                    else:
                        upward = product(rows_in, mine, there)
                    value = gate_in[:, cut]
                    sigma = 1.0 / (1.0 + jnp.exp(-value))
                    back = hidden_back[:, cut].astype(f32) * upward * sigma
                    hidden[:, cut] = (value * sigma * upward).astype(bf16)
                    gate_grad[:, cut] = (back * (1.0 + value * (1.0 - sigma))).astype(bf16)

        in_halves(4, work)

    here = spec((length // 4, units), lambda i: (i, 0))
    return pl.pallas_call(
        kernel,
        grid=(4,),
        in_specs=of_group(near, far, 4) + [here, here] + resident(up_slots),
        out_specs=[here] * 2,
        out_shape=[shaped(length, units, bf16)] * 2,
        compiler_params=pltpu.CompilerParams(vmem_limit_bytes=VMEM),
        cost_estimate=cost(2 * length * width * units, 2 * width * (length + units)),
        name="up",
    )(near, far, hidden_grad, gate, *up_slots)


def back_rows(grads, weights, side, name, far=None, shape=shaped):
    width = sum(array.shape[0] for array in weights[0][0][0])
    tile = min(512, min(array.shape[0] for parts in weights for w in parts for array in w[0]))
    first = grads[0]
    count = first[0].shape[0] if isinstance(first, tuple) else first.shape[0] // 2
    operands, specs, plan = [], [], [[] for _ in range(width // tile)]
    work = 0
    for grad, parts in zip(grads, weights):
        at = len(operands)
        if isinstance(grad, tuple):
            specs.append(spec(grad[side].shape, lambda j: (0, 0)))
            operands.append(grad[side])
        else:
            specs.append(spec((count, grad.shape[1]), lambda j: (side, 0)))
            operands.append(grad)
        for arrays, unit, columns in parts:
            start = 0
            for array, cut in zip(arrays, columns):
                tiles = array.shape[0] // tile
                for j in range(start, start + tiles):
                    plan[j].append((at, unit, cut, len(operands)))
                operands.append(array)
                specs.append(
                    spec(
                        (tile, array.shape[1]),
                        lambda j, start=start, tiles=tiles: (jnp.clip(j - start, 0, tiles - 1), 0),
                    )
                )
                start += tiles
                work += 2 * count * array.shape[0] * (cut.stop - cut.start)
    if far is not None:
        operands.append(far)
        specs.append(spec((count, tile), lambda j: (0, j)))
    ranges = []
    for j, terms in enumerate(plan):
        if ranges and ranges[-1][2] == terms:
            ranges[-1][1] = j + 1
        else:
            ranges.append([j, j + 1, terms])

    def kernel(*refs):
        result = refs[-1]
        for low, high, terms in ranges:

            @pl.when((pl.program_id(0) >= low) & (pl.program_id(0) < high))
            def _(terms=terms):
                total = None
                for at, unit, cut, place in terms:
                    units = cut.stop - cut.start
                    term = dot_nt(refs[at][:, unit : unit + units], refs[place][:, cut])
                    total = term if total is None else total + term
                if far is not None:
                    total = total + refs[-2][...].astype(f32)
                result[...] = total.astype(result.dtype)

    return pl.pallas_call(
        kernel,
        grid=(width // tile,),
        in_specs=specs,
        out_specs=spec((count, tile), lambda j: (0, j)),
        out_shape=shape(count, width, bf16),
        compiler_params=pltpu.CompilerParams(vmem_limit_bytes=VMEM),
        cost_estimate=cost(work, 2 * sum(operand.size for operand in operands)),
        name=name,
    )(*operands)


def grad_terms(near, far, refs, columns, pair):
    count = near.shape[0]
    if pair:
        first, second = refs[0][:, columns], refs[1][:, columns]
    else:
        first, second = refs[0][:count, columns], refs[0][count:, columns]
    return (dot_tn(near[...], first) + dot_tn(far[...], second)).astype(bf16)


def weight_part(rows, grads, half, s, name, columns=None, parts=1):
    near, far = rows
    pair = isinstance(grads, tuple)
    units = grads[0].shape[1] if pair else grads.shape[1]
    columns = slice(0, units) if columns is None else columns
    wide = columns.stop - columns.start
    tile = min(512, half) if parts == 1 else half // 4
    tiles = half // tile
    edges = [0, tiles] if parts == 1 else [0, 1, tiles]
    count = near.shape[0]
    row_spec = spec((count, tile), lambda j: (0, s * tiles + j))
    operands = grads if pair else (grads,)

    def kernel(near_rows, far_rows, *refs):
        total = grad_terms(near_rows, far_rows, refs, columns, pair)
        for part in range(parts):

            @pl.when((pl.program_id(0) >= edges[part]) & (pl.program_id(0) < edges[part + 1]))
            def _(part=part):
                refs[len(operands) + part][...] = total

    found = pl.pallas_call(
        kernel,
        grid=(tiles,),
        in_specs=[row_spec, row_spec] + [whole(operand.shape) for operand in operands],
        out_specs=[
            spec(
                (tile, wide),
                lambda j, part=part: (
                    jnp.clip(j, edges[part], edges[part + 1] - 1) - edges[part],
                    0,
                ),
            )
            for part in range(parts)
        ],
        out_shape=[
            in_hbm((edges[part + 1] - edges[part]) * tile, wide, bf16) for part in range(parts)
        ],
        compiler_params=pltpu.CompilerParams(vmem_limit_bytes=VMEM),
        cost_estimate=cost(4 * count * half * wide, 4 * count * (half + wide)),
        name=name,
    )(near, far, *operands)
    return found if parts > 1 else found[0]


def weight_slots(rows, grads, half, name, columns):
    near, far = rows
    wide = columns.stop - columns.start
    tile = min(512, half)
    tiles = half // tile
    inner = near.shape[1] // half
    count = near.shape[0]
    row_spec = spec((count, tile), lambda j: (0, j))

    def kernel(near_rows, far_rows, *refs):
        refs[-1][...] = grad_terms(near_rows, far_rows, refs, columns, False)

    return pl.pallas_call(
        kernel,
        grid=(inner * tiles,),
        in_specs=[row_spec, row_spec, whole(grads.shape)],
        out_specs=spec((tile, wide), lambda j: (j % tiles, j // tiles)),
        out_shape=in_hbm(half, inner * wide, bf16),
        compiler_params=pltpu.CompilerParams(vmem_limit_bytes=VMEM),
        cost_estimate=cost(4 * count * half * inner * wide, 4 * count * (half + wide)),
        name=name,
    )(near, far, grads)


def make_body(outer, inner, rows_axis, cores_axis):
    def body(
        hidden_in,
        skip_mask,
        parents,
        attention_gain,
        query_weight,
        key_weight,
        value_weight,
        output_weight,
        feedforward_gain,
        gate_weight,
        up_weight,
        down_weight,
        grad_out,
    ):
        part = hidden_in.shape[0]
        shard = query_weight.shape[0]
        pieces = rows_axis * cores_axis
        length = part * pieces
        near = part * rows_axis
        blocks = parents.shape[1]
        heads = query_weight.shape[1] // HD
        half = outer * shard
        width = half * inner
        tile = part // 2
        at_inner = lax.axis_index("inner")
        at_row = lax.axis_index("row")
        at_core = lax.axis_index("core")
        slots = range(inner)
        fence = lax.optimization_barrier

        order = jnp.stack(
            [z * inner + (at_inner + s) % inner for s in slots for z in range(outer)]
        ).astype(jnp.int32)

        def from_inner(values, k):
            return lax.ppermute(values, "inner", [((i + k) % inner, i) for i in range(inner)])

        def swap(values, axis):
            return lax.ppermute(values, axis, [(0, 1), (1, 0)])

        def spread(values):
            return [values] + [from_inner(values, s) for s in range(1, inner)]

        def gather(values):
            return lax.all_gather(values, "outer", axis=0, tiled=True)

        def scatter(values):
            return lax.psum_scatter(values, "outer", scatter_dimension=0, tiled=True)

        def collect(parts):
            total = parts[0].astype(f32)
            for s in range(1, inner):
                total = total + from_inner(parts[s], inner - s).astype(f32)
            return total

        keep_own = (1 - skip_mask).astype(f32)
        units = up_weight.shape[1]
        late = units if inner > 1 else 0
        joint_width = (heads + 2) * HD
        packed = pl.pallas_call(
            pack_kernel,
            out_shape=shaped(shard, joint_width + heads * HD + HD, bf16),
            compiler_params=pltpu.CompilerParams(vmem_limit_bytes=VMEM),
            cost_estimate=cost(0, shard * joint_width * 4),
            name="pack",
        )(
            jnp.stack([attention_gain.astype(f32), feedforward_gain.astype(f32)]),
            query_weight,
            key_weight,
            value_weight,
            output_weight,
        )
        keep_got = swap(keep_own, "row")
        row_x = swap(hidden_in, "row")
        row_g = swap(grad_out, "row")
        up_late = jnp.concatenate(spread(up_weight[:, units - late :]), axis=1) if late else None
        row_x, keep_got, up_late = fence((row_x, keep_got, up_late))
        near_x = jnp.concatenate([hidden_in, row_x], axis=0)
        far_x = swap(near_x, "core")
        packed_own = gather(packed)
        packed_own, far_x = fence((packed_own, far_x))
        packed_slots = spread(packed_own)
        keep = jnp.concatenate([keep_own, keep_got], axis=0)[:, None]
        near_g = jnp.concatenate([grad_out, row_g], axis=0)
        (near_branch,) = row_call(
            kept_kernel, "kept", near, tile, order, [(near_g, 0), (keep, 0)], [(width, bf16)]
        )
        far_branch = swap(near_branch, "core")
        down_own = gather(down_weight)
        gate_own = gather(gate_weight)
        early = units - late
        up_own = gather(up_weight[:, :early]) if early else None
        up_both = [gather(up_late)] if late else []

        cosine, sine = rotation_tables(blocks, length // blocks)
        starts = [
            (((at_row + dy) % 2) * cores_axis + (at_core + dc) % 2) * part
            for dc in range(2)
            for dy in range(2)
        ]
        table = jnp.concatenate([parents[0], jnp.stack(starts).astype(jnp.int32)])
        packed_slots, near_branch, far_branch, down_own = fence(
            (packed_slots, near_branch, far_branch, down_own)
        )
        quarter = half // 4
        down_got = [from_inner(down_own[:quarter], 1)] if inner > 1 else []
        gain_at = joint_width + heads * HD
        joint_columns = slice(0, joint_width)
        output_columns = slice(joint_width, gain_at)
        gain_one, gain_two = pl.pallas_call(
            gains_kernel,
            grid=(1,),
            in_specs=[spec((half, HD), lambda i: (0, gain_at // HD))] * inner,
            out_specs=[whole((1, width))] * 2,
            out_shape=[shaped(1, width, f32)] * 2,
            compiler_params=pltpu.CompilerParams(vmem_limit_bytes=VMEM),
            cost_estimate=cost(0, width * 8),
            name="gains",
        )(*packed_slots)
        all_branch = (near_branch, far_branch)

        def norm(rows, name):
            (result,) = row_call(
                norm_kernel, name, near, tile, order, [(rows, 0), (gain_one, None)], [(width, bf16)]
            )
            return result

        normed = (norm(near_x, "norm_near"), norm(far_x, "norm_far"))

        def all_of(arrays):
            return [(arrays, 0, [slice(0, array.shape[1]) for array in arrays])]

        attend, attend_back = attention_calls(length, blocks, heads)
        raw = through(normed, packed_slots, "joint", joint_columns, f32)
        if inner > 1:
            raw, down_got, down_own = fence((raw, down_got, down_own))
            down_got = down_got + [from_inner(down_own[quarter : 2 * quarter], 1)]
        mixed_near, mixed_far, rotated = attend(table, raw, cosine, sine)
        if inner > 1:
            mixed_near, mixed_far, down_got, down_own = fence(
                (mixed_near, mixed_far, down_got, down_own)
            )
            down_got = down_got + [from_inner(down_own[2 * quarter : 3 * quarter], 1)]
        mixed = (mixed_near, mixed_far)

        def packed_plan(columns):
            return [(packed_slots, 0, [columns] * inner)]

        attended_plan = [packed_plan(output_columns)]
        attended_far = swap(back_rows([mixed], attended_plan, 1, "attended_far"), "core")
        attended = back_rows([mixed], attended_plan, 0, "attended_near")
        attended = (attended.astype(f32) + attended_far.astype(f32)).astype(bf16)
        attended, gate_own, down_got = fence((attended, gate_own, down_got))
        if inner > 1:
            down_got = down_got + [from_inner(down_own[3 * quarter :], 1)]
        weight_down = [down_own] + down_got
        got = swap(attended, "row")
        weight_gate = spread(gate_own)
        hidden_grad = through(all_branch, weight_down, "hidden_grad", slice(0, units), bf16)
        got, hidden_grad, up_own = fence((got, hidden_grad, up_own))
        weight_up = spread(up_own) if early else []
        swapped = part // tile
        middle, normed_ff = row_call(
            middle_kernel,
            "middle",
            near,
            tile,
            order,
            [(near_x, 0), (keep, 0), (attended, 0), (got, swapped), (gain_two, None)],
            [(width, f32), (width, bf16)],
        )
        all_ff = (normed_ff, swap(normed_ff, "core"))

        up_parts = [(weight_up, 0, slice(0, early))] if early else []
        up_plan = [(weight_up, 0, [slice(0, early)] * inner)] if early else []
        if late:
            up_parts.append((up_both, early, slice(0, late)))
            up_plan.append((up_both * inner, early, [slice(s * late, (s + 1) * late) for s in slots]))
        gate, up_grad = gate_product(all_ff, hidden_grad, weight_gate)
        def weight_parts(rows, grads, name, columns=None):
            return [weight_part(rows, grads, half, s, name, columns) for s in slots]

        def core_sum(grads, weights, name):
            far = swap(back_rows(grads, weights, 1, name + "_far"), "core")
            return back_rows(grads, weights, 0, name + "_near", far)

        last = inner - 1
        up_late_sums = None
        if late:
            up_late_parts = weight_slots(all_ff, up_grad, half, "grad_up_late", slice(early, units))
            gate, up_grad, up_late_parts = fence((gate, up_grad, up_late_parts))
            up_late_sums = scatter(up_late_parts)
        hidden_ff, gate_grad = up_product(all_ff, hidden_grad, gate, up_parts)
        down_last = weight_part(all_branch, hidden_ff, half, last, "grad_down")
        gate_grad, up_grad, down_last = fence((gate_grad, up_grad, down_last))
        back_plan = ([gate_grad, up_grad], [all_of(weight_gate), up_plan])
        ff_far = back_rows(*back_plan, 1, "normed_ff_grad_far")
        ff_far, gate_grad, up_grad = fence((ff_far, gate_grad, up_grad))
        ff_far = swap(ff_far, "core")
        first = units // HD * 4 // 11 * HD if last else 0
        gate_columns = slice(first, units)
        gate_last = weight_part(all_ff, gate_grad, half, last, "grad_gate", gate_columns)
        gate_grad, up_grad, gate_last = fence((gate_grad, up_grad, gate_last))
        back_plan = ([gate_grad, up_grad], [all_of(weight_gate), up_plan])
        ff_grad = back_rows(*back_plan, 0, "normed_ff_grad_near", ff_far, in_hbm)
        ff_grad, gate_grad, up_grad, hidden_ff = fence((ff_grad, gate_grad, up_grad, hidden_ff))
        ff_got = swap(ff_grad, "row")
        gate_first_sums = None
        if first:
            gate_first = weight_slots(all_ff, gate_grad, half, "grad_gate_first", slice(0, first))
            gate_grad, hidden_ff, gate_first = fence((gate_grad, hidden_ff, gate_first))
            gate_first_sums = scatter(gate_first)

        def to_last(values):
            return from_inner(values, inner - last) if last else None

        def plus(values, got):
            if got is None:
                return values
            return (values.astype(f32) + got.astype(f32)).astype(bf16)

        down_got = to_last(down_last)
        gate_got = to_last(gate_last)
        up_last = up_got = None
        if early:
            up_last = weight_part(all_ff, up_grad, half, last, "grad_up", slice(0, early))
            up_got = to_last(up_last)
        own = [down_last, gate_last, up_last]
        if last:
            own = [
                weight_part(all_branch, hidden_ff, half, 0, "grad_down"),
                weight_part(all_ff, gate_grad, half, 0, "grad_gate", gate_columns),
                weight_part(all_ff, up_grad, half, 0, "grad_up", slice(0, early))
                if early
                else None,
            ]
        branch_plan = ([hidden_ff], [all_of(weight_down)])
        branch_far = back_rows(*branch_plan, 1, "branch_far")
        branch_near = back_rows(*branch_plan, 0, "branch_near")
        down_own, down_got, own[1], branch_far, branch_near = fence(
            (own[0], down_got, own[1], branch_far, branch_near)
        )
        down_sum = plus(down_own, down_got)
        ff_got, own, up_last, gate_last = fence((ff_got, own, up_last, gate_last))
        grad_down = scatter(down_sum)
        middle_grad, attended_grad = row_call(
            middle_back_kernel,
            "middle_back",
            near,
            tile,
            order,
            [
                (near_g, 0),
                (keep, 0),
                (ff_grad, 0),
                (ff_got, swapped),
                (gain_two, None),
                (middle, 0),
            ],
            [(width, f32), (width, bf16)],
        )
        all_attended = (attended_grad, swap(attended_grad, "core"))

        mixed_grad = through(all_attended, packed_slots, "mixed_grad", output_columns, bf16)
        output_last = weight_part(all_attended, mixed, half, last, "grad_output")
        mixed_grad, output_last = fence((mixed_grad, output_last))
        packed_grad = tuple(attend_back(table, rotated, mixed_grad, cosine, sine))
        joint_last = weight_part(normed, packed_grad, half, last, "grad_joint")
        normed_plan = ([packed_grad], [packed_plan(joint_columns)])
        normed_far = back_rows(*normed_plan, 1, "normed_grad_far")
        normed_near = back_rows(*normed_plan, 0, "normed_grad_near")
        packed_grad, gate_got, up_late_sums, joint_last, normed_far, normed_near = fence(
            (packed_grad, gate_got, up_late_sums, joint_last, normed_far, normed_near)
        )
        grad_gate = scatter(plus(own[1], gate_got))
        normed_grad = (normed_near.astype(f32) + swap(normed_far, "core").astype(f32)).astype(bf16)
        normed_got = swap(normed_grad[part:], "row")
        branch = (branch_near.astype(f32) + swap(branch_far, "core").astype(f32)).astype(bf16)
        output_sum, joint_sum = output_last, joint_last
        if last:
            output_own = weight_part(all_attended, mixed, half, 0, "grad_output")
            joint_own = weight_part(normed, packed_grad, half, 0, "grad_joint")
            output_got, joint_got = to_last(output_last), to_last(joint_last)
            output_got, joint_got, normed_got, branch = fence(
                (output_got, joint_got, normed_got, branch)
            )
            output_sum = plus(output_own, output_got)
            joint_sum = plus(joint_own, joint_got)
        branch_got = swap(branch[part:], "row")
        (layer_out,) = row_call(
            layer_kernel,
            "layer",
            part,
            tile,
            order,
            [(middle, 0), (keep, 0), (branch, 0), (branch_got, 0)],
            [(width, bf16)],
        )
        attention_sum = jnp.concatenate([output_sum, joint_sum], axis=1)
        grad_up = None
        if early:
            up_got, grad_down = fence((up_got, grad_down))
            grad_up = scatter(plus(own[2], up_got)).astype(f32)
        attention_sum, grad_down, gate_first_sums = fence(
            (attention_sum, grad_down, gate_first_sums)
        )
        attention_terms = attention_sum
        attention_sum = scatter(attention_sum)
        (input_grad,) = pl.pallas_call(
            input_kernel,
            grid=(part // tile,),
            in_specs=[
                pl.BlockSpec(memory_space=pltpu.SMEM),
                spec((tile, width), lambda i: (i, 0)),
                spec((tile, width), lambda i: (i, 0)),
                spec((tile, width), lambda i: (i, 0)),
                whole((1, width)),
                spec((tile, width), lambda i: (i, 0)),
            ],
            out_specs=[spec((tile, width), lambda i: (i, 0))],
            out_shape=[shaped(part, width, f32)],
            scratch_shapes=[pltpu.VMEM((tile, width), f32)],
            compiler_params=pltpu.CompilerParams(vmem_limit_bytes=VMEM),
            cost_estimate=cost(part * width * 10, part * width * 16),
            name="input_grad",
        )(order, hidden_in, normed_grad, normed_got, gain_one, middle_grad)
        if late:
            sums = [(up_late_sums, late)] + ([(gate_first_sums, first)] if first else [])
            grad_late = collect(
                [
                    jnp.concatenate([rows[:, s * wide : (s + 1) * wide] for rows, wide in sums], axis=1)
                    for s in slots
                ]
            )
            if first:
                grad_gate = jnp.concatenate([grad_late[:, late:], grad_gate.astype(f32)], axis=1)
                grad_late = grad_late[:, :late]
            grad_up = grad_late if grad_up is None else jnp.concatenate([grad_up, grad_late], axis=1)
        grad_down, grad_gate, grad_up = [
            grad.astype(f32) for grad in (grad_down, grad_gate, grad_up)
        ]

        def over_tensor(values):
            values = values + swap(values, "core")
            return values + swap(values, "row")

        own_weights = packed_slots[0][:, :joint_width].astype(f32)
        terms = jnp.sum(own_weights * attention_terms[:, heads * HD :].astype(f32), axis=1)
        terms = over_tensor(terms[None, :])
        step = 1
        while step < outer:
            pairs = [(z ^ step, z) for z in range(outer)]
            terms = terms + lax.ppermute(terms, "outer", pairs)
            step *= 2
        at = lax.axis_index("outer") * shard
        attention_gain_grad = lax.dynamic_slice_in_dim(terms[0], at, shard, 0)
        attention_gain_grad = attention_gain_grad / attention_gain.astype(f32)
        terms = jnp.sum(gate_weight.astype(f32) * grad_gate, axis=1)
        terms = terms + jnp.sum(up_weight.astype(f32) * grad_up, axis=1)
        feedforward_gain_grad = over_tensor(terms[None, :])[0] / feedforward_gain.astype(f32)

        attention_sum, input_grad, layer_out, attention_gain_grad, feedforward_gain_grad = fence(
            (attention_sum, input_grad, layer_out, attention_gain_grad, feedforward_gain_grad)
        )
        attention_sum = attention_sum.astype(f32)
        grad_output = attention_sum[:, : heads * HD]
        grad_joint = attention_sum[:, heads * HD :]
        query_width = heads * HD
        grad_query = grad_joint[:, :query_width]
        grad_key = grad_joint[:, query_width : query_width + HD]
        grad_value = grad_joint[:, query_width + HD :]
        return (
            layer_out,
            input_grad,
            attention_gain_grad,
            grad_query,
            grad_key,
            grad_value,
            grad_output,
            feedforward_gain_grad,
            grad_gate,
            grad_up,
            grad_down,
        )

    return body


def solution(mesh):
    replicas = mesh.shape["dp"]
    inner = 2 if replicas % 2 == 0 else 1
    outer = replicas // inner
    cores = mesh.shape["tensor"] // 2
    grid = Mesh(mesh.devices.reshape(outer, inner, 2, cores), ("outer", "inner", "row", "core"))
    dp, tensor = ("outer", "inner"), ("row", "core")
    both = dp + tensor
    weight = P(dp, tensor)
    return jax.shard_map(
        make_body(outer, inner, 2, cores),
        mesh=grid,
        in_specs=(
            P(both, None),
            P(both),
            P(dp, None),
            P(dp),
            weight,
            weight,
            weight,
            weight,
            P(dp),
            weight,
            weight,
            weight,
            P(both, None),
        ),
        out_specs=(
            P(both, None),
            P(both, None),
            P(dp),
            weight,
            weight,
            weight,
            weight,
            P(dp),
            weight,
            weight,
            weight,
        ),
        check_vma=False,
    )
```

```python
import math

import jax
import jax.numpy as jnp
from jax import lax
from jax.experimental import pallas as pl
from jax.experimental.pallas import tpu as pltpu
from jax.sharding import Mesh
from jax.sharding import PartitionSpec as P

HD = 128
TRUNK = 4
BRANCH = 2
PIECES = 4
SHARE = 4
VMEM = 32 * 2**20

epsilon = 1e-05
masked_score = -1000000000.0
bf16 = jnp.bfloat16
f32 = jnp.float32


def dot_nn(a, b):
    return lax.dot_general(a, b, (((1,), (0,)), ((), ())), preferred_element_type=f32)


def dot_nt(a, b):
    return lax.dot_general(a, b, (((1,), (1,)), ((), ())), preferred_element_type=f32)


def dot_tn(a, b):
    return lax.dot_general(a, b, (((0,), (0,)), ((), ())), preferred_element_type=f32)


def place_pieces(table, groups, tree, blocks, into_tree):
    size = tree.shape[0] // PIECES
    piece = 0
    for group in groups:
        for at in range(0, group.shape[0], size):
            start = pl.multiple_of(table[blocks + piece], 64)
            here = slice(at, at + size)
            if into_tree:
                tree[pl.ds(start, size), :] = group[here, :].astype(tree.dtype)
            else:
                group[here, :] = tree[pl.ds(start, size), :].astype(group.dtype)
            piece += 1


def segments(table, rows, block, block_len, key_at, value_at):
    def part(start, size):
        return (
            rows[pl.ds(start, size), key_at : key_at + HD],
            rows[pl.ds(start, size), value_at : value_at + HD],
        )

    found = []
    trunk = min(block, TRUNK)
    if trunk:
        found.append((0, trunk * block_len) + part(0, trunk * block_len))
    if block >= TRUNK + BRANCH:
        start = pl.multiple_of(table[block] * block_len, block_len)
        found.append((start, block_len) + part(start, block_len))
    start = block * block_len
    found.append((start, block_len) + part(start, block_len))
    return found


def block_probs(stacked, found, block_len, scale):
    rows = stacked.shape[0]
    scores = [dot_nt(stacked, keys) * scale for _, _, keys, _ in found]
    row = lax.broadcasted_iota(jnp.int32, (rows, block_len), 0) % block_len
    column = lax.broadcasted_iota(jnp.int32, (rows, block_len), 1)
    scores[-1] = jnp.where(column <= row, scores[-1], masked_score)
    top = jnp.max(scores[0], axis=-1, keepdims=True)
    for part in scores[1:]:
        top = jnp.maximum(top, jnp.max(part, axis=-1, keepdims=True))
    raw = [jnp.exp(part - top) for part in scores]
    total = jnp.sum(raw[0], axis=-1, keepdims=True)
    for part in raw[1:]:
        total = total + jnp.sum(part, axis=-1, keepdims=True)
    inverse = 1.0 / total
    return [part * inverse for part in raw]


def stack_heads(rows, block, block_len, heads):
    here = slice(block * block_len, (block + 1) * block_len)
    return jnp.concatenate([rows[here, h * HD : (h + 1) * HD] for h in range(heads)], axis=0)


def attend_kernel(
    blocks, heads, table, raw, cosine, sine, mixed_near, mixed_far, rotated, tree, result
):
    length = tree.shape[0]
    block_len = length // blocks
    key_at, value_at = heads * HD, (heads + 1) * HD
    place_pieces(table, [raw], tree, blocks, True)

    def turn(block, carry):
        here = pl.ds(pl.multiple_of(block * block_len, block_len), block_len)
        cos, sin = cosine[here, :], sine[here, :]
        for h in range(heads + 1):
            there = slice(h * HD, (h + 1) * HD)
            values = tree[here, there]
            turned = values * cos + pltpu.roll(values, HD // 2, 1) * sin
            rotated[here, there] = turned.astype(bf16)
        rotated[here, value_at : value_at + HD] = tree[here, value_at : value_at + HD].astype(bf16)
        return carry

    lax.fori_loop(0, blocks, turn, 0)
    for block in range(blocks):
        stacked = stack_heads(rotated, block, block_len, heads)
        found = segments(table, rotated, block, block_len, key_at, value_at)
        probs = block_probs(stacked, found, block_len, HD ** (-0.5))
        out = dot_nn(probs[0].astype(bf16), found[0][3])
        for part, (_, _, _, values) in zip(probs[1:], found[1:]):
            out = out + dot_nn(part.astype(bf16), values)
        out = out.astype(bf16)
        for h in range(heads):
            result[block * block_len : (block + 1) * block_len, h * HD : (h + 1) * HD] = out[
                h * block_len : (h + 1) * block_len, :
            ]
    place_pieces(table, [mixed_near, mixed_far], result, blocks, False)


def attend_back_kernel(
    blocks,
    heads,
    table,
    rotated,
    grads,
    cosine,
    sine,
    packed_near,
    packed_far,
    tree,
    keys,
    values,
    result,
):
    length = rotated.shape[0]
    block_len = length // blocks
    key_at, value_at = heads * HD, (heads + 1) * HD
    scale = HD ** (-0.5)
    place_pieces(table, [grads], tree, blocks, True)
    keys[...] = jnp.zeros_like(keys)
    values[...] = jnp.zeros_like(values)

    def turn_back(rows, here):
        return rows * cosine[here, :] + pltpu.roll(rows * sine[here, :], HD // 2, 1)

    for block in range(blocks):
        here = slice(block * block_len, (block + 1) * block_len)
        stacked = stack_heads(rotated, block, block_len, heads)
        cotangent = stack_heads(tree, block, block_len, heads)
        found = segments(table, rotated, block, block_len, key_at, value_at)
        probs = block_probs(stacked, found, block_len, scale)
        prob_grads = [dot_nt(cotangent, part) for _, _, _, part in found]
        delta = jnp.sum(probs[0] * prob_grads[0], axis=-1, keepdims=True)
        for part, grad in zip(probs[1:], prob_grads[1:]):
            delta = delta + jnp.sum(part * grad, axis=-1, keepdims=True)
        query_grad = None
        for (start, size, key_rows, _), part, grad in zip(found, probs, prob_grads):
            score_grad = (part * (grad - delta)).astype(bf16)
            term = dot_nn(score_grad, key_rows)
            query_grad = term if query_grad is None else query_grad + term
            there = pl.ds(start, size)
            keys[there, :] += dot_tn(score_grad, stacked) * scale
            values[there, :] += dot_tn(part.astype(bf16), cotangent)
        query_grad = query_grad * scale
        for h in range(heads):
            rows = query_grad[h * block_len : (h + 1) * block_len, :]
            result[here, h * HD : (h + 1) * HD] = turn_back(rows, here).astype(bf16)

    def finish(block, carry):
        here = pl.ds(pl.multiple_of(block * block_len, block_len), block_len)
        result[here, key_at : key_at + HD] = turn_back(keys[here, :], here).astype(bf16)
        result[here, value_at : value_at + HD] = values[here, :].astype(bf16)
        return carry

    lax.fori_loop(0, blocks, finish, 0)
    place_pieces(table, [packed_near, packed_far], result, blocks, False)


def attention_calls(length, blocks, heads):
    width = (heads + 2) * HD
    vmem = pl.BlockSpec(memory_space=pltpu.VMEM)
    smem = pl.BlockSpec(memory_space=pltpu.SMEM)
    params = pltpu.CompilerParams(vmem_limit_bytes=VMEM)
    pairs = (TRUNK * (TRUNK + 1) // 2 + (blocks - TRUNK) * (TRUNK + 1) + 4) * heads
    pairs = pairs * (length // blocks) ** 2

    def forward(*operands):
        return attend_kernel(blocks, heads, *operands)

    def backward(*operands):
        return attend_back_kernel(blocks, heads, *operands)

    ahead = pl.pallas_call(
        forward,
        in_specs=[smem] + [vmem] * 3,
        out_specs=[vmem] * 3,
        out_shape=[shaped(length // 2, heads * HD, bf16)] * 2 + [shaped(length, width, bf16)],
        scratch_shapes=[pltpu.VMEM((length, width), f32), pltpu.VMEM((length, heads * HD), bf16)],
        compiler_params=params,
        cost_estimate=cost(16 * pairs * HD, length * width * 8),
        name="attend",
    )
    back = pl.pallas_call(
        backward,
        in_specs=[smem] + [vmem] * 4,
        out_specs=[vmem] * 2,
        out_shape=[shaped(length // 2, width, bf16)] * 2,
        scratch_shapes=[
            pltpu.VMEM((length, heads * HD), bf16),
            pltpu.VMEM((length, HD), f32),
            pltpu.VMEM((length, HD), f32),
            pltpu.VMEM((length, width), bf16),
        ],
        compiler_params=params,
        cost_estimate=cost(24 * pairs * HD, length * width * 8),
        name="attend_back",
    )
    return ahead, back


def rotation_tables(blocks, block_len):
    depths = [min(block, TRUNK) + (block >= TRUNK + BRANCH) for block in range(blocks)]
    length = blocks * block_len
    places = jnp.arange(length, dtype=jnp.int32)
    row_depth = jnp.zeros((length,), jnp.int32)
    for block, depth in enumerate(depths):
        row_depth = jnp.where(places // block_len == block, depth, row_depth)
    position = (row_depth * block_len + places % block_len).astype(f32)
    half = HD // 2
    freqs = jnp.exp(jnp.arange(half, dtype=f32) * (-2.0 * math.log(10000.0) / HD))
    angles = position[:, None] * freqs[None, :]
    cosine, sine = jnp.cos(angles), jnp.sin(angles)
    return (
        jnp.concatenate([cosine, cosine], axis=1),
        jnp.concatenate([-sine, sine], axis=1),
    )


def spec(block, index):
    return pl.BlockSpec(block, index)


def whole(shape):
    return pl.BlockSpec(shape, lambda *_: (0,) * len(shape))


def cost(flops, moved):
    return pl.CostEstimate(flops=flops // SHARE, bytes_accessed=moved // SHARE, transcendentals=0)


def shaped(rows, columns, kind):
    return jax.ShapeDtypeStruct((rows, columns), kind)


def in_hbm(rows, columns, kind):
    return pltpu.HBM((rows, columns), kind)


def runs(order, width):
    run = width // order.shape[0]
    for j in range(order.shape[0]):
        yield slice(j * run, (j + 1) * run), pl.ds(pl.multiple_of(order[j] * run, HD), run)


def row_call(kernel, name, rows, tile, order, operands, results):
    def place(array, offset):
        if offset is None:
            return whole(array.shape)
        steps = array.shape[0] // tile
        return spec((tile, array.shape[1]), lambda i: ((i + offset) % steps, 0))

    return pl.pallas_call(
        kernel,
        grid=(rows // tile,),
        in_specs=[pl.BlockSpec(memory_space=pltpu.SMEM)] + [place(*pair) for pair in operands],
        out_specs=[spec((tile, columns), lambda i: (i, 0)) for columns, _ in results],
        out_shape=[shaped(rows, columns, kind) for columns, kind in results],
        compiler_params=pltpu.CompilerParams(vmem_limit_bytes=VMEM),
        cost_estimate=cost(rows * 2048 * 10, rows * 2048 * 8),
        name=name,
    )(order, *[array for array, _ in operands])


def row_mean(values):
    return jnp.mean(values, axis=-1, keepdims=True)


def norm_kernel(order, rows, gain, normed):
    values = rows[...].astype(f32)
    scale = lax.rsqrt(row_mean(values * values) + epsilon)
    for here, there in runs(order, rows.shape[1]):
        unit = rows[:, there].astype(f32) * scale
        normed[:, here] = (unit * gain[:, here]).astype(bf16)


def pack_kernel(*refs):
    gains, weights, result = refs[0], refs[1:-1], refs[-1]
    at = 0
    for weight in weights:
        result[:, at : at + weight.shape[1]] = weight[...]
        at += weight.shape[1]
    rows = jnp.concatenate([gains[...], jnp.zeros((HD - gains.shape[0], gains.shape[1]), f32)])
    result[:, at:] = rows.T.astype(bf16)


def gains_kernel(*refs):
    slots, first, second = refs[:-2], refs[-2], refs[-1]
    at = 0
    for slot in slots:
        columns = slot[...].astype(f32).T
        here = slice(at, at + slot.shape[0])
        first[:, here] = columns[0:1, :]
        second[:, here] = columns[1:2, :]
        at += slot.shape[0]


def kept_kernel(order, rows, keep, result):
    for here, there in runs(order, rows.shape[1]):
        result[:, here] = (rows[:, there].astype(f32) * keep[...]).astype(bf16)


def middle_kernel(order, rows, keep, mine, got, gain, middle, normed):
    for here, there in runs(order, rows.shape[1]):
        attended = mine[:, here].astype(f32) + got[:, here].astype(f32)
        middle[:, here] = rows[:, there].astype(f32) + keep[...] * attended
    values = middle[...]
    scale = lax.rsqrt(row_mean(values * values) + epsilon)
    normed[...] = (values * scale * gain[...]).astype(bf16)


def middle_back_kernel(order, cotangent, keep, mine, got, gain, middle, grad, kept):
    values = middle[...]
    scale = lax.rsqrt(row_mean(values * values) + epsilon)
    unit = values * scale
    scaled = (mine[...].astype(f32) + got[...].astype(f32)) * gain[...]
    mean = row_mean(scaled * unit)
    change = scale * (scaled - unit * mean)
    for here, there in runs(order, middle.shape[1]):
        total = cotangent[:, there].astype(f32) + change[:, here]
        grad[:, here] = total
        kept[:, here] = (keep[...] * total).astype(bf16)


def layer_kernel(order, middle, keep, mine, got, result):
    for here, there in runs(order, middle.shape[1]):
        branch = mine[:, here].astype(f32) + got[:, here].astype(f32)
        result[:, there] = (middle[:, here] + keep[...] * branch).astype(bf16)


def input_kernel(order, rows, mine, got, gain, middle_grad, result, scaled):
    values = rows[...].astype(f32)
    scale = lax.rsqrt(row_mean(values * values) + epsilon)
    scaled[...] = (mine[...].astype(f32) + got[...].astype(f32)) * gain[...]
    total = None
    for here, there in runs(order, rows.shape[1]):
        term = jnp.sum(scaled[:, here] * rows[:, there].astype(f32), axis=-1, keepdims=True)
        total = term if total is None else total + term
    mean = total * scale / rows.shape[1]
    for here, there in runs(order, rows.shape[1]):
        unit = rows[:, there].astype(f32) * scale
        result[:, there] = middle_grad[:, here] + scale * (scaled[:, here] - unit * mean)


def column_cuts(width):
    return [slice(at, min(at + 256, width)) for at in range(0, width, 256)]


def of_group(near, far, steps):
    tile = 2 * near.shape[0] // steps
    last = steps // 2 - 1
    return [
        spec((tile, near.shape[1]), lambda i: (jnp.minimum(i, last), 0)),
        spec((tile, far.shape[1]), lambda i: (jnp.maximum(i - last - 1, 0), 0)),
    ]


def resident(slots):
    return [
        pl.BlockSpec(slot.shape, lambda i: (0, 0), pipeline_mode=pl.Buffered(1)) for slot in slots
    ]


def in_halves(steps, work):
    for side in range(2):

        @pl.when(pl.program_id(0) // (steps // 2) == side)
        def _(side=side):
            work(side)


def product(rows, weights, cut):
    total, at = None, 0
    for weight in weights:
        term = dot_nn(rows[:, at : at + weight.shape[0]], weight[:, cut])
        total = term if total is None else total + term
        at += weight.shape[0]
    return total


def through(rows, weights, name, columns, kind):
    near, far = rows
    units = columns.stop - columns.start
    length, width = 2 * near.shape[0], near.shape[1]

    def kernel(*refs):
        slots, result = refs[2:-1], refs[-1]

        def work(side):
            for inside in column_cuts(units):
                cut = slice(columns.start + inside.start, columns.start + inside.stop)
                result[:, inside] = product(refs[side], slots, cut).astype(result.dtype)

        in_halves(2, work)

    return pl.pallas_call(
        kernel,
        grid=(2,),
        in_specs=of_group(near, far, 2) + resident(weights),
        out_specs=spec((length // 2, units), lambda i: (i, 0)),
        out_shape=shaped(length, units, kind),
        compiler_params=pltpu.CompilerParams(vmem_limit_bytes=VMEM),
        cost_estimate=cost(2 * length * width * units, 2 * width * (length + units)),
        name=name,
    )(near, far, *weights)


def gate_product(rows, hidden_grad, gates):
    near, far = rows
    length, units = hidden_grad.shape
    width = near.shape[1]

    def kernel(*refs):
        hidden_back, slots = refs[2], refs[3:-2]
        gate_out, up_grad = refs[-2:]

        def work(side):
            for cut in column_cuts(units):
                gate = product(refs[side], slots, cut)
                gate_out[:, cut] = gate
                active = gate / (1.0 + jnp.exp(-gate))
                up_grad[:, cut] = (hidden_back[:, cut].astype(f32) * active).astype(bf16)

        in_halves(4, work)

    here = spec((length // 4, units), lambda i: (i, 0))
    return pl.pallas_call(
        kernel,
        grid=(4,),
        in_specs=of_group(near, far, 4) + [here] + resident(gates),
        out_specs=[here] * 2,
        out_shape=[in_hbm(length, units, f32), shaped(length, units, bf16)],
        compiler_params=pltpu.CompilerParams(vmem_limit_bytes=VMEM),
        cost_estimate=cost(2 * length * width * units, 2 * width * (length + units)),
        name="gate",
    )(near, far, hidden_grad, *gates)


def up_product(rows, hidden_grad, gate, ups):
    near, far = rows
    length, units = hidden_grad.shape
    width = near.shape[1]
    up_slots = [slot for slots, _, _ in ups for slot in slots]

    def kernel(*refs):
        hidden_back, gate_in = refs[2], refs[3]
        up_refs = refs[4:-2]
        hidden, gate_grad = refs[-2:]

        def work(side):
            rows_in, at = refs[side], 0
            for slots, first, columns in ups:
                mine = up_refs[at : at + len(slots)]
                at += len(slots)
                for inside in column_cuts(columns.stop - columns.start):
                    cut = slice(first + inside.start, first + inside.stop)
                    there = slice(columns.start + inside.start, columns.start + inside.stop)
                    if len(slots) == 1 and mine[0].shape[0] < width:
                        depth = mine[0].shape[0]
                        count = width // depth
                        step = mine[0].shape[1] // count
                        upward = None
                        for s in range(count):
                            view = mine[0][:, there.start + s * step : there.stop + s * step]
                            term = dot_nn(rows_in[:, s * depth : (s + 1) * depth], view)
                            upward = term if upward is None else upward + term
                    else:
                        upward = product(rows_in, mine, there)
                    value = gate_in[:, cut]
                    sigma = 1.0 / (1.0 + jnp.exp(-value))
                    back = hidden_back[:, cut].astype(f32) * upward * sigma
                    hidden[:, cut] = (value * sigma * upward).astype(bf16)
                    gate_grad[:, cut] = (back * (1.0 + value * (1.0 - sigma))).astype(bf16)

        in_halves(4, work)

    here = spec((length // 4, units), lambda i: (i, 0))
    return pl.pallas_call(
        kernel,
        grid=(4,),
        in_specs=of_group(near, far, 4) + [here, here] + resident(up_slots),
        out_specs=[here] * 2,
        out_shape=[shaped(length, units, bf16)] * 2,
        compiler_params=pltpu.CompilerParams(vmem_limit_bytes=VMEM),
        cost_estimate=cost(2 * length * width * units, 2 * width * (length + units)),
        name="up",
    )(near, far, hidden_grad, gate, *up_slots)


def back_rows(grads, weights, side, name, far=None, shape=shaped):
    width = sum(array.shape[0] for array in weights[0][0][0])
    tile = min(512, min(array.shape[0] for parts in weights for w in parts for array in w[0]))
    first = grads[0]
    count = first[0].shape[0] if isinstance(first, tuple) else first.shape[0] // 2
    operands, specs, plan = [], [], [[] for _ in range(width // tile)]
    work = 0
    for grad, parts in zip(grads, weights):
        at = len(operands)
        if isinstance(grad, tuple):
            specs.append(spec(grad[side].shape, lambda j: (0, 0)))
            operands.append(grad[side])
        else:
            specs.append(spec((count, grad.shape[1]), lambda j: (side, 0)))
            operands.append(grad)
        for arrays, unit, columns in parts:
            start = 0
            for array, cut in zip(arrays, columns):
                tiles = array.shape[0] // tile
                for j in range(start, start + tiles):
                    plan[j].append((at, unit, cut, len(operands)))
                operands.append(array)
                specs.append(
                    spec(
                        (tile, array.shape[1]),
                        lambda j, start=start, tiles=tiles: (jnp.clip(j - start, 0, tiles - 1), 0),
                    )
                )
                start += tiles
                work += 2 * count * array.shape[0] * (cut.stop - cut.start)
    if far is not None:
        operands.append(far)
        specs.append(spec((count, tile), lambda j: (0, j)))
    ranges = []
    for j, terms in enumerate(plan):
        if ranges and ranges[-1][2] == terms:
            ranges[-1][1] = j + 1
        else:
            ranges.append([j, j + 1, terms])

    def kernel(*refs):
        result = refs[-1]
        for low, high, terms in ranges:

            @pl.when((pl.program_id(0) >= low) & (pl.program_id(0) < high))
            def _(terms=terms):
                total = None
                for at, unit, cut, place in terms:
                    units = cut.stop - cut.start
                    term = dot_nt(refs[at][:, unit : unit + units], refs[place][:, cut])
                    total = term if total is None else total + term
                if far is not None:
                    total = total + refs[-2][...].astype(f32)
                result[...] = total.astype(result.dtype)

    return pl.pallas_call(
        kernel,
        grid=(width // tile,),
        in_specs=specs,
        out_specs=spec((count, tile), lambda j: (0, j)),
        out_shape=shape(count, width, bf16),
        compiler_params=pltpu.CompilerParams(vmem_limit_bytes=VMEM),
        cost_estimate=cost(work, 2 * sum(operand.size for operand in operands)),
        name=name,
    )(*operands)


def grad_terms(near, far, refs, columns, pair):
    count = near.shape[0]
    if pair:
        first, second = refs[0][:, columns], refs[1][:, columns]
    else:
        first, second = refs[0][:count, columns], refs[0][count:, columns]
    return (dot_tn(near[...], first) + dot_tn(far[...], second)).astype(bf16)


def weight_part(rows, grads, half, s, name, columns=None, parts=1):
    near, far = rows
    pair = isinstance(grads, tuple)
    units = grads[0].shape[1] if pair else grads.shape[1]
    columns = slice(0, units) if columns is None else columns
    wide = columns.stop - columns.start
    tile = min(512, half) if parts == 1 else half // 4
    tiles = half // tile
    edges = [0, tiles] if parts == 1 else [0, 1, tiles]
    count = near.shape[0]
    row_spec = spec((count, tile), lambda j: (0, s * tiles + j))
    operands = grads if pair else (grads,)

    def kernel(near_rows, far_rows, *refs):
        total = grad_terms(near_rows, far_rows, refs, columns, pair)
        for part in range(parts):

            @pl.when((pl.program_id(0) >= edges[part]) & (pl.program_id(0) < edges[part + 1]))
            def _(part=part):
                refs[len(operands) + part][...] = total

    found = pl.pallas_call(
        kernel,
        grid=(tiles,),
        in_specs=[row_spec, row_spec] + [whole(operand.shape) for operand in operands],
        out_specs=[
            spec(
                (tile, wide),
                lambda j, part=part: (
                    jnp.clip(j, edges[part], edges[part + 1] - 1) - edges[part],
                    0,
                ),
            )
            for part in range(parts)
        ],
        out_shape=[
            in_hbm((edges[part + 1] - edges[part]) * tile, wide, bf16) for part in range(parts)
        ],
        compiler_params=pltpu.CompilerParams(vmem_limit_bytes=VMEM),
        cost_estimate=cost(4 * count * half * wide, 4 * count * (half + wide)),
        name=name,
    )(near, far, *operands)
    return found if parts > 1 else found[0]


def weight_slots(rows, grads, half, name, columns):
    near, far = rows
    wide = columns.stop - columns.start
    tile = min(512, half)
    tiles = half // tile
    inner = near.shape[1] // half
    count = near.shape[0]
    row_spec = spec((count, tile), lambda j: (0, j))

    def kernel(near_rows, far_rows, *refs):
        refs[-1][...] = grad_terms(near_rows, far_rows, refs, columns, False)

    return pl.pallas_call(
        kernel,
        grid=(inner * tiles,),
        in_specs=[row_spec, row_spec, whole(grads.shape)],
        out_specs=spec((tile, wide), lambda j: (j % tiles, j // tiles)),
        out_shape=in_hbm(half, inner * wide, bf16),
        compiler_params=pltpu.CompilerParams(vmem_limit_bytes=VMEM),
        cost_estimate=cost(4 * count * half * inner * wide, 4 * count * (half + wide)),
        name=name,
    )(near, far, grads)


def make_body(outer, inner, rows_axis, cores_axis):
    def body(
        hidden_in,
        skip_mask,
        parents,
        attention_gain,
        query_weight,
        key_weight,
        value_weight,
        output_weight,
        feedforward_gain,
        gate_weight,
        up_weight,
        down_weight,
        grad_out,
    ):
        part = hidden_in.shape[0]
        shard = query_weight.shape[0]
        pieces = rows_axis * cores_axis
        length = part * pieces
        near = part * rows_axis
        blocks = parents.shape[1]
        heads = query_weight.shape[1] // HD
        half = outer * shard
        width = half * inner
        tile = part // 2
        at_inner = lax.axis_index("inner")
        at_row = lax.axis_index("row")
        at_core = lax.axis_index("core")
        slots = range(inner)
        fence = lax.optimization_barrier

        order = jnp.stack(
            [z * inner + (at_inner + s) % inner for s in slots for z in range(outer)]
        ).astype(jnp.int32)

        def from_inner(values, k):
            return lax.ppermute(values, "inner", [((i + k) % inner, i) for i in range(inner)])

        def swap(values, axis):
            return lax.ppermute(values, axis, [(0, 1), (1, 0)])

        def spread(values):
            return [values] + [from_inner(values, s) for s in range(1, inner)]

        def gather(values):
            return lax.all_gather(values, "outer", axis=0, tiled=True)

        def scatter(values):
            return lax.psum_scatter(values, "outer", scatter_dimension=0, tiled=True)

        def collect(parts):
            total = parts[0].astype(f32)
            for s in range(1, inner):
                total = total + from_inner(parts[s], inner - s).astype(f32)
            return total

        keep_own = (1 - skip_mask).astype(f32)
        units = up_weight.shape[1]
        late = units if inner > 1 else 0
        joint_width = (heads + 2) * HD
        packed = pl.pallas_call(
            pack_kernel,
            out_shape=shaped(shard, joint_width + heads * HD + HD, bf16),
            compiler_params=pltpu.CompilerParams(vmem_limit_bytes=VMEM),
            cost_estimate=cost(0, shard * joint_width * 4),
            name="pack",
        )(
            jnp.stack([attention_gain.astype(f32), feedforward_gain.astype(f32)]),
            query_weight,
            key_weight,
            value_weight,
            output_weight,
        )
        keep_got = swap(keep_own, "row")
        row_x = swap(hidden_in, "row")
        row_g = swap(grad_out, "row")
        up_late = jnp.concatenate(spread(up_weight[:, units - late :]), axis=1) if late else None
        row_x, keep_got, up_late = fence((row_x, keep_got, up_late))
        near_x = jnp.concatenate([hidden_in, row_x], axis=0)
        far_x = swap(near_x, "core")
        packed_own = gather(packed)
        packed_own, far_x = fence((packed_own, far_x))
        packed_slots = spread(packed_own)
        keep = jnp.concatenate([keep_own, keep_got], axis=0)[:, None]
        near_g = jnp.concatenate([grad_out, row_g], axis=0)
        (near_branch,) = row_call(
            kept_kernel, "kept", near, tile, order, [(near_g, 0), (keep, 0)], [(width, bf16)]
        )
        far_branch = swap(near_branch, "core")
        down_own = gather(down_weight)
        gate_own = gather(gate_weight)
        early = units - late
        up_own = gather(up_weight[:, :early]) if early else None
        up_both = [gather(up_late)] if late else []

        cosine, sine = rotation_tables(blocks, length // blocks)
        starts = [
            (((at_row + dy) % 2) * cores_axis + (at_core + dc) % 2) * part
            for dc in range(2)
            for dy in range(2)
        ]
        table = jnp.concatenate([parents[0], jnp.stack(starts).astype(jnp.int32)])
        packed_slots, near_branch, far_branch, down_own = fence(
            (packed_slots, near_branch, far_branch, down_own)
        )
        quarter = half // 4
        down_got = [from_inner(down_own[:quarter], 1)] if inner > 1 else []
        gain_at = joint_width + heads * HD
        joint_columns = slice(0, joint_width)
        output_columns = slice(joint_width, gain_at)
        gain_one, gain_two = pl.pallas_call(
            gains_kernel,
            grid=(1,),
            in_specs=[spec((half, HD), lambda i: (0, gain_at // HD))] * inner,
            out_specs=[whole((1, width))] * 2,
            out_shape=[shaped(1, width, f32)] * 2,
            compiler_params=pltpu.CompilerParams(vmem_limit_bytes=VMEM),
            cost_estimate=cost(0, width * 8),
            name="gains",
        )(*packed_slots)
        all_branch = (near_branch, far_branch)

        def norm(rows, name):
            (result,) = row_call(
                norm_kernel, name, near, tile, order, [(rows, 0), (gain_one, None)], [(width, bf16)]
            )
            return result

        normed = (norm(near_x, "norm_near"), norm(far_x, "norm_far"))

        def all_of(arrays):
            return [(arrays, 0, [slice(0, array.shape[1]) for array in arrays])]

        attend, attend_back = attention_calls(length, blocks, heads)
        raw = through(normed, packed_slots, "joint", joint_columns, f32)
        if inner > 1:
            raw, down_got, down_own = fence((raw, down_got, down_own))
            down_got = down_got + [from_inner(down_own[quarter : 2 * quarter], 1)]
        mixed_near, mixed_far, rotated = attend(table, raw, cosine, sine)
        if inner > 1:
            mixed_near, mixed_far, down_got, down_own = fence(
                (mixed_near, mixed_far, down_got, down_own)
            )
            down_got = down_got + [from_inner(down_own[2 * quarter : 3 * quarter], 1)]
        mixed = (mixed_near, mixed_far)

        def packed_plan(columns):
            return [(packed_slots, 0, [columns] * inner)]

        attended_plan = [packed_plan(output_columns)]
        attended_far = swap(back_rows([mixed], attended_plan, 1, "attended_far"), "core")
        attended = back_rows([mixed], attended_plan, 0, "attended_near")
        attended = (attended.astype(f32) + attended_far.astype(f32)).astype(bf16)
        attended, gate_own, down_got = fence((attended, gate_own, down_got))
        if inner > 1:
            down_got = down_got + [from_inner(down_own[3 * quarter :], 1)]
        weight_down = [down_own] + down_got
        got = swap(attended, "row")
        weight_gate = spread(gate_own)
        hidden_grad = through(all_branch, weight_down, "hidden_grad", slice(0, units), bf16)
        got, hidden_grad, up_own = fence((got, hidden_grad, up_own))
        weight_up = spread(up_own) if early else []
        swapped = part // tile
        middle, normed_ff = row_call(
            middle_kernel,
            "middle",
            near,
            tile,
            order,
            [(near_x, 0), (keep, 0), (attended, 0), (got, swapped), (gain_two, None)],
            [(width, f32), (width, bf16)],
        )
        all_ff = (normed_ff, swap(normed_ff, "core"))

        up_parts = [(weight_up, 0, slice(0, early))] if early else []
        up_plan = [(weight_up, 0, [slice(0, early)] * inner)] if early else []
        if late:
            up_parts.append((up_both, early, slice(0, late)))
            up_plan.append((up_both * inner, early, [slice(s * late, (s + 1) * late) for s in slots]))
        gate, up_grad = gate_product(all_ff, hidden_grad, weight_gate)
        def weight_parts(rows, grads, name, columns=None):
            return [weight_part(rows, grads, half, s, name, columns) for s in slots]

        def core_sum(grads, weights, name):
            far = swap(back_rows(grads, weights, 1, name + "_far"), "core")
            return back_rows(grads, weights, 0, name + "_near", far)

        last = inner - 1
        up_late_sums = None
        if late:
            up_late_parts = weight_slots(all_ff, up_grad, half, "grad_up_late", slice(early, units))
            gate, up_grad, up_late_parts = fence((gate, up_grad, up_late_parts))
            up_late_sums = scatter(up_late_parts)
        hidden_ff, gate_grad = up_product(all_ff, hidden_grad, gate, up_parts)
        down_last = weight_part(all_branch, hidden_ff, half, last, "grad_down")
        gate_grad, up_grad, down_last = fence((gate_grad, up_grad, down_last))
        first = units // HD * 4 // 11 * HD if last else 0
        gate_first_sums = None
        if first:
            gate_first = weight_slots(all_ff, gate_grad, half, "grad_gate_first", slice(0, first))
            gate_grad, up_grad, gate_first = fence((gate_grad, up_grad, gate_first))
            gate_first_sums = scatter(gate_first)
        back_plan = ([gate_grad, up_grad], [all_of(weight_gate), up_plan])
        ff_far = back_rows(*back_plan, 1, "normed_ff_grad_far")
        ff_far, gate_grad, up_grad = fence((ff_far, gate_grad, up_grad))
        ff_far = swap(ff_far, "core")
        gate_columns = slice(first, units)
        gate_last = weight_part(all_ff, gate_grad, half, last, "grad_gate", gate_columns)
        gate_grad, up_grad, gate_last = fence((gate_grad, up_grad, gate_last))
        back_plan = ([gate_grad, up_grad], [all_of(weight_gate), up_plan])
        ff_grad = back_rows(*back_plan, 0, "normed_ff_grad_near", ff_far, in_hbm)
        ff_grad, gate_grad, up_grad, hidden_ff = fence((ff_grad, gate_grad, up_grad, hidden_ff))
        ff_got = swap(ff_grad, "row")

        def to_last(values):
            return from_inner(values, inner - last) if last else None

        def plus(values, got):
            if got is None:
                return values
            return (values.astype(f32) + got.astype(f32)).astype(bf16)

        down_got = to_last(down_last)
        gate_got = to_last(gate_last)
        up_last = up_got = None
        if early:
            up_last = weight_part(all_ff, up_grad, half, last, "grad_up", slice(0, early))
            up_got = to_last(up_last)
        own = [down_last, gate_last, up_last]
        if last:
            own = [
                weight_part(all_branch, hidden_ff, half, 0, "grad_down"),
                weight_part(all_ff, gate_grad, half, 0, "grad_gate", gate_columns),
                weight_part(all_ff, up_grad, half, 0, "grad_up", slice(0, early))
                if early
                else None,
            ]
        branch_plan = ([hidden_ff], [all_of(weight_down)])
        branch_far = back_rows(*branch_plan, 1, "branch_far")
        branch_near = back_rows(*branch_plan, 0, "branch_near")
        down_own, down_got, own[1], branch_far, branch_near = fence(
            (own[0], down_got, own[1], branch_far, branch_near)
        )
        down_sum = plus(down_own, down_got)
        ff_got, own, up_last, gate_last = fence((ff_got, own, up_last, gate_last))
        grad_down = scatter(down_sum)
        middle_grad, attended_grad = row_call(
            middle_back_kernel,
            "middle_back",
            near,
            tile,
            order,
            [
                (near_g, 0),
                (keep, 0),
                (ff_grad, 0),
                (ff_got, swapped),
                (gain_two, None),
                (middle, 0),
            ],
            [(width, f32), (width, bf16)],
        )
        all_attended = (attended_grad, swap(attended_grad, "core"))

        mixed_grad = through(all_attended, packed_slots, "mixed_grad", output_columns, bf16)
        output_last = weight_part(all_attended, mixed, half, last, "grad_output")
        mixed_grad, output_last = fence((mixed_grad, output_last))
        packed_grad = tuple(attend_back(table, rotated, mixed_grad, cosine, sine))
        joint_last = weight_part(normed, packed_grad, half, last, "grad_joint")
        normed_plan = ([packed_grad], [packed_plan(joint_columns)])
        normed_far = back_rows(*normed_plan, 1, "normed_grad_far")
        normed_near = back_rows(*normed_plan, 0, "normed_grad_near")
        packed_grad, gate_got, up_late_sums, joint_last, normed_far, normed_near = fence(
            (packed_grad, gate_got, up_late_sums, joint_last, normed_far, normed_near)
        )
        grad_gate = scatter(plus(own[1], gate_got))
        normed_grad = (normed_near.astype(f32) + swap(normed_far, "core").astype(f32)).astype(bf16)
        normed_got = swap(normed_grad[part:], "row")
        branch = (branch_near.astype(f32) + swap(branch_far, "core").astype(f32)).astype(bf16)
        output_sum, joint_sum = output_last, joint_last
        if last:
            output_own = weight_part(all_attended, mixed, half, 0, "grad_output")
            joint_own = weight_part(normed, packed_grad, half, 0, "grad_joint")
            output_got, joint_got = to_last(output_last), to_last(joint_last)
            output_got, joint_got, normed_got, branch = fence(
                (output_got, joint_got, normed_got, branch)
            )
            output_sum = plus(output_own, output_got)
            joint_sum = plus(joint_own, joint_got)
        branch_got = swap(branch[part:], "row")
        (layer_out,) = row_call(
            layer_kernel,
            "layer",
            part,
            tile,
            order,
            [(middle, 0), (keep, 0), (branch, 0), (branch_got, 0)],
            [(width, bf16)],
        )
        attention_sum = jnp.concatenate([output_sum, joint_sum], axis=1)
        grad_up = None
        if early:
            up_got, grad_down = fence((up_got, grad_down))
            grad_up = scatter(plus(own[2], up_got)).astype(f32)
        attention_sum, grad_down, gate_first_sums = fence(
            (attention_sum, grad_down, gate_first_sums)
        )
        attention_terms = attention_sum
        attention_sum = scatter(attention_sum)
        (input_grad,) = pl.pallas_call(
            input_kernel,
            grid=(part // tile,),
            in_specs=[
                pl.BlockSpec(memory_space=pltpu.SMEM),
                spec((tile, width), lambda i: (i, 0)),
                spec((tile, width), lambda i: (i, 0)),
                spec((tile, width), lambda i: (i, 0)),
                whole((1, width)),
                spec((tile, width), lambda i: (i, 0)),
            ],
            out_specs=[spec((tile, width), lambda i: (i, 0))],
            out_shape=[shaped(part, width, f32)],
            scratch_shapes=[pltpu.VMEM((tile, width), f32)],
            compiler_params=pltpu.CompilerParams(vmem_limit_bytes=VMEM),
            cost_estimate=cost(part * width * 10, part * width * 16),
            name="input_grad",
        )(order, hidden_in, normed_grad, normed_got, gain_one, middle_grad)
        if late:
            sums = [(up_late_sums, late)] + ([(gate_first_sums, first)] if first else [])
            grad_late = collect(
                [
                    jnp.concatenate([rows[:, s * wide : (s + 1) * wide] for rows, wide in sums], axis=1)
                    for s in slots
                ]
            )
            if first:
                grad_gate = jnp.concatenate([grad_late[:, late:], grad_gate.astype(f32)], axis=1)
                grad_late = grad_late[:, :late]
            grad_up = grad_late if grad_up is None else jnp.concatenate([grad_up, grad_late], axis=1)
        grad_down, grad_gate, grad_up = [
            grad.astype(f32) for grad in (grad_down, grad_gate, grad_up)
        ]

        def over_tensor(values):
            values = values + swap(values, "core")
            return values + swap(values, "row")

        own_weights = packed_slots[0][:, :joint_width].astype(f32)
        terms = jnp.sum(own_weights * attention_terms[:, heads * HD :].astype(f32), axis=1)
        terms = over_tensor(terms[None, :])
        step = 1
        while step < outer:
            pairs = [(z ^ step, z) for z in range(outer)]
            terms = terms + lax.ppermute(terms, "outer", pairs)
            step *= 2
        at = lax.axis_index("outer") * shard
        attention_gain_grad = lax.dynamic_slice_in_dim(terms[0], at, shard, 0)
        attention_gain_grad = attention_gain_grad / attention_gain.astype(f32)
        terms = jnp.sum(gate_weight.astype(f32) * grad_gate, axis=1)
        terms = terms + jnp.sum(up_weight.astype(f32) * grad_up, axis=1)
        feedforward_gain_grad = over_tensor(terms[None, :])[0] / feedforward_gain.astype(f32)

        attention_sum, input_grad, layer_out, attention_gain_grad, feedforward_gain_grad = fence(
            (attention_sum, input_grad, layer_out, attention_gain_grad, feedforward_gain_grad)
        )
        attention_sum = attention_sum.astype(f32)
        grad_output = attention_sum[:, : heads * HD]
        grad_joint = attention_sum[:, heads * HD :]
        query_width = heads * HD
        grad_query = grad_joint[:, :query_width]
        grad_key = grad_joint[:, query_width : query_width + HD]
        grad_value = grad_joint[:, query_width + HD :]
        return (
            layer_out,
            input_grad,
            attention_gain_grad,
            grad_query,
            grad_key,
            grad_value,
            grad_output,
            feedforward_gain_grad,
            grad_gate,
            grad_up,
            grad_down,
        )

    return body


def solution(mesh):
    replicas = mesh.shape["dp"]
    inner = 2 if replicas % 2 == 0 else 1
    outer = replicas // inner
    cores = mesh.shape["tensor"] // 2
    grid = Mesh(mesh.devices.reshape(outer, inner, 2, cores), ("outer", "inner", "row", "core"))
    dp, tensor = ("outer", "inner"), ("row", "core")
    both = dp + tensor
    weight = P(dp, tensor)
    return jax.shard_map(
        make_body(outer, inner, 2, cores),
        mesh=grid,
        in_specs=(
            P(both, None),
            P(both),
            P(dp, None),
            P(dp),
            weight,
            weight,
            weight,
            weight,
            P(dp),
            weight,
            weight,
            weight,
            P(both, None),
        ),
        out_specs=(
            P(both, None),
            P(both, None),
            P(dp),
            weight,
            weight,
            weight,
            weight,
            P(dp),
            weight,
            weight,
            weight,
        ),
        check_vma=False,
    )
```

```python
import math

import jax
import jax.numpy as jnp
from jax import lax
from jax.experimental import pallas as pl
from jax.experimental.pallas import tpu as pltpu
from jax.sharding import Mesh
from jax.sharding import PartitionSpec as P

HD = 128
TRUNK = 4
BRANCH = 2
PIECES = 4
SHARE = 4
VMEM = 32 * 2**20

epsilon = 1e-05
masked_score = -1000000000.0
bf16 = jnp.bfloat16
f32 = jnp.float32


def dot_nn(a, b):
    return lax.dot_general(a, b, (((1,), (0,)), ((), ())), preferred_element_type=f32)


def dot_nt(a, b):
    return lax.dot_general(a, b, (((1,), (1,)), ((), ())), preferred_element_type=f32)


def dot_tn(a, b):
    return lax.dot_general(a, b, (((0,), (0,)), ((), ())), preferred_element_type=f32)


def place_pieces(table, groups, tree, blocks, into_tree):
    size = tree.shape[0] // PIECES
    piece = 0
    for group in groups:
        for at in range(0, group.shape[0], size):
            start = pl.multiple_of(table[blocks + piece], 64)
            here = slice(at, at + size)
            if into_tree:
                tree[pl.ds(start, size), :] = group[here, :].astype(tree.dtype)
            else:
                group[here, :] = tree[pl.ds(start, size), :].astype(group.dtype)
            piece += 1


def segments(table, rows, block, block_len, key_at, value_at):
    def part(start, size):
        return (
            rows[pl.ds(start, size), key_at : key_at + HD],
            rows[pl.ds(start, size), value_at : value_at + HD],
        )

    found = []
    trunk = min(block, TRUNK)
    if trunk:
        found.append((0, trunk * block_len) + part(0, trunk * block_len))
    if block >= TRUNK + BRANCH:
        start = pl.multiple_of(table[block] * block_len, block_len)
        found.append((start, block_len) + part(start, block_len))
    start = block * block_len
    found.append((start, block_len) + part(start, block_len))
    return found


def block_probs(stacked, found, block_len, scale):
    rows = stacked.shape[0]
    scores = [dot_nt(stacked, keys) * scale for _, _, keys, _ in found]
    row = lax.broadcasted_iota(jnp.int32, (rows, block_len), 0) % block_len
    column = lax.broadcasted_iota(jnp.int32, (rows, block_len), 1)
    scores[-1] = jnp.where(column <= row, scores[-1], masked_score)
    top = jnp.max(scores[0], axis=-1, keepdims=True)
    for part in scores[1:]:
        top = jnp.maximum(top, jnp.max(part, axis=-1, keepdims=True))
    raw = [jnp.exp(part - top) for part in scores]
    total = jnp.sum(raw[0], axis=-1, keepdims=True)
    for part in raw[1:]:
        total = total + jnp.sum(part, axis=-1, keepdims=True)
    inverse = 1.0 / total
    return [part * inverse for part in raw]


def stack_heads(rows, block, block_len, heads):
    here = slice(block * block_len, (block + 1) * block_len)
    return jnp.concatenate([rows[here, h * HD : (h + 1) * HD] for h in range(heads)], axis=0)


def attend_kernel(
    blocks, heads, table, raw, cosine, sine, mixed_near, mixed_far, rotated, tree, result
):
    length = tree.shape[0]
    block_len = length // blocks
    key_at, value_at = heads * HD, (heads + 1) * HD
    place_pieces(table, [raw], tree, blocks, True)

    def turn(block, carry):
        here = pl.ds(pl.multiple_of(block * block_len, block_len), block_len)
        cos, sin = cosine[here, :], sine[here, :]
        for h in range(heads + 1):
            there = slice(h * HD, (h + 1) * HD)
            values = tree[here, there]
            turned = values * cos + pltpu.roll(values, HD // 2, 1) * sin
            rotated[here, there] = turned.astype(bf16)
        rotated[here, value_at : value_at + HD] = tree[here, value_at : value_at + HD].astype(bf16)
        return carry

    lax.fori_loop(0, blocks, turn, 0)
    for block in range(blocks):
        stacked = stack_heads(rotated, block, block_len, heads)
        found = segments(table, rotated, block, block_len, key_at, value_at)
        probs = block_probs(stacked, found, block_len, HD ** (-0.5))
        out = dot_nn(probs[0].astype(bf16), found[0][3])
        for part, (_, _, _, values) in zip(probs[1:], found[1:]):
            out = out + dot_nn(part.astype(bf16), values)
        out = out.astype(bf16)
        for h in range(heads):
            result[block * block_len : (block + 1) * block_len, h * HD : (h + 1) * HD] = out[
                h * block_len : (h + 1) * block_len, :
            ]
    place_pieces(table, [mixed_near, mixed_far], result, blocks, False)


def attend_back_kernel(
    blocks,
    heads,
    table,
    rotated,
    grads,
    cosine,
    sine,
    packed_near,
    packed_far,
    tree,
    keys,
    values,
    result,
):
    length = rotated.shape[0]
    block_len = length // blocks
    key_at, value_at = heads * HD, (heads + 1) * HD
    scale = HD ** (-0.5)
    place_pieces(table, [grads], tree, blocks, True)
    keys[...] = jnp.zeros_like(keys)
    values[...] = jnp.zeros_like(values)

    def turn_back(rows, here):
        return rows * cosine[here, :] + pltpu.roll(rows * sine[here, :], HD // 2, 1)

    for block in range(blocks):
        here = slice(block * block_len, (block + 1) * block_len)
        stacked = stack_heads(rotated, block, block_len, heads)
        cotangent = stack_heads(tree, block, block_len, heads)
        found = segments(table, rotated, block, block_len, key_at, value_at)
        probs = block_probs(stacked, found, block_len, scale)
        prob_grads = [dot_nt(cotangent, part) for _, _, _, part in found]
        delta = jnp.sum(probs[0] * prob_grads[0], axis=-1, keepdims=True)
        for part, grad in zip(probs[1:], prob_grads[1:]):
            delta = delta + jnp.sum(part * grad, axis=-1, keepdims=True)
        query_grad = None
        for (start, size, key_rows, _), part, grad in zip(found, probs, prob_grads):
            score_grad = (part * (grad - delta)).astype(bf16)
            term = dot_nn(score_grad, key_rows)
            query_grad = term if query_grad is None else query_grad + term
            there = pl.ds(start, size)
            keys[there, :] += dot_tn(score_grad, stacked) * scale
            values[there, :] += dot_tn(part.astype(bf16), cotangent)
        query_grad = query_grad * scale
        for h in range(heads):
            rows = query_grad[h * block_len : (h + 1) * block_len, :]
            result[here, h * HD : (h + 1) * HD] = turn_back(rows, here).astype(bf16)

    def finish(block, carry):
        here = pl.ds(pl.multiple_of(block * block_len, block_len), block_len)
        result[here, key_at : key_at + HD] = turn_back(keys[here, :], here).astype(bf16)
        result[here, value_at : value_at + HD] = values[here, :].astype(bf16)
        return carry

    lax.fori_loop(0, blocks, finish, 0)
    place_pieces(table, [packed_near, packed_far], result, blocks, False)


def attention_calls(length, blocks, heads):
    width = (heads + 2) * HD
    vmem = pl.BlockSpec(memory_space=pltpu.VMEM)
    smem = pl.BlockSpec(memory_space=pltpu.SMEM)
    params = pltpu.CompilerParams(vmem_limit_bytes=VMEM)
    pairs = (TRUNK * (TRUNK + 1) // 2 + (blocks - TRUNK) * (TRUNK + 1) + 4) * heads
    pairs = pairs * (length // blocks) ** 2

    def forward(*operands):
        return attend_kernel(blocks, heads, *operands)

    def backward(*operands):
        return attend_back_kernel(blocks, heads, *operands)

    ahead = pl.pallas_call(
        forward,
        in_specs=[smem] + [vmem] * 3,
        out_specs=[vmem] * 3,
        out_shape=[shaped(length // 2, heads * HD, bf16)] * 2 + [shaped(length, width, bf16)],
        scratch_shapes=[pltpu.VMEM((length, width), f32), pltpu.VMEM((length, heads * HD), bf16)],
        compiler_params=params,
        cost_estimate=cost(16 * pairs * HD, length * width * 8),
        name="attend",
    )
    back = pl.pallas_call(
        backward,
        in_specs=[smem] + [vmem] * 4,
        out_specs=[vmem] * 2,
        out_shape=[shaped(length // 2, width, bf16)] * 2,
        scratch_shapes=[
            pltpu.VMEM((length, heads * HD), bf16),
            pltpu.VMEM((length, HD), f32),
            pltpu.VMEM((length, HD), f32),
            pltpu.VMEM((length, width), bf16),
        ],
        compiler_params=params,
        cost_estimate=cost(24 * pairs * HD, length * width * 8),
        name="attend_back",
    )
    return ahead, back


def rotation_tables(blocks, block_len):
    depths = [min(block, TRUNK) + (block >= TRUNK + BRANCH) for block in range(blocks)]
    length = blocks * block_len
    places = jnp.arange(length, dtype=jnp.int32)
    row_depth = jnp.zeros((length,), jnp.int32)
    for block, depth in enumerate(depths):
        row_depth = jnp.where(places // block_len == block, depth, row_depth)
    position = (row_depth * block_len + places % block_len).astype(f32)
    half = HD // 2
    freqs = jnp.exp(jnp.arange(half, dtype=f32) * (-2.0 * math.log(10000.0) / HD))
    angles = position[:, None] * freqs[None, :]
    cosine, sine = jnp.cos(angles), jnp.sin(angles)
    return (
        jnp.concatenate([cosine, cosine], axis=1),
        jnp.concatenate([-sine, sine], axis=1),
    )


def spec(block, index):
    return pl.BlockSpec(block, index)


def whole(shape):
    return pl.BlockSpec(shape, lambda *_: (0,) * len(shape))


def cost(flops, moved):
    return pl.CostEstimate(flops=flops // SHARE, bytes_accessed=moved // SHARE, transcendentals=0)


def shaped(rows, columns, kind):
    return jax.ShapeDtypeStruct((rows, columns), kind)


def in_hbm(rows, columns, kind):
    return pltpu.HBM((rows, columns), kind)


def runs(order, width):
    run = width // order.shape[0]
    for j in range(order.shape[0]):
        yield slice(j * run, (j + 1) * run), pl.ds(pl.multiple_of(order[j] * run, HD), run)


def row_call(kernel, name, rows, tile, order, operands, results):
    def place(array, offset):
        if offset is None:
            return whole(array.shape)
        steps = array.shape[0] // tile
        return spec((tile, array.shape[1]), lambda i: ((i + offset) % steps, 0))

    return pl.pallas_call(
        kernel,
        grid=(rows // tile,),
        in_specs=[pl.BlockSpec(memory_space=pltpu.SMEM)] + [place(*pair) for pair in operands],
        out_specs=[spec((tile, columns), lambda i: (i, 0)) for columns, _ in results],
        out_shape=[shaped(rows, columns, kind) for columns, kind in results],
        compiler_params=pltpu.CompilerParams(vmem_limit_bytes=VMEM),
        cost_estimate=cost(rows * 2048 * 10, rows * 2048 * 8),
        name=name,
    )(order, *[array for array, _ in operands])


def row_mean(values):
    return jnp.mean(values, axis=-1, keepdims=True)


def norm_kernel(order, rows, gain, normed):
    values = rows[...].astype(f32)
    scale = lax.rsqrt(row_mean(values * values) + epsilon)
    for here, there in runs(order, rows.shape[1]):
        unit = rows[:, there].astype(f32) * scale
        normed[:, here] = (unit * gain[:, here]).astype(bf16)


def pack_kernel(*refs):
    gains, weights, result = refs[0], refs[1:-1], refs[-1]
    at = 0
    for weight in weights:
        result[:, at : at + weight.shape[1]] = weight[...]
        at += weight.shape[1]
    rows = jnp.concatenate([gains[...], jnp.zeros((HD - gains.shape[0], gains.shape[1]), f32)])
    result[:, at:] = rows.T.astype(bf16)


def gains_kernel(*refs):
    slots, first, second = refs[:-2], refs[-2], refs[-1]
    at = 0
    for slot in slots:
        columns = slot[...].astype(f32).T
        here = slice(at, at + slot.shape[0])
        first[:, here] = columns[0:1, :]
        second[:, here] = columns[1:2, :]
        at += slot.shape[0]


def kept_kernel(order, rows, keep, result):
    for here, there in runs(order, rows.shape[1]):
        result[:, here] = (rows[:, there].astype(f32) * keep[...]).astype(bf16)


def middle_kernel(order, rows, keep, mine, got, gain, middle, normed):
    for here, there in runs(order, rows.shape[1]):
        attended = mine[:, here].astype(f32) + got[:, here].astype(f32)
        middle[:, here] = rows[:, there].astype(f32) + keep[...] * attended
    values = middle[...]
    scale = lax.rsqrt(row_mean(values * values) + epsilon)
    normed[...] = (values * scale * gain[...]).astype(bf16)


def middle_back_kernel(order, cotangent, keep, mine, got, gain, middle, grad, kept):
    values = middle[...]
    scale = lax.rsqrt(row_mean(values * values) + epsilon)
    unit = values * scale
    scaled = (mine[...].astype(f32) + got[...].astype(f32)) * gain[...]
    mean = row_mean(scaled * unit)
    change = scale * (scaled - unit * mean)
    for here, there in runs(order, middle.shape[1]):
        total = cotangent[:, there].astype(f32) + change[:, here]
        grad[:, here] = total
        kept[:, here] = (keep[...] * total).astype(bf16)


def layer_kernel(order, middle, keep, mine, got, result):
    for here, there in runs(order, middle.shape[1]):
        branch = mine[:, here].astype(f32) + got[:, here].astype(f32)
        result[:, there] = (middle[:, here] + keep[...] * branch).astype(bf16)


def input_kernel(order, rows, mine, got, gain, middle_grad, result, scaled):
    values = rows[...].astype(f32)
    scale = lax.rsqrt(row_mean(values * values) + epsilon)
    scaled[...] = (mine[...].astype(f32) + got[...].astype(f32)) * gain[...]
    total = None
    for here, there in runs(order, rows.shape[1]):
        term = jnp.sum(scaled[:, here] * rows[:, there].astype(f32), axis=-1, keepdims=True)
        total = term if total is None else total + term
    mean = total * scale / rows.shape[1]
    for here, there in runs(order, rows.shape[1]):
        unit = rows[:, there].astype(f32) * scale
        result[:, there] = middle_grad[:, here] + scale * (scaled[:, here] - unit * mean)


def column_cuts(width):
    return [slice(at, min(at + 256, width)) for at in range(0, width, 256)]


def of_group(near, far, steps):
    tile = 2 * near.shape[0] // steps
    last = steps // 2 - 1
    return [
        spec((tile, near.shape[1]), lambda i: (jnp.minimum(i, last), 0)),
        spec((tile, far.shape[1]), lambda i: (jnp.maximum(i - last - 1, 0), 0)),
    ]


def resident(slots):
    return [
        pl.BlockSpec(slot.shape, lambda i: (0, 0), pipeline_mode=pl.Buffered(1)) for slot in slots
    ]


def in_halves(steps, work):
    for side in range(2):

        @pl.when(pl.program_id(0) // (steps // 2) == side)
        def _(side=side):
            work(side)


def product(rows, weights, cut):
    total, at = None, 0
    for weight in weights:
        term = dot_nn(rows[:, at : at + weight.shape[0]], weight[:, cut])
        total = term if total is None else total + term
        at += weight.shape[0]
    return total


def through(rows, weights, name, columns, kind):
    near, far = rows
    units = columns.stop - columns.start
    length, width = 2 * near.shape[0], near.shape[1]

    def kernel(*refs):
        slots, result = refs[2:-1], refs[-1]

        def work(side):
            for inside in column_cuts(units):
                cut = slice(columns.start + inside.start, columns.start + inside.stop)
                result[:, inside] = product(refs[side], slots, cut).astype(result.dtype)

        in_halves(2, work)

    return pl.pallas_call(
        kernel,
        grid=(2,),
        in_specs=of_group(near, far, 2) + resident(weights),
        out_specs=spec((length // 2, units), lambda i: (i, 0)),
        out_shape=shaped(length, units, kind),
        compiler_params=pltpu.CompilerParams(vmem_limit_bytes=VMEM),
        cost_estimate=cost(2 * length * width * units, 2 * width * (length + units)),
        name=name,
    )(near, far, *weights)


def gate_product(rows, hidden_grad, gates):
    near, far = rows
    length, units = hidden_grad.shape
    width = near.shape[1]

    def kernel(*refs):
        hidden_back, slots = refs[2], refs[3:-2]
        gate_out, up_grad = refs[-2:]

        def work(side):
            for cut in column_cuts(units):
                gate = product(refs[side], slots, cut)
                gate_out[:, cut] = gate
                active = gate / (1.0 + jnp.exp(-gate))
                up_grad[:, cut] = (hidden_back[:, cut].astype(f32) * active).astype(bf16)

        in_halves(4, work)

    here = spec((length // 4, units), lambda i: (i, 0))
    return pl.pallas_call(
        kernel,
        grid=(4,),
        in_specs=of_group(near, far, 4) + [here] + resident(gates),
        out_specs=[here] * 2,
        out_shape=[in_hbm(length, units, f32), shaped(length, units, bf16)],
        compiler_params=pltpu.CompilerParams(vmem_limit_bytes=VMEM),
        cost_estimate=cost(2 * length * width * units, 2 * width * (length + units)),
        name="gate",
    )(near, far, hidden_grad, *gates)


def up_product(rows, hidden_grad, gate, ups):
    near, far = rows
    length, units = hidden_grad.shape
    width = near.shape[1]
    up_slots = [slot for slots, _, _ in ups for slot in slots]

    def kernel(*refs):
        hidden_back, gate_in = refs[2], refs[3]
        up_refs = refs[4:-2]
        hidden, gate_grad = refs[-2:]

        def work(side):
            rows_in, at = refs[side], 0
            for slots, first, columns in ups:
                mine = up_refs[at : at + len(slots)]
                at += len(slots)
                for inside in column_cuts(columns.stop - columns.start):
                    cut = slice(first + inside.start, first + inside.stop)
                    there = slice(columns.start + inside.start, columns.start + inside.stop)
                    if len(slots) == 1 and mine[0].shape[0] < width:
                        depth = mine[0].shape[0]
                        count = width // depth
                        step = mine[0].shape[1] // count
                        upward = None
                        for s in range(count):
                            view = mine[0][:, there.start + s * step : there.stop + s * step]
                            term = dot_nn(rows_in[:, s * depth : (s + 1) * depth], view)
                            upward = term if upward is None else upward + term
                    else:
                        upward = product(rows_in, mine, there)
                    value = gate_in[:, cut]
                    sigma = 1.0 / (1.0 + jnp.exp(-value))
                    back = hidden_back[:, cut].astype(f32) * upward * sigma
                    hidden[:, cut] = (value * sigma * upward).astype(bf16)
                    gate_grad[:, cut] = (back * (1.0 + value * (1.0 - sigma))).astype(bf16)

        in_halves(4, work)

    here = spec((length // 4, units), lambda i: (i, 0))
    return pl.pallas_call(
        kernel,
        grid=(4,),
        in_specs=of_group(near, far, 4) + [here, here] + resident(up_slots),
        out_specs=[here] * 2,
        out_shape=[shaped(length, units, bf16)] * 2,
        compiler_params=pltpu.CompilerParams(vmem_limit_bytes=VMEM),
        cost_estimate=cost(2 * length * width * units, 2 * width * (length + units)),
        name="up",
    )(near, far, hidden_grad, gate, *up_slots)


def back_rows(grads, weights, side, name, far=None, shape=shaped):
    width = sum(array.shape[0] for array in weights[0][0][0])
    tile = min(512, min(array.shape[0] for parts in weights for w in parts for array in w[0]))
    first = grads[0]
    count = first[0].shape[0] if isinstance(first, tuple) else first.shape[0] // 2
    operands, specs, plan = [], [], [[] for _ in range(width // tile)]
    work = 0
    for grad, parts in zip(grads, weights):
        at = len(operands)
        if isinstance(grad, tuple):
            specs.append(spec(grad[side].shape, lambda j: (0, 0)))
            operands.append(grad[side])
        else:
            specs.append(spec((count, grad.shape[1]), lambda j: (side, 0)))
            operands.append(grad)
        for arrays, unit, columns in parts:
            start = 0
            for array, cut in zip(arrays, columns):
                tiles = array.shape[0] // tile
                for j in range(start, start + tiles):
                    plan[j].append((at, unit, cut, len(operands)))
                operands.append(array)
                specs.append(
                    spec(
                        (tile, array.shape[1]),
                        lambda j, start=start, tiles=tiles: (jnp.clip(j - start, 0, tiles - 1), 0),
                    )
                )
                start += tiles
                work += 2 * count * array.shape[0] * (cut.stop - cut.start)
    if far is not None:
        operands.append(far)
        specs.append(spec((count, tile), lambda j: (0, j)))
    ranges = []
    for j, terms in enumerate(plan):
        if ranges and ranges[-1][2] == terms:
            ranges[-1][1] = j + 1
        else:
            ranges.append([j, j + 1, terms])

    def kernel(*refs):
        result = refs[-1]
        for low, high, terms in ranges:

            @pl.when((pl.program_id(0) >= low) & (pl.program_id(0) < high))
            def _(terms=terms):
                total = None
                for at, unit, cut, place in terms:
                    units = cut.stop - cut.start
                    term = dot_nt(refs[at][:, unit : unit + units], refs[place][:, cut])
                    total = term if total is None else total + term
                if far is not None:
                    total = total + refs[-2][...].astype(f32)
                result[...] = total.astype(result.dtype)

    return pl.pallas_call(
        kernel,
        grid=(width // tile,),
        in_specs=specs,
        out_specs=spec((count, tile), lambda j: (0, j)),
        out_shape=shape(count, width, bf16),
        compiler_params=pltpu.CompilerParams(vmem_limit_bytes=VMEM),
        cost_estimate=cost(work, 2 * sum(operand.size for operand in operands)),
        name=name,
    )(*operands)


def grad_terms(near, far, refs, columns, pair):
    count = near.shape[0]
    if pair:
        first, second = refs[0][:, columns], refs[1][:, columns]
    else:
        first, second = refs[0][:count, columns], refs[0][count:, columns]
    return (dot_tn(near[...], first) + dot_tn(far[...], second)).astype(bf16)


def weight_part(rows, grads, half, s, name, columns=None, parts=1):
    near, far = rows
    pair = isinstance(grads, tuple)
    units = grads[0].shape[1] if pair else grads.shape[1]
    columns = slice(0, units) if columns is None else columns
    wide = columns.stop - columns.start
    tile = min(512, half) if parts == 1 else half // 4
    tiles = half // tile
    edges = [0, tiles] if parts == 1 else [0, 1, tiles]
    count = near.shape[0]
    row_spec = spec((count, tile), lambda j: (0, s * tiles + j))
    operands = grads if pair else (grads,)

    def kernel(near_rows, far_rows, *refs):
        total = grad_terms(near_rows, far_rows, refs, columns, pair)
        for part in range(parts):

            @pl.when((pl.program_id(0) >= edges[part]) & (pl.program_id(0) < edges[part + 1]))
            def _(part=part):
                refs[len(operands) + part][...] = total

    found = pl.pallas_call(
        kernel,
        grid=(tiles,),
        in_specs=[row_spec, row_spec] + [whole(operand.shape) for operand in operands],
        out_specs=[
            spec(
                (tile, wide),
                lambda j, part=part: (
                    jnp.clip(j, edges[part], edges[part + 1] - 1) - edges[part],
                    0,
                ),
            )
            for part in range(parts)
        ],
        out_shape=[
            in_hbm((edges[part + 1] - edges[part]) * tile, wide, bf16) for part in range(parts)
        ],
        compiler_params=pltpu.CompilerParams(vmem_limit_bytes=VMEM),
        cost_estimate=cost(4 * count * half * wide, 4 * count * (half + wide)),
        name=name,
    )(near, far, *operands)
    return found if parts > 1 else found[0]


def weight_slots(rows, grads, half, name, columns):
    near, far = rows
    wide = columns.stop - columns.start
    tile = min(512, half)
    tiles = half // tile
    inner = near.shape[1] // half
    count = near.shape[0]
    row_spec = spec((count, tile), lambda j: (0, j))

    def kernel(near_rows, far_rows, *refs):
        refs[-1][...] = grad_terms(near_rows, far_rows, refs, columns, False)

    return pl.pallas_call(
        kernel,
        grid=(inner * tiles,),
        in_specs=[row_spec, row_spec, whole(grads.shape)],
        out_specs=spec((tile, wide), lambda j: (j % tiles, j // tiles)),
        out_shape=in_hbm(half, inner * wide, bf16),
        compiler_params=pltpu.CompilerParams(vmem_limit_bytes=VMEM),
        cost_estimate=cost(4 * count * half * inner * wide, 4 * count * (half + wide)),
        name=name,
    )(near, far, grads)


def make_body(outer, inner, rows_axis, cores_axis):
    def body(
        hidden_in,
        skip_mask,
        parents,
        attention_gain,
        query_weight,
        key_weight,
        value_weight,
        output_weight,
        feedforward_gain,
        gate_weight,
        up_weight,
        down_weight,
        grad_out,
    ):
        part = hidden_in.shape[0]
        shard = query_weight.shape[0]
        pieces = rows_axis * cores_axis
        length = part * pieces
        near = part * rows_axis
        blocks = parents.shape[1]
        heads = query_weight.shape[1] // HD
        half = outer * shard
        width = half * inner
        tile = part // 2
        at_inner = lax.axis_index("inner")
        at_row = lax.axis_index("row")
        at_core = lax.axis_index("core")
        slots = range(inner)
        fence = lax.optimization_barrier

        order = jnp.stack(
            [z * inner + (at_inner + s) % inner for s in slots for z in range(outer)]
        ).astype(jnp.int32)

        def from_inner(values, k):
            return lax.ppermute(values, "inner", [((i + k) % inner, i) for i in range(inner)])

        def swap(values, axis):
            return lax.ppermute(values, axis, [(0, 1), (1, 0)])

        def spread(values):
            return [values] + [from_inner(values, s) for s in range(1, inner)]

        def gather(values):
            return lax.all_gather(values, "outer", axis=0, tiled=True)

        def scatter(values):
            return lax.psum_scatter(values, "outer", scatter_dimension=0, tiled=True)

        def collect(parts):
            total = parts[0].astype(f32)
            for s in range(1, inner):
                total = total + from_inner(parts[s], inner - s).astype(f32)
            return total

        keep_own = (1 - skip_mask).astype(f32)
        units = up_weight.shape[1]
        late = units if inner > 1 else 0
        joint_width = (heads + 2) * HD
        packed = pl.pallas_call(
            pack_kernel,
            out_shape=shaped(shard, joint_width + heads * HD + HD, bf16),
            compiler_params=pltpu.CompilerParams(vmem_limit_bytes=VMEM),
            cost_estimate=cost(0, shard * joint_width * 4),
            name="pack",
        )(
            jnp.stack([attention_gain.astype(f32), feedforward_gain.astype(f32)]),
            query_weight,
            key_weight,
            value_weight,
            output_weight,
        )
        keep_got = swap(keep_own, "row")
        row_x = swap(hidden_in, "row")
        row_g = swap(grad_out, "row")
        up_late = jnp.concatenate(spread(up_weight[:, units - late :]), axis=1) if late else None
        row_x, keep_got, up_late = fence((row_x, keep_got, up_late))
        near_x = jnp.concatenate([hidden_in, row_x], axis=0)
        far_x = swap(near_x, "core")
        packed_own = gather(packed)
        packed_own, far_x = fence((packed_own, far_x))
        packed_slots = spread(packed_own)
        keep = jnp.concatenate([keep_own, keep_got], axis=0)[:, None]
        near_g = jnp.concatenate([grad_out, row_g], axis=0)
        (near_branch,) = row_call(
            kept_kernel, "kept", near, tile, order, [(near_g, 0), (keep, 0)], [(width, bf16)]
        )
        far_branch = swap(near_branch, "core")
        down_own = gather(down_weight)
        gate_own = gather(gate_weight)
        early = units - late
        up_own = gather(up_weight[:, :early]) if early else None
        up_both = [gather(up_late)] if late else []

        cosine, sine = rotation_tables(blocks, length // blocks)
        starts = [
            (((at_row + dy) % 2) * cores_axis + (at_core + dc) % 2) * part
            for dc in range(2)
            for dy in range(2)
        ]
        table = jnp.concatenate([parents[0], jnp.stack(starts).astype(jnp.int32)])
        packed_slots, near_branch, far_branch, down_own = fence(
            (packed_slots, near_branch, far_branch, down_own)
        )
        quarter = half // 4
        down_got = [from_inner(down_own[:quarter], 1)] if inner > 1 else []
        gain_at = joint_width + heads * HD
        joint_columns = slice(0, joint_width)
        output_columns = slice(joint_width, gain_at)
        gain_one, gain_two = pl.pallas_call(
            gains_kernel,
            grid=(1,),
            in_specs=[spec((half, HD), lambda i: (0, gain_at // HD))] * inner,
            out_specs=[whole((1, width))] * 2,
            out_shape=[shaped(1, width, f32)] * 2,
            compiler_params=pltpu.CompilerParams(vmem_limit_bytes=VMEM),
            cost_estimate=cost(0, width * 8),
            name="gains",
        )(*packed_slots)
        all_branch = (near_branch, far_branch)

        def norm(rows, name):
            (result,) = row_call(
                norm_kernel, name, near, tile, order, [(rows, 0), (gain_one, None)], [(width, bf16)]
            )
            return result

        normed = (norm(near_x, "norm_near"), norm(far_x, "norm_far"))

        def all_of(arrays):
            return [(arrays, 0, [slice(0, array.shape[1]) for array in arrays])]

        attend, attend_back = attention_calls(length, blocks, heads)
        raw = through(normed, packed_slots, "joint", joint_columns, f32)
        if inner > 1:
            raw, down_got, down_own = fence((raw, down_got, down_own))
            down_got = down_got + [from_inner(down_own[quarter : 2 * quarter], 1)]
        mixed_near, mixed_far, rotated = attend(table, raw, cosine, sine)
        if inner > 1:
            mixed_near, mixed_far, down_got, down_own = fence(
                (mixed_near, mixed_far, down_got, down_own)
            )
            down_got = down_got + [from_inner(down_own[2 * quarter : 3 * quarter], 1)]
        mixed = (mixed_near, mixed_far)

        def packed_plan(columns):
            return [(packed_slots, 0, [columns] * inner)]

        attended_plan = [packed_plan(output_columns)]
        attended_far = swap(back_rows([mixed], attended_plan, 1, "attended_far"), "core")
        attended = back_rows([mixed], attended_plan, 0, "attended_near")
        attended = (attended.astype(f32) + attended_far.astype(f32)).astype(bf16)
        attended, gate_own, down_got = fence((attended, gate_own, down_got))
        if inner > 1:
            down_got = down_got + [from_inner(down_own[3 * quarter :], 1)]
        weight_down = [down_own] + down_got
        got = swap(attended, "row")
        weight_gate = spread(gate_own)
        hidden_grad = through(all_branch, weight_down, "hidden_grad", slice(0, units), bf16)
        got, hidden_grad, up_own = fence((got, hidden_grad, up_own))
        weight_up = spread(up_own) if early else []
        swapped = part // tile
        middle, normed_ff = row_call(
            middle_kernel,
            "middle",
            near,
            tile,
            order,
            [(near_x, 0), (keep, 0), (attended, 0), (got, swapped), (gain_two, None)],
            [(width, f32), (width, bf16)],
        )
        all_ff = (normed_ff, swap(normed_ff, "core"))

        up_parts = [(weight_up, 0, slice(0, early))] if early else []
        up_plan = [(weight_up, 0, [slice(0, early)] * inner)] if early else []
        if late:
            up_parts.append((up_both, early, slice(0, late)))
            up_plan.append((up_both * inner, early, [slice(s * late, (s + 1) * late) for s in slots]))
        gate, up_grad = gate_product(all_ff, hidden_grad, weight_gate)
        def weight_parts(rows, grads, name, columns=None):
            return [weight_part(rows, grads, half, s, name, columns) for s in slots]

        def core_sum(grads, weights, name):
            far = swap(back_rows(grads, weights, 1, name + "_far"), "core")
            return back_rows(grads, weights, 0, name + "_near", far)

        last = inner - 1
        up_late_sums = None
        if late:
            up_late_parts = weight_slots(all_ff, up_grad, half, "grad_up_late", slice(early, units))
            gate, up_grad, up_late_parts = fence((gate, up_grad, up_late_parts))
            up_late_sums = scatter(up_late_parts)
        hidden_ff, gate_grad = up_product(all_ff, hidden_grad, gate, up_parts)
        down_last = weight_part(all_branch, hidden_ff, half, last, "grad_down")
        gate_grad, up_grad, down_last = fence((gate_grad, up_grad, down_last))
        back_plan = ([gate_grad, up_grad], [all_of(weight_gate), up_plan])
        ff_far = back_rows(*back_plan, 1, "normed_ff_grad_far")
        ff_far, gate_grad, up_grad = fence((ff_far, gate_grad, up_grad))
        ff_far = swap(ff_far, "core")
        first = units // HD * 4 // 11 * HD if last else 0
        gate_columns = slice(first, units)
        gate_last = weight_part(all_ff, gate_grad, half, last, "grad_gate", gate_columns)
        gate_grad, up_grad, gate_last = fence((gate_grad, up_grad, gate_last))
        back_plan = ([gate_grad, up_grad], [all_of(weight_gate), up_plan])
        ff_grad = back_rows(*back_plan, 0, "normed_ff_grad_near", ff_far, in_hbm)
        ff_grad, gate_grad, up_grad, hidden_ff = fence((ff_grad, gate_grad, up_grad, hidden_ff))
        ff_got = swap(ff_grad, "row")
        gate_first_sums = None
        if first:
            gate_first = weight_slots(all_ff, gate_grad, half, "grad_gate_first", slice(0, first))
            gate_grad, hidden_ff, gate_first = fence((gate_grad, hidden_ff, gate_first))
            gate_first_sums = scatter(gate_first)

        def to_last(values):
            return from_inner(values, inner - last) if last else None

        def plus(values, got):
            if got is None:
                return values
            return (values.astype(f32) + got.astype(f32)).astype(bf16)

        down_got = to_last(down_last)
        gate_got = to_last(gate_last)
        up_last = up_got = None
        if early:
            up_last = weight_part(all_ff, up_grad, half, last, "grad_up", slice(0, early))
            up_got = to_last(up_last)
        own = [down_last, gate_last, up_last]
        if last:
            own = [
                weight_part(all_branch, hidden_ff, half, 0, "grad_down"),
                weight_part(all_ff, gate_grad, half, 0, "grad_gate", gate_columns),
                weight_part(all_ff, up_grad, half, 0, "grad_up", slice(0, early))
                if early
                else None,
            ]
        branch_plan = ([hidden_ff], [all_of(weight_down)])
        branch_far = back_rows(*branch_plan, 1, "branch_far")
        branch_near = back_rows(*branch_plan, 0, "branch_near")
        down_own, down_got, own[1], branch_far, branch_near = fence(
            (own[0], down_got, own[1], branch_far, branch_near)
        )
        down_sum = plus(down_own, down_got)
        ff_got, own, up_last, gate_last = fence((ff_got, own, up_last, gate_last))
        grad_down = scatter(down_sum)
        middle_grad, attended_grad = row_call(
            middle_back_kernel,
            "middle_back",
            near,
            tile,
            order,
            [
                (near_g, 0),
                (keep, 0),
                (ff_grad, 0),
                (ff_got, swapped),
                (gain_two, None),
                (middle, 0),
            ],
            [(width, f32), (width, bf16)],
        )
        all_attended = (attended_grad, swap(attended_grad, "core"))

        mixed_grad = through(all_attended, packed_slots, "mixed_grad", output_columns, bf16)
        output_last = weight_part(all_attended, mixed, half, last, "grad_output")
        mixed_grad, output_last = fence((mixed_grad, output_last))
        packed_grad = tuple(attend_back(table, rotated, mixed_grad, cosine, sine))
        joint_last = weight_part(normed, packed_grad, half, last, "grad_joint")
        normed_plan = ([packed_grad], [packed_plan(joint_columns)])
        normed_far = back_rows(*normed_plan, 1, "normed_grad_far")
        packed_grad, gate_got, up_late_sums, joint_last, normed_far = fence(
            (packed_grad, gate_got, up_late_sums, joint_last, normed_far)
        )
        normed_plan = ([packed_grad], [packed_plan(joint_columns)])
        normed_near = back_rows(*normed_plan, 0, "normed_grad_near")
        grad_gate = scatter(plus(own[1], gate_got))
        normed_grad = (normed_near.astype(f32) + swap(normed_far, "core").astype(f32)).astype(bf16)
        normed_got = swap(normed_grad[part:], "row")
        branch = (branch_near.astype(f32) + swap(branch_far, "core").astype(f32)).astype(bf16)
        output_sum, joint_sum = output_last, joint_last
        if last:
            output_own = weight_part(all_attended, mixed, half, 0, "grad_output")
            joint_own = weight_part(normed, packed_grad, half, 0, "grad_joint")
            output_got, joint_got = to_last(output_last), to_last(joint_last)
            output_got, joint_got, normed_got, branch = fence(
                (output_got, joint_got, normed_got, branch)
            )
            output_sum = plus(output_own, output_got)
            joint_sum = plus(joint_own, joint_got)
        branch_got = swap(branch[part:], "row")
        (layer_out,) = row_call(
            layer_kernel,
            "layer",
            part,
            tile,
            order,
            [(middle, 0), (keep, 0), (branch, 0), (branch_got, 0)],
            [(width, bf16)],
        )
        attention_sum = jnp.concatenate([output_sum, joint_sum], axis=1)
        grad_up = None
        if early:
            up_got, grad_down = fence((up_got, grad_down))
            grad_up = scatter(plus(own[2], up_got)).astype(f32)
        attention_sum, grad_down, gate_first_sums = fence(
            (attention_sum, grad_down, gate_first_sums)
        )
        attention_terms = attention_sum
        attention_sum = scatter(attention_sum)
        (input_grad,) = pl.pallas_call(
            input_kernel,
            grid=(part // tile,),
            in_specs=[
                pl.BlockSpec(memory_space=pltpu.SMEM),
                spec((tile, width), lambda i: (i, 0)),
                spec((tile, width), lambda i: (i, 0)),
                spec((tile, width), lambda i: (i, 0)),
                whole((1, width)),
                spec((tile, width), lambda i: (i, 0)),
            ],
            out_specs=[spec((tile, width), lambda i: (i, 0))],
            out_shape=[shaped(part, width, f32)],
            scratch_shapes=[pltpu.VMEM((tile, width), f32)],
            compiler_params=pltpu.CompilerParams(vmem_limit_bytes=VMEM),
            cost_estimate=cost(part * width * 10, part * width * 16),
            name="input_grad",
        )(order, hidden_in, normed_grad, normed_got, gain_one, middle_grad)
        if late:
            sums = [(up_late_sums, late)] + ([(gate_first_sums, first)] if first else [])
            grad_late = collect(
                [
                    jnp.concatenate([rows[:, s * wide : (s + 1) * wide] for rows, wide in sums], axis=1)
                    for s in slots
                ]
            )
            if first:
                grad_gate = jnp.concatenate([grad_late[:, late:], grad_gate.astype(f32)], axis=1)
                grad_late = grad_late[:, :late]
            grad_up = grad_late if grad_up is None else jnp.concatenate([grad_up, grad_late], axis=1)
        grad_down, grad_gate, grad_up = [
            grad.astype(f32) for grad in (grad_down, grad_gate, grad_up)
        ]

        def over_tensor(values):
            values = values + swap(values, "core")
            return values + swap(values, "row")

        own_weights = packed_slots[0][:, :joint_width].astype(f32)
        terms = jnp.sum(own_weights * attention_terms[:, heads * HD :].astype(f32), axis=1)
        terms = over_tensor(terms[None, :])
        step = 1
        while step < outer:
            pairs = [(z ^ step, z) for z in range(outer)]
            terms = terms + lax.ppermute(terms, "outer", pairs)
            step *= 2
        at = lax.axis_index("outer") * shard
        attention_gain_grad = lax.dynamic_slice_in_dim(terms[0], at, shard, 0)
        attention_gain_grad = attention_gain_grad / attention_gain.astype(f32)
        terms = jnp.sum(gate_weight.astype(f32) * grad_gate, axis=1)
        terms = terms + jnp.sum(up_weight.astype(f32) * grad_up, axis=1)
        feedforward_gain_grad = over_tensor(terms[None, :])[0] / feedforward_gain.astype(f32)

        attention_sum, input_grad, layer_out, attention_gain_grad, feedforward_gain_grad = fence(
            (attention_sum, input_grad, layer_out, attention_gain_grad, feedforward_gain_grad)
        )
        attention_sum = attention_sum.astype(f32)
        grad_output = attention_sum[:, : heads * HD]
        grad_joint = attention_sum[:, heads * HD :]
        query_width = heads * HD
        grad_query = grad_joint[:, :query_width]
        grad_key = grad_joint[:, query_width : query_width + HD]
        grad_value = grad_joint[:, query_width + HD :]
        return (
            layer_out,
            input_grad,
            attention_gain_grad,
            grad_query,
            grad_key,
            grad_value,
            grad_output,
            feedforward_gain_grad,
            grad_gate,
            grad_up,
            grad_down,
        )

    return body


def solution(mesh):
    replicas = mesh.shape["dp"]
    inner = 2 if replicas % 2 == 0 else 1
    outer = replicas // inner
    cores = mesh.shape["tensor"] // 2
    grid = Mesh(mesh.devices.reshape(outer, inner, 2, cores), ("outer", "inner", "row", "core"))
    dp, tensor = ("outer", "inner"), ("row", "core")
    both = dp + tensor
    weight = P(dp, tensor)
    return jax.shard_map(
        make_body(outer, inner, 2, cores),
        mesh=grid,
        in_specs=(
            P(both, None),
            P(both),
            P(dp, None),
            P(dp),
            weight,
            weight,
            weight,
            weight,
            P(dp),
            weight,
            weight,
            weight,
            P(both, None),
        ),
        out_specs=(
            P(both, None),
            P(both, None),
            P(dp),
            weight,
            weight,
            weight,
            weight,
            P(dp),
            weight,
            weight,
            weight,
        ),
        check_vma=False,
    )
```
